32 devices in a mesh: samp: 4 (over y, x), probe: 8 (over z, core).
Axes of the slice: x: 2, y: 2, z: 4, core: 2. Of those that a mesh axis runs over, the one named last changes fastest.
Arguments:
- methyl: bfloat16 [4096, 16384], P('samp', 'probe'), may hold values from -0.25 to 1.25
- atlas: bfloat16 [64, 16384], P(None, 'probe'), may hold values from 0 to 1, as said below
- panel_ids: int32 [64], replicated, may hold values from 0 to 63, each once
Outputs:
- relmat: float32 [3, 4096, 1024], P(None, 'samp', 'probe')
- scores: float32 [32, 4096], P(None, ('samp', 'probe'))
The draws below stay inside these ranges and needn't reach their ends.
Inputs may be any that keep to these rules, and one draw needn't show every extreme that they name: atlas values are beta values between 0 and 1.
All inputs are finite; a program needn't handle non-finite values.
Results may differ from the reference program's by a relative error of at most 0.003.
Values may be sent and summed in bfloat16 or wider, within the bound.
No kernel may reach another device: no remote copies, remote signals or barrier semaphores. Data moves between devices by JAX's collectives and lax.ppermute only.
A program may use at most 128 MiB of HBM per device.

```python
import jax
import jax.numpy as jnp
from jax import lax

K = 32
ATLAS = 64
PANEL = 1024
ITERS = 128
PANELS = 4
SAMPLES = 4096
PROBES = 16384


def atlas_values(key):
    state_key, level_key = jax.random.split(jax.random.fold_in(key, 7101))
    methylated = jax.random.uniform(state_key, (ATLAS, PROBES), jnp.float32) < 0.25
    levels = jax.random.uniform(level_key, (2, ATLAS, PROBES), jnp.float32)
    high_level = 0.74 + 0.24 * levels[0]
    low_level = 0.02 + 0.14 * levels[1]
    return jnp.where(methylated, high_level, low_level)


def draw_atlas(key, part):
    return atlas_values(key).astype(jnp.bfloat16)


def draw_methyl(key, part):
    profiles = atlas_values(key).astype(jnp.bfloat16).astype(jnp.float32)
    mix_key, noise_key, absent_key = jax.random.split(jax.random.fold_in(key, 7202), 3)
    present = jax.random.uniform(absent_key, (SAMPLES, ATLAS), jnp.float32) < 0.55
    position = jnp.arange(PROBES, dtype=jnp.float32) / PROBES
    logits = jax.random.normal(mix_key, (SAMPLES, ATLAS), jnp.float32)
    noise = 0.08 * jax.random.normal(noise_key, (SAMPLES, PROBES), jnp.float32)
    gain = 0.125 * jnp.power(8.0, position)
    shares = jax.nn.softmax(jnp.where(present, logits, -1000000000.0), axis=1)
    values = (jnp.dot(shares, profiles, precision=lax.Precision.HIGHEST) + noise) * gain[None, :]
    return jnp.clip(values, -0.25, 1.25).astype(jnp.bfloat16)


def setup_inputs(seed: int = 0) -> dict:
    splits = jax.random.split(jax.random.key(seed), 4)
    methyl = draw_methyl(jax.random.fold_in(splits[3], 71), 0)
    atlas = draw_atlas(jax.random.fold_in(splits[3], 71), 0)
    panel_ids = jax.random.permutation(splits[2], ATLAS).astype(jnp.int32)
    return {"methyl": methyl, "atlas": atlas, "panel_ids": panel_ids}


def ridge_solve(wgram, cross, ridge):
    eye = jnp.eye(wgram.shape[0], dtype=wgram.dtype)
    factor = jnp.linalg.cholesky(wgram + ridge * eye)
    middle = lax.linalg.triangular_solve(factor, cross, left_side=True, lower=True)
    return lax.linalg.triangular_solve(factor, middle, left_side=True, lower=True, transpose_a=True)

def reference(methyl, atlas, panel_ids):
    selector = (panel_ids[:K, None] == jnp.arange(ATLAS, dtype=jnp.int32)[None, :]).astype(jnp.bfloat16)
    panel = jnp.dot(selector.astype(jnp.float32), atlas.astype(jnp.float32), preferred_element_type=jnp.float32).astype(jnp.bfloat16)
    gram = jnp.dot(panel.astype(jnp.float32), panel.T.astype(jnp.float32), preferred_element_type=jnp.float32)
    proj = lax.dot_general(panel.astype(jnp.float32), methyl.astype(jnp.float32), (((1,), (1,)), ((), ())), preferred_element_type=jnp.float32)
    step_rate = 1.0 / jnp.trace(gram)

    def descend(turn_index, weights):
        grad_term = jnp.dot(gram, weights, precision=lax.Precision.HIGHEST) - proj
        return jnp.maximum(weights - step_rate * grad_term, 0.0)
    weights = lax.fori_loop(0, ITERS, descend, jnp.full(proj.shape, 1.0 / K, jnp.float32))
    scores = K * weights
    design = weights.astype(jnp.bfloat16)
    cross = jnp.dot(design.astype(jnp.float32), methyl.astype(jnp.float32), preferred_element_type=jnp.float32)
    wgram = jnp.dot(design.astype(jnp.float32), design.T.astype(jnp.float32), preferred_element_type=jnp.float32)
    loadings = ridge_solve(wgram, cross, 0.0001 * SAMPLES)
    fitted = lax.dot_general(design.astype(jnp.float32), loadings, (((0,), (0,)), ((), ())), precision=lax.Precision.HIGHEST)
    residual = methyl.astype(jnp.float32) - fitted
    spread = lax.optimization_barrier(jnp.sum(residual * residual, axis=0))
    zscore = (residual * lax.rsqrt(spread / SAMPLES + 1e-06)).astype(jnp.bfloat16)
    blocks = zscore.reshape(PANELS, PANEL, PROBES)

    def tiles_of(index):
        first_block = blocks[index]
        before = blocks[(index + PANELS - 1) % PANELS]
        after = blocks[(index + 1) % PANELS]
        return jnp.stack([lax.dot_general(first_block.astype(jnp.float32), first_block.astype(jnp.float32), (((1,), (1,)), ((), ())), preferred_element_type=jnp.float32), lax.dot_general(first_block.astype(jnp.float32), before.astype(jnp.float32), (((1,), (1,)), ((), ())), preferred_element_type=jnp.float32), lax.dot_general(first_block.astype(jnp.float32), after.astype(jnp.float32), (((1,), (1,)), ((), ())), preferred_element_type=jnp.float32)])
    tiles = lax.map(tiles_of, jnp.arange(PANELS, dtype=jnp.int32))
    tiles = jnp.transpose(tiles, (1, 0, 2, 3)).reshape(3, SAMPLES, PANEL)
    return (tiles / PROBES, scores)
```

```python
import functools

import jax
import jax.numpy as jnp
from jax import lax
from jax.experimental import pallas as pl
from jax.experimental.pallas import tpu as pltpu
from jax.sharding import PartitionSpec as P

K = 32
ITERS = 128
F32, BF16 = jnp.float32, jnp.bfloat16
HIGHEST = lax.Precision.HIGHEST
LANES = 128
VMEM_LIMIT = 60 * 1024 * 1024


def nt(a, b):
    return lax.dot_general(a, b, (((1,), (1,)), ((), ())), preferred_element_type=F32)


def tn(a, b):
    return lax.dot_general(a, b, (((0,), (0,)), ((), ())), preferred_element_type=F32)


def params(*semantics):
    return pltpu.CompilerParams(dimension_semantics=semantics, vmem_limit_bytes=VMEM_LIMIT)


def cost(flops, nbytes):
    return pl.CostEstimate(flops=int(flops), bytes_accessed=int(nbytes), transcendentals=0)


def three_terms(value):
    high = value.astype(BF16)
    rest = value - high.astype(F32)
    mid = rest.astype(BF16)
    low = (rest - mid.astype(F32)).astype(BF16)
    return jnp.concatenate([high, mid, low], axis=0)


def project_kernel(ids_ref, atlas_ref, methyl_ref, out_ref, panel_ref, gram_ref):
    kk = panel_ref.shape[0]

    @pl.when(pl.program_id(0) == 0)
    def _():
        rows = atlas_ref.shape[0]
        pick = ids_ref[...] == lax.broadcasted_iota(jnp.int32, (kk, rows), 1)
        chosen = jnp.where(pick, 1.0, 0.0).astype(BF16)
        panel = jnp.dot(chosen, atlas_ref[...], preferred_element_type=F32).astype(BF16)
        panel_ref[...] = panel
        gram_ref[...] = nt(panel, panel)

    out_ref[0, :kk, :] = nt(panel_ref[...], methyl_ref[...])
    out_ref[0, kk:, :] = jnp.zeros((kk, out_ref.shape[2]), F32)
    out_ref[0, kk:, :kk] = gram_ref[...]


def project(panel_ids, atlas, methyl, shares):
    rows, probes = methyl.shape
    share = rows // shares
    return pl.pallas_call(
        project_kernel,
        grid=(shares,),
        in_specs=[
            pl.BlockSpec((K, 1), lambda i: (0, 0)),
            pl.BlockSpec(atlas.shape, lambda i: (0, 0)),
            pl.BlockSpec((share, probes), lambda i: (i, 0)),
        ],
        out_specs=pl.BlockSpec((1, 2 * K, share), lambda i: (i, 0, 0)),
        out_shape=jax.ShapeDtypeStruct((shares, 2 * K, share), F32),
        scratch_shapes=[pltpu.VMEM((K, probes), BF16), pltpu.VMEM((K, K), F32)],
        compiler_params=params("arbitrary"),
        cost_estimate=cost(2 * K * rows * probes, 2 * rows * probes),
        name="project",
    )(panel_ids[:K, None], atlas, methyl)


def descend_kernel(parts_ref, scores_ref, design_ref, spread_ref, w_ref):
    kk, share = w_ref.shape
    total = parts_ref[0]
    for peer in range(1, parts_ref.shape[0]):
        total = total + parts_ref[peer]
    gram = total[kk:, :kk]
    row = lax.broadcasted_iota(jnp.int32, (kk, kk), 0)
    col = lax.broadcasted_iota(jnp.int32, (kk, kk), 1)
    trace = jnp.sum(jnp.where(row == col, gram, 0.0), axis=(0, 1), keepdims=True)
    rate = 1.0 / trace
    step = jnp.where(row == col, 1.0, 0.0) - rate * gram
    pull = rate * total[:kk, :]
    for k in range(kk):
        spread_ref[k] = jnp.broadcast_to(step[:, k : k + 1], (kk, share))
    w_ref[...] = jnp.full((kk, share), 1.0 / kk, F32)

    def descend(_, carry):
        acc = [pull, None, None, None]
        for k in range(kk):
            term = spread_ref[k] * w_ref[k : k + 1, :]
            acc[k % 4] = term if acc[k % 4] is None else acc[k % 4] + term
        w_ref[...] = jnp.maximum((acc[0] + acc[1]) + (acc[2] + acc[3]), 0.0)
        return carry

    lax.fori_loop(0, ITERS, descend, 0)
    weights = w_ref[...]
    scores_ref[...] = kk * weights
    design = weights.astype(BF16)
    for peer in range(design_ref.shape[0]):
        design_ref[peer] = design


def descend(parts):
    shares, _, share = parts.shape
    return pl.pallas_call(
        descend_kernel,
        out_shape=(
            jax.ShapeDtypeStruct((K, share), F32),
            jax.ShapeDtypeStruct((shares, K, share), BF16),
        ),
        scratch_shapes=[pltpu.VMEM((K, K, share), F32), pltpu.VMEM((K, share), F32)],
        compiler_params=params(),
        cost_estimate=cost(2 * ITERS * K * K * share, 4 * K * share),
        name="descend",
    )(parts)


def cross_kernel(design_ref, methyl_ref, out_ref):
    kk = design_ref.shape[1]
    probes = methyl_ref.shape[1]
    design = design_ref[0]
    cross = jnp.dot(design, methyl_ref[...], preferred_element_type=F32)
    wgram = nt(design, design)

    @pl.when(pl.program_id(0) == 0)
    def _():
        out_ref[:, :probes] = cross
        out_ref[:, probes:] = jnp.zeros((kk, LANES), F32)
        out_ref[:, probes : probes + kk] = wgram

    @pl.when(pl.program_id(0) > 0)
    def _():
        out_ref[:, :probes] += cross
        out_ref[:, probes : probes + kk] += wgram


def cross_products(design, methyl):
    shares, _, share = design.shape
    rows, probes = methyl.shape
    return pl.pallas_call(
        cross_kernel,
        grid=(shares,),
        in_specs=[
            pl.BlockSpec((1, K, share), lambda i: (i, 0, 0)),
            pl.BlockSpec((share, probes), lambda i: (i, 0)),
        ],
        out_specs=pl.BlockSpec((K, probes + LANES), lambda i: (0, 0)),
        out_shape=jax.ShapeDtypeStruct((K, probes + LANES), F32),
        compiler_params=params("arbitrary"),
        cost_estimate=cost(2 * K * rows * probes, 2 * rows * probes),
        name="cross",
    )(design, methyl)


def ridge_inverse(matrix):
    kk = matrix.shape[0]
    row = lax.broadcasted_iota(jnp.int32, (kk, kk), 0)
    col = lax.broadcasted_iota(jnp.int32, (kk, kk), 1)
    work = jnp.concatenate([matrix, jnp.where(row == col, 1.0, 0.0)], axis=1)
    which = lax.broadcasted_iota(jnp.int32, (kk, 1), 0)
    for k in range(kk):
        pivot_row = work[k : k + 1, :] / work[k : k + 1, k : k + 1]
        factor = jnp.where(which == k, 0.0, work[:, k : k + 1])
        work = jnp.where(which == k, pivot_row, work - factor * pivot_row)
    return work[:, kk:]


def solve_kernel(ridge, peers, *refs):
    part_refs, (design_ref, methyl_ref, terms_ref, spread_ref) = refs[:peers], refs[peers:]
    kk = design_ref.shape[1]
    probes = methyl_ref.shape[1]

    @pl.when(pl.program_id(0) == 0)
    def _():
        total = part_refs[0][...]
        for ref in part_refs[1:]:
            total = total + ref[...]
        cross = total[:, :probes]
        wgram = total[:, probes : probes + kk]
        row = lax.broadcasted_iota(jnp.int32, (kk, kk), 0)
        col = lax.broadcasted_iota(jnp.int32, (kk, kk), 1)
        system = wgram + jnp.where(row == col, ridge, 0.0)
        inverse = ridge_inverse(system)
        loadings = jnp.dot(inverse, cross, precision=HIGHEST)
        short = cross - jnp.dot(system, loadings, precision=HIGHEST)
        loadings = loadings + jnp.dot(inverse, short, precision=HIGHEST)
        terms_ref[...] = three_terms(loadings)
        spread_ref[...] = jnp.zeros_like(spread_ref)

    design = design_ref[0]
    fitted = tn(jnp.concatenate([design] * 3, axis=0), terms_ref[...])
    residual = methyl_ref[...].astype(F32) - fitted
    spread_ref[...] += jnp.sum(residual * residual, axis=0, keepdims=True)


def solve(parts, design, methyl, ridge):
    shares, _, share = design.shape
    rows, probes = methyl.shape
    whole = pl.BlockSpec((K, probes + LANES), lambda i: (0, 0))
    return pl.pallas_call(
        functools.partial(solve_kernel, ridge, len(parts)),
        grid=(shares,),
        in_specs=[whole] * len(parts)
        + [
            pl.BlockSpec((1, K, share), lambda i: (i, 0, 0)),
            pl.BlockSpec((share, probes), lambda i: (i, 0)),
        ],
        out_specs=(
            pl.BlockSpec((3 * K, probes), lambda i: (0, 0)),
            pl.BlockSpec((1, probes), lambda i: (0, 0)),
        ),
        out_shape=(
            jax.ShapeDtypeStruct((3 * K, probes), BF16),
            jax.ShapeDtypeStruct((1, probes), F32),
        ),
        compiler_params=params("arbitrary"),
        cost_estimate=cost(6 * K * rows * probes, 2 * rows * probes),
        name="solve",
    )(*parts, design, methyl)


def standardised(design, terms, methyl, rate):
    fitted = tn(jnp.concatenate([design] * 3, axis=0), terms)
    return ((methyl.astype(F32) - fitted) * rate).astype(BF16)


def zscore_kernel(
    samples, design_ref, mine_ref, theirs_ref, terms_ref, more_ref, spread_ref, out_ref
):
    probes = mine_ref.shape[1]
    rate = lax.rsqrt(spread_ref[...] / samples + 1e-06)
    design = design_ref[0]
    out_ref[:, :probes] = standardised(design, terms_ref[...], mine_ref[...], rate[:1])
    out_ref[:, probes:] = standardised(design, more_ref[...], theirs_ref[...], rate[1:])


def zscores(design, mine, theirs, terms, more, spread, samples):
    blocks, _, share = design.shape
    rows, probes = mine.shape
    return pl.pallas_call(
        functools.partial(zscore_kernel, samples),
        grid=(blocks,),
        in_specs=[
            pl.BlockSpec((1, K, share), lambda i: (i, 0, 0)),
            pl.BlockSpec((share, probes), lambda i: (i, 0)),
            pl.BlockSpec((share, probes), lambda i: (i, 0)),
            pl.BlockSpec((3 * K, probes), lambda i: (0, 0)),
            pl.BlockSpec((3 * K, probes), lambda i: (0, 0)),
            pl.BlockSpec((2, probes), lambda i: (0, 0)),
        ],
        out_specs=pl.BlockSpec((share, 2 * probes), lambda i: (i, 0)),
        out_shape=jax.ShapeDtypeStruct((rows, 2 * probes), BF16),
        compiler_params=params("arbitrary"),
        cost_estimate=cost(12 * K * rows * probes, 8 * rows * probes),
        name="zscores",
    )(design, mine, theirs, terms, more, spread)


def tile_kernel(order_ref, left_ref, right_ref, sends_ref, keep_ref):
    part = nt(left_ref[...], right_ref[...])
    sends_ref[0] = part.astype(BF16)

    @pl.when(pl.program_id(0) == 0)
    def _():
        keep_ref[...] = part


def tile_parts(order, left, right, steps):
    rows, depth = left.shape
    share = rows // (2 * steps)
    return pl.pallas_call(
        tile_kernel,
        grid_spec=pltpu.PrefetchScalarGridSpec(
            num_scalar_prefetch=1,
            grid=(steps,),
            in_specs=[
                pl.BlockSpec((rows, depth), lambda j, order: (0, 0)),
                pl.BlockSpec((share, depth), lambda j, order: (order[j], 0)),
            ],
            out_specs=[
                pl.BlockSpec((1, rows, share), lambda j, order: (j, 0, 0)),
                pl.BlockSpec((rows, share), lambda j, order: (0, 0)),
            ],
        ),
        out_shape=(
            jax.ShapeDtypeStruct((steps, rows, share), BF16),
            jax.ShapeDtypeStruct((rows, share), F32),
        ),
        compiler_params=params("arbitrary"),
        cost_estimate=cost(2 * rows * share * steps * depth, 4 * rows * depth),
        name="tile",
    )(order, left, right)


def body(methyl, atlas, panel_ids):
    panels, shares = lax.axis_size("samp"), lax.axis_size("probe")
    rows = methyl.shape[0]
    samples = rows * panels
    probes = methyl.shape[1] * shares
    share = rows // shares
    line = shares // 2
    position = lax.axis_index("probe")
    place, core = position // 2, position % 2

    def to_sibling(value):
        return lax.ppermute(value, "probe", [(i, i ^ 1) for i in range(shares)])

    def to_panel(value, by):
        return lax.ppermute(value, "samp", [(i, (i + by) % panels) for i in range(panels)])

    def along_line(value, by):
        pairs = [(2 * i + c, 2 * ((i + by) % line) + c) for i in range(line) for c in (0, 1)]
        return lax.ppermute(value, "probe", pairs)

    def own_half(value):
        halves = value.reshape(line, 2, share, value.shape[1])
        return lax.dynamic_index_in_dim(halves, core, 1, False).reshape(line * share, -1)

    theirs = to_sibling(methyl)
    before_mine = to_panel(own_half(methyl), 1)
    before_theirs = to_panel(own_half(theirs), 1)

    parts = project(panel_ids, atlas, methyl, shares)
    parts = lax.all_to_all(parts, "probe", 0, 0)
    scores, copies = descend(parts)
    design = lax.all_to_all(copies, "probe", 0, 0)
    design_before = to_panel(
        lax.dynamic_index_in_dim(design.reshape(line, 2, K, share), core, 1, False), 1
    )

    part = cross_products(design, methyl)
    parts = [part] + [to_panel(part, by) for by in range(1, panels)]
    terms, spread = solve(parts, design, methyl, 0.0001 * samples)
    more = to_sibling(terms)
    spread = jnp.concatenate([spread, to_sibling(spread)], axis=0)
    spread = sum([to_panel(spread, by) for by in range(1, panels)], spread)

    zscore = zscores(design, methyl, theirs, terms, more, spread, samples)
    ahead = (place + jnp.arange(line, dtype=jnp.int32)) % line

    def reduced(left, right, order):
        sends, keep = tile_parts(order, left, right, line)
        arrived = [along_line(sends[j], j) for j in range(1, line)]
        return sum([a.astype(F32) for a in arrived], keep)

    own = reduced(zscore, zscore, 2 * ahead + core)
    zbefore = zscores(design_before, before_mine, before_theirs, terms, more, spread, samples)
    left = reduced(zscore, zbefore, ahead)
    blocks = lax.all_to_all(left.reshape(shares, share, share), "probe", 0, 0)
    blocks = to_panel(blocks, -1)
    after = jnp.swapaxes(blocks, 1, 2).reshape(rows, share)
    return jnp.stack([own, left, after]) / probes, scores


def solution(mesh):
    placed = (P("samp", "probe"), P(None, "probe"), P())
    return jax.shard_map(
        body,
        mesh=mesh,
        in_specs=placed,
        out_specs=(P(None, "samp", "probe"), P(None, ("samp", "probe"))),
        check_vma=False,
    )
```

```python
import functools

import jax
import jax.numpy as jnp
from jax import lax
from jax.experimental import pallas as pl
from jax.experimental.pallas import tpu as pltpu
from jax.sharding import PartitionSpec as P

K = 32
ITERS = 128
F32, BF16 = jnp.float32, jnp.bfloat16
HIGHEST = lax.Precision.HIGHEST
LANES = 128
VMEM_LIMIT = 60 * 1024 * 1024


def nt(a, b):
    return lax.dot_general(a, b, (((1,), (1,)), ((), ())), preferred_element_type=F32)


def tn(a, b):
    return lax.dot_general(a, b, (((0,), (0,)), ((), ())), preferred_element_type=F32)


def params(*semantics):
    return pltpu.CompilerParams(dimension_semantics=semantics, vmem_limit_bytes=VMEM_LIMIT)


def cost(flops, nbytes):
    return pl.CostEstimate(flops=int(flops), bytes_accessed=int(nbytes), transcendentals=0)


def three_terms(value):
    high = value.astype(BF16)
    rest = value - high.astype(F32)
    mid = rest.astype(BF16)
    low = (rest - mid.astype(F32)).astype(BF16)
    return jnp.concatenate([high, mid, low], axis=0)


def project_kernel(core_ref, ids_ref, atlas_ref, methyl_ref, out_ref, panel_ref, same_ref, other_ref, gram_ref):
    kk = panel_ref.shape[0]
    blocks, _, share = out_ref.shape
    core = core_ref[0]

    @pl.when(pl.program_id(0) == 0)
    def _():
        rows = atlas_ref.shape[0]
        row = lax.broadcasted_iota(jnp.int32, (kk, rows), 0)
        wanted = jnp.zeros((kk, rows), jnp.int32)
        for k in range(kk):
            wanted = jnp.where(row == k, ids_ref[k], wanted)
        pick = wanted == lax.broadcasted_iota(jnp.int32, (kk, rows), 1)
        chosen = jnp.where(pick, 1.0, 0.0).astype(BF16)
        panel = jnp.dot(chosen, atlas_ref[...], preferred_element_type=F32).astype(BF16)
        panel_ref[...] = panel
        gram_ref[...] = nt(panel, panel)

    proj = nt(methyl_ref[...], panel_ref[...]).T
    for b in range(blocks):
        out_ref[b, :kk, :] = proj[:, b * share : (b + 1) * share]
        out_ref[b, kk:, :] = jnp.zeros((kk, share), F32)
        out_ref[b, kk:, :kk] = gram_ref[...]
    for b in range(blocks // 2):
        same = pl.multiple_of((2 * b + core) * share, share)
        other = pl.multiple_of((2 * b + 1 - core) * share, share)
        same_ref[b * share : (b + 1) * share, :] = methyl_ref[pl.ds(same, share), :]
        other_ref[b * share : (b + 1) * share, :] = methyl_ref[pl.ds(other, share), :]


def project(core, panel_ids, atlas, methyl, shares):
    rows, probes = methyl.shape
    share = rows // shares
    chunk = row_chunk(share)
    half = pl.BlockSpec((chunk // 2, probes), lambda i: (i, 0))
    return pl.pallas_call(
        project_kernel,
        grid=(rows // chunk,),
        in_specs=[
            pl.BlockSpec(memory_space=pltpu.SMEM),
            pl.BlockSpec(memory_space=pltpu.SMEM),
            pl.BlockSpec(atlas.shape, lambda i: (0, 0)),
            pl.BlockSpec((chunk, probes), lambda i: (i, 0)),
        ],
        out_specs=(
            pl.BlockSpec((chunk // share, 2 * K, share), lambda i: (i, 0, 0)),
            pl.BlockSpec((K, probes), lambda i: (0, 0)),
            half,
            half,
        ),
        out_shape=(
            jax.ShapeDtypeStruct((shares, 2 * K, share), F32),
            jax.ShapeDtypeStruct((K, probes), BF16),
            jax.ShapeDtypeStruct((rows // 2, probes), BF16),
            jax.ShapeDtypeStruct((rows // 2, probes), BF16),
        ),
        scratch_shapes=[pltpu.VMEM((K, K), F32)],
        compiler_params=params("arbitrary"),
        cost_estimate=cost(2 * K * rows * probes, 4 * rows * probes),
        name="project",
    )(core, panel_ids, atlas, methyl)


def row_chunk(share):
    return 2 * share * max(1, 128 // share)


def descend_kernel(parts_ref, scores_ref, design_ref, spread_ref, w_ref):
    kk, share = w_ref.shape
    total = parts_ref[0]
    for peer in range(1, parts_ref.shape[0]):
        total = total + parts_ref[peer]
    gram = total[kk:, :kk]
    row = lax.broadcasted_iota(jnp.int32, (kk, kk), 0)
    col = lax.broadcasted_iota(jnp.int32, (kk, kk), 1)
    trace = jnp.sum(jnp.where(row == col, gram, 0.0), axis=(0, 1), keepdims=True)
    rate = 1.0 / trace
    step = jnp.where(row == col, 1.0, 0.0) - rate * gram
    pull = rate * total[:kk, :]
    for k in range(kk):
        spread_ref[k] = jnp.broadcast_to(step[:, k : k + 1], (kk, share))
    w_ref[...] = jnp.full((kk, share), 1.0 / kk, F32)

    def descend(_, carry):
        acc = [pull, None, None, None]
        for k in range(kk):
            term = spread_ref[k] * w_ref[k : k + 1, :]
            acc[k % 4] = term if acc[k % 4] is None else acc[k % 4] + term
        w_ref[...] = jnp.maximum((acc[0] + acc[1]) + (acc[2] + acc[3]), 0.0)
        return carry

    lax.fori_loop(0, ITERS, descend, 0)
    weights = w_ref[...]
    scores_ref[...] = kk * weights
    design = weights.astype(BF16)
    for peer in range(design_ref.shape[0]):
        design_ref[peer] = design


def descend(parts):
    shares, _, share = parts.shape
    return pl.pallas_call(
        descend_kernel,
        out_shape=(
            jax.ShapeDtypeStruct((K, share), F32),
            jax.ShapeDtypeStruct((shares, K, share), BF16),
        ),
        scratch_shapes=[pltpu.VMEM((K, K, share), F32), pltpu.VMEM((K, share), F32)],
        compiler_params=params(),
        cost_estimate=cost(2 * ITERS * K * K * share, 4 * K * share),
        name="descend",
    )(parts)


def cross_kernel(design_ref, methyl_ref, panel_ref, out_ref):
    blocks, kk, share = design_ref.shape
    probes = methyl_ref.shape[1]
    design = jnp.concatenate([design_ref[b] for b in range(blocks)], axis=1)

    @pl.when(pl.program_id(0) == 0)
    def _():
        out_ref[...] = jnp.zeros_like(out_ref)

    out_ref[:, probes : probes + kk] += nt(design, design)
    width = min(probes, 512)
    for at in range(0, probes, width):
        cols = slice(at, at + width)
        out_ref[:, cols] += jnp.dot(design, methyl_ref[:, cols], preferred_element_type=F32)
        left = methyl_ref[:, cols].astype(F32) - tn(design, panel_ref[:, cols])
        squares = jnp.sum(left * left, axis=0, keepdims=True)
        for b in range(0, width, LANES):
            row = (at + b) // LANES
            out_ref[row : row + 1, probes + LANES :] += squares[:, b : b + LANES]


def cross_products(design, methyl, panel):
    shares, _, share = design.shape
    rows, probes = methyl.shape
    chunk = row_chunk(share)
    return pl.pallas_call(
        cross_kernel,
        grid=(rows // chunk,),
        in_specs=[
            pl.BlockSpec((chunk // share, K, share), lambda i: (i, 0, 0)),
            pl.BlockSpec((chunk, probes), lambda i: (i, 0)),
            pl.BlockSpec((K, probes), lambda i: (0, 0)),
        ],
        out_specs=pl.BlockSpec((K, probes + 2 * LANES), lambda i: (0, 0)),
        out_shape=jax.ShapeDtypeStruct((K, probes + 2 * LANES), F32),
        compiler_params=params("arbitrary"),
        cost_estimate=cost(4 * K * rows * probes, 2 * rows * probes),
        name="cross",
    )(design, methyl, panel)


def ridge_inverse(matrix):
    kk = matrix.shape[0]
    row = lax.broadcasted_iota(jnp.int32, (kk, kk), 0)
    col = lax.broadcasted_iota(jnp.int32, (kk, kk), 1)
    work = jnp.concatenate([matrix, jnp.where(row == col, 1.0, 0.0)], axis=1)
    which = lax.broadcasted_iota(jnp.int32, (kk, 1), 0)
    for k in range(kk):
        pivot_row = work[k : k + 1, :] / work[k : k + 1, k : k + 1]
        factor = jnp.where(which == k, 0.0, work[:, k : k + 1])
        work = jnp.where(which == k, pivot_row, work - factor * pivot_row)
    return work[:, kk:]


def solve_kernel(ridge, samples, mine_ref, peer_ref, panel_ref, out_ref):
    kk, probes = panel_ref.shape
    total = mine_ref[...] + peer_ref[...]
    cross = total[:, :probes]
    wgram = total[:, probes : probes + kk]
    start = jnp.concatenate(
        [total[r : r + 1, probes + LANES :] for r in range(probes // LANES)], axis=1
    )
    row = lax.broadcasted_iota(jnp.int32, (kk, kk), 0)
    col = lax.broadcasted_iota(jnp.int32, (kk, kk), 1)
    system = wgram + jnp.where(row == col, ridge, 0.0)
    inverse = ridge_inverse(system)
    loadings = jnp.dot(inverse, cross, precision=HIGHEST)
    short = cross - jnp.dot(system, loadings, precision=HIGHEST)
    loadings = loadings + jnp.dot(inverse, short, precision=HIGHEST)
    panel = panel_ref[...].astype(F32)
    slope = jnp.dot(wgram, loadings + panel, precision=HIGHEST) - 2.0 * cross
    spread = start + jnp.sum((loadings - panel) * slope, axis=0, keepdims=True)
    rate = lax.rsqrt(jnp.maximum(spread, 0.0) / samples + 1e-06)
    out_ref[:kk, :] = loadings
    out_ref[kk:, :] = jnp.broadcast_to(rate, (out_ref.shape[0] - kk, probes))


def solve(mine, peer, panel, ridge, samples):
    probes = panel.shape[1]
    return pl.pallas_call(
        functools.partial(solve_kernel, ridge, samples),
        out_shape=jax.ShapeDtypeStruct((K + 8, probes), F32),
        compiler_params=params(),
        cost_estimate=cost(50 * K * K * probes, 20 * K * probes),
        name="solve",
    )(mine, peer, panel)


def standardise(design, methyl_ref, terms_ref, rate, store):
    probes = methyl_ref.shape[1]
    stacked = jnp.concatenate([design] * 3, axis=0)
    width = min(probes, 512)
    for at in range(0, probes, width):
        cols = slice(at, at + width)
        fitted = tn(stacked, terms_ref[:, cols])
        left = methyl_ref[:, cols].astype(F32) - fitted
        store(at, width, (left * rate[:, cols]).astype(BF16))


def put_tile(left, right, slots_ref, sends_ref, keep_ref):
    share = keep_ref.shape[1]
    part = nt(left, right)
    for p in range(right.shape[0] // share):
        block = part[:, p * share : (p + 1) * share]
        slot = slots_ref[p]

        @pl.when(slot < 0)
        def _():
            keep_ref[...] = block

        @pl.when(slot >= 0)
        def _():
            sends_ref[jnp.maximum(slot, 0)] = block.astype(BF16)


def own_kernel(
    steps, slots_ref, core_ref, design_ref, mine_ref, theirs_ref, facts_ref, more_ref,
    zscore_ref, sends_ref, keep_ref, z_ref, half_ref, terms_ref, moreterms_ref,
):
    step = pl.program_id(0)
    blocks, kk, share = design_ref.shape
    chunk, probes = mine_ref.shape
    core = core_ref[0]

    @pl.when(step == 0)
    def _():
        terms_ref[...] = three_terms(facts_ref[:kk, :])
        moreterms_ref[...] = three_terms(more_ref[:kk, :])

    @pl.when(step < steps)
    def _():
        design = jnp.concatenate([design_ref[b] for b in range(blocks)], axis=1)
        rows = pl.ds(pl.multiple_of(step * chunk, chunk), chunk)

        def store(base, at, width, value):
            zscore_ref[:, base + at : base + at + width] = value
            z_ref[rows, base + at : base + at + width] = value

        standardise(design, mine_ref, terms_ref, facts_ref[kk : kk + 1, :], functools.partial(store, 0))
        standardise(
            design, theirs_ref, moreterms_ref, more_ref[kk : kk + 1, :], functools.partial(store, probes)
        )
        for b in range(blocks // 2):
            here = pl.ds(pl.multiple_of((2 * b + core) * share, share), share)
            there = pl.ds(pl.multiple_of(step * (chunk // 2) + b * share, share), share)
            half_ref[there, :] = zscore_ref[here, :]

    @pl.when(step >= steps)
    def _():
        rows = pl.ds(pl.multiple_of((step - steps) * chunk, chunk), chunk)
        put_tile(z_ref[rows, :], half_ref[...], slots_ref, sends_ref, keep_ref)


def own_tile(slots, core, rounds, design, mine, theirs, facts, more):
    shares, _, share = design.shape
    rows, probes = mine.shape
    chunk = row_chunk(share)
    steps = rows // chunk

    def first(i, *_):
        return (jnp.minimum(i, steps - 1), 0)

    def second(i, *_):
        return (jnp.maximum(i - steps, 0), 0)

    whole = pl.BlockSpec((K + 8, probes), lambda i, *_: (0, 0))
    return pl.pallas_call(
        functools.partial(own_kernel, steps),
        grid_spec=pltpu.PrefetchScalarGridSpec(
            num_scalar_prefetch=2,
            grid=(2 * steps,),
            in_specs=[
                pl.BlockSpec((chunk // share, K, share), lambda i, *_: (*first(i), 0)),
                pl.BlockSpec((chunk, probes), first),
                pl.BlockSpec((chunk, probes), first),
                whole,
                whole,
            ],
            out_specs=[
                pl.BlockSpec((chunk, 2 * probes), first),
                pl.BlockSpec((rounds, chunk, share), lambda i, *_: (0, *second(i))),
                pl.BlockSpec((chunk, share), second),
            ],
            scratch_shapes=[
                pltpu.VMEM((rows, 2 * probes), BF16),
                pltpu.VMEM((rows // 2, 2 * probes), BF16),
                pltpu.VMEM((3 * K, probes), BF16),
                pltpu.VMEM((3 * K, probes), BF16),
            ],
        ),
        out_shape=(
            jax.ShapeDtypeStruct((rows, 2 * probes), BF16),
            jax.ShapeDtypeStruct((rounds, rows, share), BF16),
            jax.ShapeDtypeStruct((rows, share), F32),
        ),
        compiler_params=params("arbitrary"),
        cost_estimate=cost(2 * rows * rows * probes, 12 * rows * probes),
        name="own",
    )(slots, core, design, mine, theirs, facts, more)


def pair_kernel(
    steps, slots_ref, design_ref, mine_ref, theirs_ref, facts_ref, more_ref, zscore_ref,
    sends_ref, keep_ref, z_ref, terms_ref, moreterms_ref,
):
    step = pl.program_id(0)
    blocks, kk, share = design_ref.shape
    chunk, probes = mine_ref.shape

    @pl.when(step == 0)
    def _():
        terms_ref[...] = three_terms(facts_ref[:kk, :])
        moreterms_ref[...] = three_terms(more_ref[:kk, :])

    @pl.when(step < steps)
    def _():
        design = jnp.concatenate([design_ref[b] for b in range(blocks)], axis=1)
        rows = pl.ds(pl.multiple_of(step * chunk, chunk), chunk)

        def store(base, at, width, value):
            z_ref[rows, base + at : base + at + width] = value

        standardise(design, mine_ref, terms_ref, facts_ref[kk : kk + 1, :], functools.partial(store, 0))
        standardise(
            design, theirs_ref, moreterms_ref, more_ref[kk : kk + 1, :], functools.partial(store, probes)
        )

    @pl.when(step >= steps)
    def _():
        put_tile(zscore_ref[...], z_ref[...], slots_ref, sends_ref, keep_ref)


def pair_tile(slots, rounds, design, mine, theirs, facts, more, zscore):
    blocks, _, share = design.shape
    half, probes = mine.shape
    rows = zscore.shape[0]
    chunk = row_chunk(share)
    steps = half // chunk

    def first(i, *_):
        return (jnp.minimum(i, steps - 1), 0)

    def second(i, *_):
        return (jnp.maximum(i - steps, 0), 0)

    whole = pl.BlockSpec((K + 8, probes), lambda i, *_: (0, 0))
    return pl.pallas_call(
        functools.partial(pair_kernel, steps),
        grid_spec=pltpu.PrefetchScalarGridSpec(
            num_scalar_prefetch=1,
            grid=(steps + rows // chunk,),
            in_specs=[
                pl.BlockSpec((chunk // share, K, share), lambda i, *_: (*first(i), 0)),
                pl.BlockSpec((chunk, probes), first),
                pl.BlockSpec((chunk, probes), first),
                whole,
                whole,
                pl.BlockSpec((chunk, 2 * probes), second),
            ],
            out_specs=[
                pl.BlockSpec((rounds, chunk, share), lambda i, *_: (0, *second(i))),
                pl.BlockSpec((chunk, share), second),
            ],
            scratch_shapes=[
                pltpu.VMEM((half, 2 * probes), BF16),
                pltpu.VMEM((3 * K, probes), BF16),
                pltpu.VMEM((3 * K, probes), BF16),
            ],
        ),
        out_shape=(
            jax.ShapeDtypeStruct((rounds, rows, share), BF16),
            jax.ShapeDtypeStruct((rows, share), F32),
        ),
        compiler_params=params("arbitrary"),
        cost_estimate=cost(2 * rows * rows * probes, 8 * rows * probes),
        name="pair",
    )(slots, design, mine, theirs, facts, more, zscore)


def line_rounds(line):
    far = line > 3
    rounds = [[(0, 1), (line - 1, line - 2)] if far else []]
    slots = [[-1] * line for _ in range(line)]
    for j in range(1, line):
        pairs = []
        for i in range(line):
            to = (i + j) % line
            if far and abs(to - i) == line - 1:
                slots[i][to] = 0
            else:
                pairs.append((i, to))
                slots[i][to] = j
        rounds.append(pairs)
    return rounds, slots


def body(methyl, atlas, panel_ids):
    panels, shares = lax.axis_size("samp"), lax.axis_size("probe")
    rows = methyl.shape[0]
    samples = rows * panels
    probes = methyl.shape[1] * shares
    share = rows // shares
    line = shares // 2
    position = lax.axis_index("probe")
    place, core = position // 2, position % 2
    core_only = core[None]

    def to_sibling(value):
        return lax.ppermute(value, "probe", [(i, i ^ 1) for i in range(shares)])

    def to_panel(value, by):
        return lax.ppermute(value, "samp", [(i, (i + by) % panels) for i in range(panels)])

    def to_panel_sibling(value, by):
        pairs = [
            (s * shares + i, ((s + by) % panels) * shares + (i ^ 1))
            for s in range(panels)
            for i in range(shares)
        ]
        return lax.ppermute(value, ("samp", "probe"), pairs)

    def swap_panels(value, bit):
        return lax.ppermute(value, "samp", [(i, i ^ bit) for i in range(panels)])

    theirs = to_sibling(methyl)
    parts, panel, same, other = project(core_only, panel_ids, atlas, methyl, shares)
    before_mine = to_panel(same, 1)
    parts = lax.all_to_all(parts, "probe", 0, 0)
    scores, copies = descend(parts)
    design = lax.all_to_all(copies, "probe", 0, 0)
    part = cross_products(design, methyl, panel)
    bit = panels // 2
    while bit > 1:
        part = part + swap_panels(part, bit)
        bit //= 2
    peer = swap_panels(part, 1)
    other, peer = lax.optimization_barrier((other, peer))
    before_theirs = to_panel_sibling(other, 1)
    facts = solve(part, peer, panel, 0.0001 * samples, samples)
    more = to_sibling(facts)
    design_before = to_panel(
        lax.dynamic_index_in_dim(design.reshape(line, 2, K, share), core, 1, False), 1
    )

    rounds, table = line_rounds(line)
    slots = jnp.take(jnp.array(table, jnp.int32), place, axis=0)

    def reduced(sends, keep):
        def send(value, pairs):
            return lax.ppermute(
                value, "probe", [(2 * i + c, 2 * to + c) for i, to in pairs for c in (0, 1)]
            )

        relay = send(sends[0], rounds[0]) if rounds[0] else None
        total = keep
        for j in [*range(1, 2), *range(line - 1, 1, -1)]:
            value = sends[j]
            if relay is not None and j in (2, line - 2):
                at = (place == line - 2) & (j == 2) | (place == 1) & (j == line - 2)
                value = jnp.where(at, value.astype(F32) + relay.astype(F32), value.astype(F32)).astype(BF16)
            total = total + send(value, rounds[j]).astype(F32)
        return total

    zscore, sends, keep = own_tile(slots, core_only, line, design, methyl, theirs, facts, more)
    own = reduced(sends, keep)
    left = reduced(
        *pair_tile(slots, line, design_before, before_mine, before_theirs, facts, more, zscore)
    )
    blocks = lax.all_to_all(left.astype(BF16).reshape(shares, share, share), "probe", 0, 0)
    blocks = to_panel(blocks, -1)
    after = jnp.swapaxes(blocks.astype(F32), 1, 2).reshape(rows, share)
    return jnp.stack([own, left, after]) / probes, scores


def solution(mesh):
    placed = (P("samp", "probe"), P(None, "probe"), P())
    return jax.shard_map(
        body,
        mesh=mesh,
        in_specs=placed,
        out_specs=(P(None, "samp", "probe"), P(None, ("samp", "probe"))),
        check_vma=False,
    )
```

```python
import functools

import jax
import jax.numpy as jnp
from jax import lax
from jax.experimental import pallas as pl
from jax.experimental.pallas import tpu as pltpu
from jax.sharding import PartitionSpec as P


K = 32
ITERS = 128
F32, BF16 = jnp.float32, jnp.bfloat16
HIGHEST = lax.Precision.HIGHEST
LANES = 128
VMEM_LIMIT = 60 * 1024 * 1024


def nt(a, b):
    return lax.dot_general(a, b, (((1,), (1,)), ((), ())), preferred_element_type=F32)


def tn(a, b):
    return lax.dot_general(a, b, (((0,), (0,)), ((), ())), preferred_element_type=F32)


def params(*semantics):
    return pltpu.CompilerParams(dimension_semantics=semantics, vmem_limit_bytes=VMEM_LIMIT)


def cost(flops, nbytes):
    return pl.CostEstimate(flops=int(flops), bytes_accessed=int(nbytes), transcendentals=0)


def three_terms(value):
    high = value.astype(BF16)
    rest = value - high.astype(F32)
    mid = rest.astype(BF16)
    low = (rest - mid.astype(F32)).astype(BF16)
    return jnp.concatenate([high, mid, low], axis=0)


def project_kernel(core_ref, ids_ref, atlas_ref, methyl_ref, out_ref, panel_ref, same_ref, other_ref, gram_ref):
    kk = panel_ref.shape[0]
    blocks, _, share = out_ref.shape
    core = core_ref[0]

    @pl.when(pl.program_id(0) == 0)
    def _():
        rows = atlas_ref.shape[0]
        row = lax.broadcasted_iota(jnp.int32, (kk, rows), 0)
        wanted = jnp.zeros((kk, rows), jnp.int32)
        for k in range(kk):
            wanted = jnp.where(row == k, ids_ref[k], wanted)
        pick = wanted == lax.broadcasted_iota(jnp.int32, (kk, rows), 1)
        chosen = jnp.where(pick, 1.0, 0.0).astype(BF16)
        panel = jnp.dot(chosen, atlas_ref[...], preferred_element_type=F32).astype(BF16)
        panel_ref[...] = panel
        gram_ref[...] = nt(panel, panel)

    proj = nt(methyl_ref[...], panel_ref[...]).T
    for b in range(blocks):
        out_ref[b, :kk, :] = proj[:, b * share : (b + 1) * share]
        out_ref[b, kk:, :] = jnp.zeros((kk, share), F32)
        out_ref[b, kk:, :kk] = gram_ref[...]
    for b in range(blocks // 2):
        same = pl.multiple_of((2 * b + core) * share, share)
        other = pl.multiple_of((2 * b + 1 - core) * share, share)
        same_ref[b * share : (b + 1) * share, :] = methyl_ref[pl.ds(same, share), :]
        other_ref[b * share : (b + 1) * share, :] = methyl_ref[pl.ds(other, share), :]


def project(core, panel_ids, atlas, methyl, shares):
    rows, probes = methyl.shape
    share = rows // shares
    chunk = row_chunk(share)
    half = pl.BlockSpec((chunk // 2, probes), lambda i: (i, 0))
    return pl.pallas_call(
        project_kernel,
        grid=(rows // chunk,),
        in_specs=[
            pl.BlockSpec(memory_space=pltpu.SMEM),
            pl.BlockSpec(memory_space=pltpu.SMEM),
            pl.BlockSpec(atlas.shape, lambda i: (0, 0)),
            pl.BlockSpec((chunk, probes), lambda i: (i, 0)),
        ],
        out_specs=(
            pl.BlockSpec((chunk // share, 2 * K, share), lambda i: (i, 0, 0)),
            pl.BlockSpec((K, probes), lambda i: (0, 0)),
            half,
            half,
        ),
        out_shape=(
            jax.ShapeDtypeStruct((shares, 2 * K, share), F32),
            jax.ShapeDtypeStruct((K, probes), BF16),
            jax.ShapeDtypeStruct((rows // 2, probes), BF16),
            jax.ShapeDtypeStruct((rows // 2, probes), BF16),
        ),
        scratch_shapes=[pltpu.VMEM((K, K), F32)],
        compiler_params=params("arbitrary"),
        cost_estimate=cost(2 * K * rows * probes, 4 * rows * probes),
        name="project",
    )(core, panel_ids, atlas, methyl)


def row_chunk(share):
    return 2 * share * max(1, 128 // share)


def descend_kernel(parts_ref, scores_ref, design_ref, spread_ref, w_ref):
    kk, share = w_ref.shape
    total = parts_ref[0]
    for peer in range(1, parts_ref.shape[0]):
        total = total + parts_ref[peer]
    gram = total[kk:, :kk]
    row = lax.broadcasted_iota(jnp.int32, (kk, kk), 0)
    col = lax.broadcasted_iota(jnp.int32, (kk, kk), 1)
    trace = jnp.sum(jnp.where(row == col, gram, 0.0), axis=(0, 1), keepdims=True)
    rate = 1.0 / trace
    step = jnp.where(row == col, 1.0, 0.0) - rate * gram
    pull = rate * total[:kk, :]
    for k in range(kk):
        spread_ref[k] = jnp.broadcast_to(step[:, k : k + 1], (kk, share))
    w_ref[...] = jnp.full((kk, share), 1.0 / kk, F32)

    def descend(_, carry):
        acc = [pull, None, None, None]
        for k in range(kk):
            term = spread_ref[k] * w_ref[k : k + 1, :]
            acc[k % 4] = term if acc[k % 4] is None else acc[k % 4] + term
        w_ref[...] = jnp.maximum((acc[0] + acc[1]) + (acc[2] + acc[3]), 0.0)
        return carry

    lax.fori_loop(0, ITERS, descend, 0)
    weights = w_ref[...]
    scores_ref[...] = kk * weights
    design = weights.astype(BF16)
    for peer in range(design_ref.shape[0]):
        design_ref[peer] = design


def descend(parts):
    shares, _, share = parts.shape
    return pl.pallas_call(
        descend_kernel,
        out_shape=(
            jax.ShapeDtypeStruct((K, share), F32),
            jax.ShapeDtypeStruct((shares, K, share), BF16),
        ),
        scratch_shapes=[pltpu.VMEM((K, K, share), F32), pltpu.VMEM((K, share), F32)],
        compiler_params=params(),
        cost_estimate=cost(2 * ITERS * K * K * share, 4 * K * share),
        name="descend",
    )(parts)


def cross_kernel(design_ref, methyl_ref, panel_ref, out_ref):
    blocks, kk, _ = design_ref.shape
    probes = methyl_ref.shape[1]
    design = jnp.concatenate([design_ref[b] for b in range(blocks)], axis=1)

    @pl.when(pl.program_id(0) == 0)
    def _():
        out_ref[...] = jnp.zeros_like(out_ref)

    out_ref[:, probes : probes + kk] += nt(design, design)
    width = min(probes, 512)
    for at in range(0, probes, width):
        cols = slice(at, at + width)
        out_ref[:, cols] += jnp.dot(design, methyl_ref[:, cols], preferred_element_type=F32)
        left = methyl_ref[:, cols].astype(F32) - tn(design, panel_ref[:, cols])
        squares = jnp.sum(left * left, axis=0, keepdims=True)
        for b in range(0, width, LANES):
            row = (at + b) // LANES
            out_ref[row : row + 1, probes + LANES :] += squares[:, b : b + LANES]


def cross_products(design, methyl, panel):
    _, _, share = design.shape
    rows, probes = methyl.shape
    chunk = row_chunk(share)
    return pl.pallas_call(
        cross_kernel,
        grid=(rows // chunk,),
        in_specs=[
            pl.BlockSpec((chunk // share, K, share), lambda i: (i, 0, 0)),
            pl.BlockSpec((chunk, probes), lambda i: (i, 0)),
            pl.BlockSpec((K, probes), lambda i: (0, 0)),
        ],
        out_specs=pl.BlockSpec((K, probes + 2 * LANES), lambda i: (0, 0)),
        out_shape=jax.ShapeDtypeStruct((K, probes + 2 * LANES), F32),
        compiler_params=params("arbitrary"),
        cost_estimate=cost(4 * K * rows * probes, 2 * rows * probes),
        name="cross",
    )(design, methyl, panel)


def ridge_inverse(matrix):
    kk = matrix.shape[0]
    row = lax.broadcasted_iota(jnp.int32, (kk, kk), 0)
    col = lax.broadcasted_iota(jnp.int32, (kk, kk), 1)
    work = jnp.concatenate([matrix, jnp.where(row == col, 1.0, 0.0)], axis=1)
    which = lax.broadcasted_iota(jnp.int32, (kk, 1), 0)
    for k in range(kk):
        pivot_row = work[k : k + 1, :] / work[k : k + 1, k : k + 1]
        factor = jnp.where(which == k, 0.0, work[:, k : k + 1])
        work = jnp.where(which == k, pivot_row, work - factor * pivot_row)
    return work[:, kk:]


def solve_kernel(ridge, samples, mine_ref, peer_ref, panel_ref, out_ref):
    kk, probes = panel_ref.shape
    total = mine_ref[...] + peer_ref[...]
    cross = total[:, :probes]
    wgram = total[:, probes : probes + kk]
    start = jnp.concatenate(
        [total[r : r + 1, probes + LANES :] for r in range(probes // LANES)], axis=1
    )
    row = lax.broadcasted_iota(jnp.int32, (kk, kk), 0)
    col = lax.broadcasted_iota(jnp.int32, (kk, kk), 1)
    system = wgram + jnp.where(row == col, ridge, 0.0)
    inverse = ridge_inverse(system)
    loadings = jnp.dot(inverse, cross, precision=HIGHEST)
    short = cross - jnp.dot(system, loadings, precision=HIGHEST)
    loadings = loadings + jnp.dot(inverse, short, precision=HIGHEST)
    panel = panel_ref[...].astype(F32)
    slope = jnp.dot(wgram, loadings + panel, precision=HIGHEST) - 2.0 * cross
    spread = start + jnp.sum((loadings - panel) * slope, axis=0, keepdims=True)
    rate = lax.rsqrt(jnp.maximum(spread, 0.0) / samples + 1e-06)
    out_ref[:kk, :] = loadings
    out_ref[kk:, :] = jnp.broadcast_to(rate, (out_ref.shape[0] - kk, probes))


def solve(mine, peer, panel, ridge, samples):
    probes = panel.shape[1]
    return pl.pallas_call(
        functools.partial(solve_kernel, ridge, samples),
        out_shape=jax.ShapeDtypeStruct((K + 8, probes), F32),
        compiler_params=params(),
        cost_estimate=cost(50 * K * K * probes, 20 * K * probes),
        name="solve",
    )(mine, peer, panel)


def standardise(design, methyl_ref, terms_ref, rate, store):
    probes = methyl_ref.shape[1]
    stacked = jnp.concatenate([design] * 3, axis=0)
    width = min(probes, 512)
    for at in range(0, probes, width):
        cols = slice(at, at + width)
        fitted = tn(stacked, terms_ref[:, cols])
        left = methyl_ref[:, cols].astype(F32) - fitted
        store(at, width, (left * rate[:, cols]).astype(BF16))


def put_tile(left, right, slots_ref, sends_ref, keep_ref):
    share = keep_ref.shape[1]
    part = nt(left, right)
    for p in range(right.shape[0] // share):
        block = part[:, p * share : (p + 1) * share]
        slot = slots_ref[p]

        @pl.when(slot < 0)
        def _():
            keep_ref[...] = block

        @pl.when(slot >= 0)
        def _():
            sends_ref[jnp.maximum(slot, 0)] = block.astype(BF16)


def own_kernel(
    steps, slots_ref, core_ref, design_ref, mine_ref, theirs_ref, facts_ref, more_ref,
    zscore_ref, sends_ref, keep_ref, z_ref, half_ref, terms_ref, moreterms_ref,
):
    step = pl.program_id(0)
    blocks, kk, share = design_ref.shape
    chunk, probes = mine_ref.shape
    core = core_ref[0]

    @pl.when(step == 0)
    def _():
        terms_ref[...] = three_terms(facts_ref[:kk, :])
        moreterms_ref[...] = three_terms(more_ref[:kk, :])

    @pl.when(step < steps)
    def _():
        design = jnp.concatenate([design_ref[b] for b in range(blocks)], axis=1)
        rows = pl.ds(pl.multiple_of(step * chunk, chunk), chunk)

        def store(base, at, width, value):
            zscore_ref[:, base + at : base + at + width] = value
            z_ref[rows, base + at : base + at + width] = value

        standardise(design, mine_ref, terms_ref, facts_ref[kk : kk + 1, :], functools.partial(store, 0))
        standardise(
            design, theirs_ref, moreterms_ref, more_ref[kk : kk + 1, :], functools.partial(store, probes)
        )
        for b in range(blocks // 2):
            here = pl.ds(pl.multiple_of((2 * b + core) * share, share), share)
            there = pl.ds(pl.multiple_of(step * (chunk // 2) + b * share, share), share)
            half_ref[there, :] = zscore_ref[here, :]

    @pl.when(step >= steps)
    def _():
        rows = pl.ds(pl.multiple_of((step - steps) * chunk, chunk), chunk)
        put_tile(z_ref[rows, :], half_ref[...], slots_ref, sends_ref, keep_ref)


def own_tile(slots, core, rounds, design, mine, theirs, facts, more):
    _, _, share = design.shape
    rows, probes = mine.shape
    chunk = row_chunk(share)
    steps = rows // chunk

    def first(i, *_):
        return (jnp.minimum(i, steps - 1), 0)

    def second(i, *_):
        return (jnp.maximum(i - steps, 0), 0)

    whole = pl.BlockSpec((K + 8, probes), lambda i, *_: (0, 0))
    return pl.pallas_call(
        functools.partial(own_kernel, steps),
        grid_spec=pltpu.PrefetchScalarGridSpec(
            num_scalar_prefetch=2,
            grid=(2 * steps,),
            in_specs=[
                pl.BlockSpec((chunk // share, K, share), lambda i, *_: (*first(i), 0)),
                pl.BlockSpec((chunk, probes), first),
                pl.BlockSpec((chunk, probes), first),
                whole,
                whole,
            ],
            out_specs=[
                pl.BlockSpec((chunk, 2 * probes), first),
                pl.BlockSpec((rounds, chunk, share), lambda i, *_: (0, *second(i))),
                pl.BlockSpec((chunk, share), second),
            ],
            scratch_shapes=[
                pltpu.VMEM((rows, 2 * probes), BF16),
                pltpu.VMEM((rows // 2, 2 * probes), BF16),
                pltpu.VMEM((3 * K, probes), BF16),
                pltpu.VMEM((3 * K, probes), BF16),
            ],
        ),
        out_shape=(
            jax.ShapeDtypeStruct((rows, 2 * probes), BF16),
            jax.ShapeDtypeStruct((rounds, rows, share), BF16),
            jax.ShapeDtypeStruct((rows, share), F32),
        ),
        compiler_params=params("arbitrary"),
        cost_estimate=cost(2 * rows * rows * probes, 12 * rows * probes),
        name="own",
    )(slots, core, design, mine, theirs, facts, more)


def pair_kernel(
    steps, slots_ref, design_ref, mine_ref, theirs_ref, facts_ref, more_ref, zscore_ref,
    sends_ref, keep_ref, z_ref, terms_ref, moreterms_ref,
):
    step = pl.program_id(0)
    blocks, kk, _ = design_ref.shape
    chunk, probes = mine_ref.shape

    @pl.when(step == 0)
    def _():
        terms_ref[...] = three_terms(facts_ref[:kk, :])
        moreterms_ref[...] = three_terms(more_ref[:kk, :])

    @pl.when(step < steps)
    def _():
        design = jnp.concatenate([design_ref[b] for b in range(blocks)], axis=1)
        rows = pl.ds(pl.multiple_of(step * chunk, chunk), chunk)

        def store(base, at, width, value):
            z_ref[rows, base + at : base + at + width] = value

        standardise(design, mine_ref, terms_ref, facts_ref[kk : kk + 1, :], functools.partial(store, 0))
        standardise(
            design, theirs_ref, moreterms_ref, more_ref[kk : kk + 1, :], functools.partial(store, probes)
        )

    @pl.when(step >= steps)
    def _():
        put_tile(zscore_ref[...], z_ref[...], slots_ref, sends_ref, keep_ref)


def pair_tile(slots, rounds, design, mine, theirs, facts, more, zscore):
    _, _, share = design.shape
    half, probes = mine.shape
    rows = zscore.shape[0]
    chunk = row_chunk(share)
    steps = half // chunk

    def first(i, *_):
        return (jnp.minimum(i, steps - 1), 0)

    def second(i, *_):
        return (jnp.maximum(i - steps, 0), 0)

    whole = pl.BlockSpec((K + 8, probes), lambda i, *_: (0, 0))
    return pl.pallas_call(
        functools.partial(pair_kernel, steps),
        grid_spec=pltpu.PrefetchScalarGridSpec(
            num_scalar_prefetch=1,
            grid=(steps + rows // chunk,),
            in_specs=[
                pl.BlockSpec((chunk // share, K, share), lambda i, *_: (*first(i), 0)),
                pl.BlockSpec((chunk, probes), first),
                pl.BlockSpec((chunk, probes), first),
                whole,
                whole,
                pl.BlockSpec((chunk, 2 * probes), second),
            ],
            out_specs=[
                pl.BlockSpec((rounds, chunk, share), lambda i, *_: (0, *second(i))),
                pl.BlockSpec((chunk, share), second),
            ],
            scratch_shapes=[
                pltpu.VMEM((half, 2 * probes), BF16),
                pltpu.VMEM((3 * K, probes), BF16),
                pltpu.VMEM((3 * K, probes), BF16),
            ],
        ),
        out_shape=(
            jax.ShapeDtypeStruct((rounds, rows, share), BF16),
            jax.ShapeDtypeStruct((rows, share), F32),
        ),
        compiler_params=params("arbitrary"),
        cost_estimate=cost(2 * rows * rows * probes, 8 * rows * probes),
        name="pair",
    )(slots, design, mine, theirs, facts, more, zscore)


def line_rounds(line):
    far = line > 3
    rounds = [[(0, 1), (line - 1, line - 2)] if far else []]
    slots = [[-1] * line for _ in range(line)]
    for j in range(1, line):
        pairs = []
        for i in range(line):
            to = (i + j) % line
            if far and abs(to - i) == line - 1:
                slots[i][to] = 0
            else:
                pairs.append((i, to))
                slots[i][to] = j
        rounds.append(pairs)
    return rounds, slots


def body(methyl, atlas, panel_ids):
    panels, shares = lax.axis_size("samp"), lax.axis_size("probe")
    rows = methyl.shape[0]
    samples = rows * panels
    probes = methyl.shape[1] * shares
    share = rows // shares
    line = shares // 2
    position = lax.axis_index("probe")
    place, core = position // 2, position % 2
    core_only = core[None]

    def to_sibling(value):
        return lax.ppermute(value, "probe", [(i, i ^ 1) for i in range(shares)])

    def to_panel(value, by):
        return lax.ppermute(value, "samp", [(i, (i + by) % panels) for i in range(panels)])

    def to_panel_sibling(value, by):
        pairs = [
            (s * shares + i, ((s + by) % panels) * shares + (i ^ 1))
            for s in range(panels)
            for i in range(shares)
        ]
        return lax.ppermute(value, ("samp", "probe"), pairs)

    def swap_panels(value, bit):
        return lax.ppermute(value, "samp", [(i, i ^ bit) for i in range(panels)])

    theirs = to_sibling(methyl)
    parts, panel, same, other = project(core_only, panel_ids, atlas, methyl, shares)
    before_mine = to_panel(same, 1)
    parts = lax.all_to_all(parts, "probe", 0, 0)
    scores, copies = descend(parts)
    design = lax.all_to_all(copies, "probe", 0, 0)
    part = cross_products(design, methyl, panel)
    bit = panels // 2
    while bit > 1:
        part = part + swap_panels(part, bit)
        bit //= 2
    peer = swap_panels(part, 1)
    half = lax.dynamic_index_in_dim(design.reshape(line, 2, K, share), core, 1, False)
    design_before = to_panel(half, 1)
    before_theirs = to_panel_sibling(other, 1)
    facts = solve(part, peer, panel, 0.0001 * samples, samples)
    more = to_sibling(facts)

    rounds, table = line_rounds(line)
    slots = jnp.take(jnp.array(table, jnp.int32), place, axis=0)

    def reduced(sends, keep):
        def send(value, pairs):
            return lax.ppermute(
                value, "probe", [(2 * i + c, 2 * to + c) for i, to in pairs for c in (0, 1)]
            )

        relay = send(sends[0], rounds[0]) if rounds[0] else None
        total = keep
        for j in [*range(1, 2), *range(line - 1, 1, -1)]:
            value = sends[j]
            if relay is not None and j in (2, line - 2):
                at = (place == line - 2) & (j == 2) | (place == 1) & (j == line - 2)
                value = jnp.where(at, value.astype(F32) + relay.astype(F32), value.astype(F32)).astype(BF16)
            total = total + send(value, rounds[j]).astype(F32)
        return total

    zscore, sends, keep = own_tile(slots, core_only, line, design, methyl, theirs, facts, more)
    own = reduced(sends, keep)
    sends, keep = pair_tile(
        slots, line, design_before, before_mine, before_theirs, facts, more, zscore
    )
    left = reduced(sends, keep)
    blocks = lax.all_to_all(left.astype(BF16).reshape(shares, share, share), "probe", 0, 0)
    blocks = to_panel(blocks, -1)
    after = jnp.swapaxes(blocks.astype(F32), 1, 2).reshape(rows, share)
    return jnp.stack([own, left, after]) / probes, scores


def solution(mesh):
    placed = (P("samp", "probe"), P(None, "probe"), P())
    return jax.shard_map(
        body,
        mesh=mesh,
        in_specs=placed,
        out_specs=(P(None, "samp", "probe"), P(None, ("samp", "probe"))),
        check_vma=False,
    )
```

```python
import functools

import jax
import jax.numpy as jnp
from jax import lax
from jax.experimental import pallas as pl
from jax.experimental.pallas import tpu as pltpu
from jax.sharding import PartitionSpec as P


K = 32
ITERS = 128
F32, BF16 = jnp.float32, jnp.bfloat16
HIGHEST = lax.Precision.HIGHEST
LANES = 128
VMEM_LIMIT = 60 * 1024 * 1024


def nt(a, b):
    return lax.dot_general(a, b, (((1,), (1,)), ((), ())), preferred_element_type=F32)


def tn(a, b):
    return lax.dot_general(a, b, (((0,), (0,)), ((), ())), preferred_element_type=F32)


def params(*semantics):
    return pltpu.CompilerParams(dimension_semantics=semantics, vmem_limit_bytes=VMEM_LIMIT)


def cost(flops, nbytes):
    return pl.CostEstimate(flops=int(flops), bytes_accessed=int(nbytes), transcendentals=0)


def three_terms(value):
    high = value.astype(BF16)
    rest = value - high.astype(F32)
    mid = rest.astype(BF16)
    low = (rest - mid.astype(F32)).astype(BF16)
    return jnp.concatenate([high, mid, low], axis=0)


def project_kernel(core_ref, ids_ref, atlas_ref, methyl_ref, out_ref, panel_ref, other_ref, gram_ref):
    kk = panel_ref.shape[0]
    blocks, _, share = out_ref.shape
    core = core_ref[0]

    @pl.when(pl.program_id(0) == 0)
    def _():
        rows = atlas_ref.shape[0]
        row = lax.broadcasted_iota(jnp.int32, (kk, rows), 0)
        wanted = jnp.zeros((kk, rows), jnp.int32)
        for k in range(kk):
            wanted = jnp.where(row == k, ids_ref[k], wanted)
        pick = wanted == lax.broadcasted_iota(jnp.int32, (kk, rows), 1)
        chosen = jnp.where(pick, 1.0, 0.0).astype(BF16)
        panel = jnp.dot(chosen, atlas_ref[...], preferred_element_type=F32).astype(BF16)
        panel_ref[...] = panel
        gram_ref[...] = nt(panel, panel)

    proj = nt(methyl_ref[...], panel_ref[...]).T
    for b in range(blocks):
        out_ref[b, :kk, :] = proj[:, b * share : (b + 1) * share]
        out_ref[b, kk:, :] = jnp.zeros((kk, share), F32)
        out_ref[b, kk:, :kk] = gram_ref[...]
    for b in range(blocks // 2):
        other = pl.multiple_of((2 * b + 1 - core) * share, share)
        other_ref[b * share : (b + 1) * share, :] = methyl_ref[pl.ds(other, share), :]


def project(core, panel_ids, atlas, methyl, shares):
    rows, probes = methyl.shape
    share = rows // shares
    chunk = row_chunk(share)
    half = pl.BlockSpec((chunk // 2, probes), lambda i: (i, 0))
    return pl.pallas_call(
        project_kernel,
        grid=(rows // chunk,),
        in_specs=[
            pl.BlockSpec(memory_space=pltpu.SMEM),
            pl.BlockSpec(memory_space=pltpu.SMEM),
            pl.BlockSpec(atlas.shape, lambda i: (0, 0)),
            pl.BlockSpec((chunk, probes), lambda i: (i, 0)),
        ],
        out_specs=(
            pl.BlockSpec((chunk // share, 2 * K, share), lambda i: (i, 0, 0)),
            pl.BlockSpec((K, probes), lambda i: (0, 0)),
            half,
        ),
        out_shape=(
            jax.ShapeDtypeStruct((shares, 2 * K, share), F32),
            jax.ShapeDtypeStruct((K, probes), BF16),
            jax.ShapeDtypeStruct((rows // 2, probes), BF16),
        ),
        scratch_shapes=[pltpu.VMEM((K, K), F32)],
        compiler_params=params("arbitrary"),
        cost_estimate=cost(2 * K * rows * probes, 4 * rows * probes),
        name="project",
    )(core, panel_ids, atlas, methyl)


def row_chunk(share):
    return 2 * share * max(1, 128 // share)


def descend_kernel(parts_ref, scores_ref, design_ref, spread_ref, w_ref):
    kk, share = w_ref.shape
    total = parts_ref[0]
    for peer in range(1, parts_ref.shape[0]):
        total = total + parts_ref[peer]
    gram = total[kk:, :kk]
    row = lax.broadcasted_iota(jnp.int32, (kk, kk), 0)
    col = lax.broadcasted_iota(jnp.int32, (kk, kk), 1)
    trace = jnp.sum(jnp.where(row == col, gram, 0.0), axis=(0, 1), keepdims=True)
    rate = 1.0 / trace
    step = jnp.where(row == col, 1.0, 0.0) - rate * gram
    pull = rate * total[:kk, :]
    for k in range(kk):
        spread_ref[k] = jnp.broadcast_to(step[:, k : k + 1], (kk, share))
    w_ref[...] = jnp.full((kk, share), 1.0 / kk, F32)

    def descend(_, carry):
        acc = [pull, None, None, None]
        for k in range(kk):
            term = spread_ref[k] * w_ref[k : k + 1, :]
            acc[k % 4] = term if acc[k % 4] is None else acc[k % 4] + term
        w_ref[...] = jnp.maximum((acc[0] + acc[1]) + (acc[2] + acc[3]), 0.0)
        return carry

    lax.fori_loop(0, ITERS, descend, 0)
    weights = w_ref[...]
    scores_ref[...] = kk * weights
    design = weights.astype(BF16)
    for peer in range(design_ref.shape[0]):
        design_ref[peer] = design


def descend(parts):
    shares, _, share = parts.shape
    return pl.pallas_call(
        descend_kernel,
        out_shape=(
            jax.ShapeDtypeStruct((K, share), F32),
            jax.ShapeDtypeStruct((shares, K, share), BF16),
        ),
        scratch_shapes=[pltpu.VMEM((K, K, share), F32), pltpu.VMEM((K, share), F32)],
        compiler_params=params(),
        cost_estimate=cost(2 * ITERS * K * K * share, 4 * K * share),
        name="descend",
    )(parts)


def cross_kernel(design_ref, methyl_ref, panel_ref, out_ref):
    blocks, kk, _ = design_ref.shape
    probes = methyl_ref.shape[1]
    design = jnp.concatenate([design_ref[b] for b in range(blocks)], axis=1)

    @pl.when(pl.program_id(0) == 0)
    def _():
        out_ref[...] = jnp.zeros_like(out_ref)

    out_ref[:, probes : probes + kk] += nt(design, design)
    width = min(probes, 512)
    for at in range(0, probes, width):
        cols = slice(at, at + width)
        out_ref[:, cols] += jnp.dot(design, methyl_ref[:, cols], preferred_element_type=F32)
        left = methyl_ref[:, cols].astype(F32) - tn(design, panel_ref[:, cols])
        squares = jnp.sum(left * left, axis=0, keepdims=True)
        for b in range(0, width, LANES):
            row = (at + b) // LANES
            out_ref[row : row + 1, probes + LANES :] += squares[:, b : b + LANES]


def cross_products(design, methyl, panel):
    _, _, share = design.shape
    rows, probes = methyl.shape
    chunk = row_chunk(share)
    return pl.pallas_call(
        cross_kernel,
        grid=(rows // chunk,),
        in_specs=[
            pl.BlockSpec((chunk // share, K, share), lambda i: (i, 0, 0)),
            pl.BlockSpec((chunk, probes), lambda i: (i, 0)),
            pl.BlockSpec((K, probes), lambda i: (0, 0)),
        ],
        out_specs=pl.BlockSpec((K, probes + 2 * LANES), lambda i: (0, 0)),
        out_shape=jax.ShapeDtypeStruct((K, probes + 2 * LANES), F32),
        compiler_params=params("arbitrary"),
        cost_estimate=cost(4 * K * rows * probes, 2 * rows * probes),
        name="cross",
    )(design, methyl, panel)


def ridge_inverse(matrix):
    kk = matrix.shape[0]
    row = lax.broadcasted_iota(jnp.int32, (kk, kk), 0)
    col = lax.broadcasted_iota(jnp.int32, (kk, kk), 1)
    work = jnp.concatenate([matrix, jnp.where(row == col, 1.0, 0.0)], axis=1)
    which = lax.broadcasted_iota(jnp.int32, (kk, 1), 0)
    for k in range(kk):
        pivot_row = work[k : k + 1, :] / work[k : k + 1, k : k + 1]
        factor = jnp.where(which == k, 0.0, work[:, k : k + 1])
        work = jnp.where(which == k, pivot_row, work - factor * pivot_row)
    return work[:, kk:]


def solve_kernel(ridge, samples, mine_ref, peer_ref, panel_ref, out_ref):
    kk, probes = panel_ref.shape
    total = mine_ref[...] + peer_ref[...]
    cross = total[:, :probes]
    wgram = total[:, probes : probes + kk]
    start = jnp.concatenate(
        [total[r : r + 1, probes + LANES :] for r in range(probes // LANES)], axis=1
    )
    row = lax.broadcasted_iota(jnp.int32, (kk, kk), 0)
    col = lax.broadcasted_iota(jnp.int32, (kk, kk), 1)
    system = wgram + jnp.where(row == col, ridge, 0.0)
    inverse = ridge_inverse(system)
    loadings = jnp.dot(inverse, cross, precision=HIGHEST)
    short = cross - jnp.dot(system, loadings, precision=HIGHEST)
    loadings = loadings + jnp.dot(inverse, short, precision=HIGHEST)
    panel = panel_ref[...].astype(F32)
    slope = jnp.dot(wgram, loadings + panel, precision=HIGHEST) - 2.0 * cross
    spread = start + jnp.sum((loadings - panel) * slope, axis=0, keepdims=True)
    rate = lax.rsqrt(jnp.maximum(spread, 0.0) / samples + 1e-06)
    out_ref[:kk, :] = loadings
    out_ref[kk:, :] = jnp.broadcast_to(rate, (out_ref.shape[0] - kk, probes))


def solve(mine, peer, panel, ridge, samples):
    probes = panel.shape[1]
    return pl.pallas_call(
        functools.partial(solve_kernel, ridge, samples),
        out_shape=jax.ShapeDtypeStruct((K + 8, probes), F32),
        compiler_params=params(),
        cost_estimate=cost(50 * K * K * probes, 20 * K * probes),
        name="solve",
    )(mine, peer, panel)


def standardise(design, methyl_ref, terms_ref, rate, store):
    probes = methyl_ref.shape[1]
    stacked = jnp.concatenate([design] * 3, axis=0)
    width = min(probes, 512)
    for at in range(0, probes, width):
        cols = slice(at, at + width)
        fitted = tn(stacked, terms_ref[:, cols])
        left = methyl_ref[:, cols].astype(F32) - fitted
        store(at, width, (left * rate[:, cols]).astype(BF16))


def put_tile(part, unused, sends, keep_ref):
    share = keep_ref.shape[1]
    keep = None
    for j, ref in enumerate(sends):
        block = part[:, j * share : (j + 1) * share]
        ref[...] = block.astype(BF16)
        mine = jnp.where(unused == j, block, 0.0)
        keep = mine if keep is None else keep + mine
    keep_ref[...] = keep


def own_kernel(
    steps, line, slots_ref, at_ref, design_ref, mine_ref, theirs_ref, facts_ref, more_ref, *refs
):
    (zscore_ref, *sends), (keep_ref, z_ref, half_ref, terms_ref, moreterms_ref) = (
        refs[: line + 1],
        refs[line + 1 :],
    )
    step = pl.program_id(0)
    blocks, kk, share = design_ref.shape
    chunk, probes = mine_ref.shape
    place, core = at_ref[0], at_ref[1]

    @pl.when(step == 0)
    def _():
        terms_ref[...] = three_terms(facts_ref[:kk, :])
        moreterms_ref[...] = three_terms(more_ref[:kk, :])

    @pl.when(step < steps)
    def _():
        design = jnp.concatenate([design_ref[b] for b in range(blocks)], axis=1)
        rows = pl.ds(pl.multiple_of(step * chunk, chunk), chunk)

        def store(base, at, width, value):
            zscore_ref[:, base + at : base + at + width] = value
            z_ref[rows, base + at : base + at + width] = value

        standardise(design, mine_ref, terms_ref, facts_ref[kk : kk + 1, :], functools.partial(store, 0))
        standardise(
            design, theirs_ref, moreterms_ref, more_ref[kk : kk + 1, :], functools.partial(store, probes)
        )
        for b in range(blocks // 2):
            here = pl.ds(pl.multiple_of((2 * b + core) * share, share), share)
            slot = slots_ref[step * (blocks // 2) + b]
            half_ref[pl.ds(pl.multiple_of(slot * share, share), share), :] = zscore_ref[here, :]

    @pl.when(step >= steps)
    def _():
        rows = pl.ds(pl.multiple_of((step - steps) * chunk, chunk), chunk)
        put_tile(nt(z_ref[rows, :], half_ref[...]), slots_ref[place], sends, keep_ref)


def own_tile(slots, at, line, design, mine, theirs, facts, more):
    _, _, share = design.shape
    rows, probes = mine.shape
    chunk = row_chunk(share)
    steps = rows // chunk

    def first(i, *_):
        return (jnp.minimum(i, steps - 1), 0)

    def second(i, *_):
        return (jnp.maximum(i - steps, 0), 0)

    whole = pl.BlockSpec((K + 8, probes), lambda i, *_: (0, 0))
    return pl.pallas_call(
        functools.partial(own_kernel, steps, line),
        grid_spec=pltpu.PrefetchScalarGridSpec(
            num_scalar_prefetch=2,
            grid=(2 * steps,),
            in_specs=[
                pl.BlockSpec((chunk // share, K, share), lambda i, *_: (*first(i), 0)),
                pl.BlockSpec((chunk, probes), first),
                pl.BlockSpec((chunk, probes), first),
                whole,
                whole,
            ],
            out_specs=[pl.BlockSpec((chunk, 2 * probes), first)]
            + [pl.BlockSpec((chunk, share), second)] * (line + 1),
            scratch_shapes=[
                pltpu.VMEM((rows, 2 * probes), BF16),
                pltpu.VMEM((rows // 2, 2 * probes), BF16),
                pltpu.VMEM((3 * K, probes), BF16),
                pltpu.VMEM((3 * K, probes), BF16),
            ],
        ),
        out_shape=[jax.ShapeDtypeStruct((rows, 2 * probes), BF16)]
        + [jax.ShapeDtypeStruct((rows, share), BF16)] * line
        + [jax.ShapeDtypeStruct((rows, share), F32)],
        compiler_params=params("arbitrary"),
        cost_estimate=cost(2 * rows * rows * probes, 12 * rows * probes),
        name="own",
    )(slots, at, design, mine, theirs, facts, more)


def pair_kernel(steps, last, slots_ref, at_ref, design_ref, raw_ref, facts_ref, zscore_ref, *refs):
    refs, (z_ref, terms_ref) = refs[:-2], refs[-2:]
    step = pl.program_id(0)
    blocks, kk, share = design_ref.shape

    @pl.when(step == 0)
    def _():
        terms_ref[...] = three_terms(facts_ref[:kk, :])

    @pl.when(step < steps)
    def _():
        design = jnp.concatenate([design_ref[b] for b in range(blocks)], axis=1)

        def store(at, width, value):
            for b in range(blocks):
                slot = slots_ref[step * blocks + b]
                rows = pl.ds(pl.multiple_of(slot * share, share), share)
                z_ref[rows, at : at + width] = value[b * share : (b + 1) * share, :]

        standardise(design, raw_ref, terms_ref, facts_ref[kk : kk + 1, :], store)

    @pl.when(step >= steps)
    def _():
        part = nt(zscore_ref[...], z_ref[...])
        if last:
            put_tile(part + refs[0][...], slots_ref[at_ref[0]], refs[1:-1], refs[-1])
        else:
            refs[0][...] = part


def pair_tile(slots, at, line, design, raw, facts, zscore, which, partial):
    _, _, share = design.shape
    half, probes = raw.shape
    rows = zscore.shape[0]
    chunk = row_chunk(share)
    steps = half // chunk
    last = partial is not None

    def first(i, *_):
        return (jnp.minimum(i, steps - 1), 0)

    def second(i, *_):
        return (jnp.maximum(i - steps, 0), 0)

    total = pl.BlockSpec((chunk, half), second)
    if last:
        out_specs = [pl.BlockSpec((chunk, share), second)] * (line + 1)
        out_shape = [jax.ShapeDtypeStruct((rows, share), BF16)] * line
        out_shape += [jax.ShapeDtypeStruct((rows, share), F32)]
    else:
        out_specs = total
        out_shape = jax.ShapeDtypeStruct((rows, half), F32)
    return pl.pallas_call(
        functools.partial(pair_kernel, steps, last),
        grid_spec=pltpu.PrefetchScalarGridSpec(
            num_scalar_prefetch=2,
            grid=(steps + rows // chunk,),
            in_specs=[
                pl.BlockSpec((chunk // share, K, share), lambda i, *_: (*first(i), 0)),
                pl.BlockSpec((chunk, probes), first),
                pl.BlockSpec((K + 8, probes), lambda i, *_: (0, 0)),
                pl.BlockSpec((chunk, probes), lambda i, *_: (second(i)[0], which)),
            ]
            + [total] * last,
            out_specs=out_specs,
            scratch_shapes=[pltpu.VMEM((half, probes), BF16), pltpu.VMEM((3 * K, probes), BF16)],
        ),
        out_shape=out_shape,
        compiler_params=params("arbitrary"),
        cost_estimate=cost(rows * rows * probes, 8 * rows * probes),
        name="pair_last" if last else "pair_first",
    )(slots, at, design, raw, facts, zscore, *([partial] * last))


def fold_kernel(line, at_ref, keep_ref, *refs):
    parts, (total_ref, same_ref, other_ref) = refs[:-3], refs[-3:]
    place, core = at_ref[0], at_ref[1]
    share = same_ref.shape[1]
    total = keep_ref[...]
    for ref in parts:
        total = total + ref[...].astype(F32)
    total_ref[...] = total
    for j in range(line):
        block = 2 * lax.rem(place + j, line)
        same = pl.ds(pl.multiple_of((block + core) * share, share), share)
        other = pl.ds(pl.multiple_of((block + 1 - core) * share, share), share)
        same_ref[j] = total_ref[same, :].astype(BF16)
        other_ref[j] = total_ref[other, :].astype(BF16)


def fold(at, line, keep, parts):
    rows, share = keep.shape
    blocks = jax.ShapeDtypeStruct((line, share, share), BF16)
    vmem = pl.BlockSpec(memory_space=pltpu.VMEM)
    return pl.pallas_call(
        functools.partial(fold_kernel, line),
        in_specs=[pl.BlockSpec(memory_space=pltpu.SMEM)] + [vmem] * (1 + len(parts)),
        out_shape=(jax.ShapeDtypeStruct((rows, share), F32), blocks, blocks),
        compiler_params=params(),
        cost_estimate=cost(rows * share * 8, rows * share * 16),
        name="fold",
    )(at, keep, *parts)


def finish_kernel(line, probes, count, at_ref, keep_ref, *refs):
    parts, left_ref, same_ref, other_ref, shifted, out_ref = (
        refs[:count],
        *refs[count : count + 3],
        refs[count + 3 : -1],
        refs[-1],
    )
    place, core = at_ref[0], at_ref[1]
    share = keep_ref.shape[1]
    total = keep_ref[...]
    for ref in parts:
        total = total + ref[...].astype(F32)
    out_ref[0] = total * (1.0 / probes)
    out_ref[1] = left_ref[...] * (1.0 / probes)
    for j in range(line):
        block = 2 * lax.rem(place - j + line, line)
        for side in range(2):
            if j == 0:
                piece = (same_ref, other_ref)[side][0]
            else:
                piece = shifted[j - 1][side]
            to = block + (core if side == 0 else 1 - core)
            rows = pl.ds(pl.multiple_of(to * share, share), share)
            out_ref[2, rows, :] = piece.astype(F32).T * (1.0 / probes)


def finish(at, line, probes, keep, parts, left, same, other, shifted):
    rows, share = keep.shape
    vmem = pl.BlockSpec(memory_space=pltpu.VMEM)
    return pl.pallas_call(
        functools.partial(finish_kernel, line, probes, len(parts)),
        in_specs=[pl.BlockSpec(memory_space=pltpu.SMEM)] + [vmem] * (4 + len(parts) + len(shifted)),
        out_shape=jax.ShapeDtypeStruct((3, rows, share), F32),
        compiler_params=params(),
        cost_estimate=cost(rows * share * 16, rows * share * 30),
        name="finish",
    )(at, keep, *parts, left, same, other, *shifted)


def line_rounds(line):
    far = line > 3
    rounds, onward = [[]], []
    slots = [[None] * line for _ in range(line)]
    for j in range(1, line):
        pairs = []
        for i in range(line):
            to = (i + j) % line
            if far and abs(to - i) == line - 1:
                rounds[0].append((i, 1 if i == 0 else line - 2))
                slots[i][to] = 0
            elif far and (i, to) in ((1, line - 1), (line - 2, 0)):
                onward.append((i, to))
                slots[i][to] = 0
            else:
                pairs.append((i, to))
                slots[i][to] = j
        rounds.append(pairs)
    for i in range(line):
        slots[i][i] = next(j for j in range(line) if j not in slots[i])
    return rounds, onward, slots


def body(methyl, atlas, panel_ids):
    panels, shares = lax.axis_size("samp"), lax.axis_size("probe")
    rows = methyl.shape[0]
    samples = rows * panels
    probes = methyl.shape[1] * shares
    share = rows // shares
    line = shares // 2
    position = lax.axis_index("probe")
    place, core = position // 2, position % 2
    at = jnp.stack([place, core]).astype(jnp.int32)

    def along(value, axis, pairs):
        return lax.ppermute(value, axis, pairs)

    def to_sibling(value):
        return along(value, "probe", [(i, i ^ 1) for i in range(shares)])

    def to_panel(value, by):
        return along(value, "samp", [(i, (i + by) % panels) for i in range(panels)])

    def to_panel_sibling(value, by):
        pairs = [
            (s * shares + i, ((s + by) % panels) * shares + (i ^ 1))
            for s in range(panels)
            for i in range(shares)
        ]
        return along(value, ("samp", "probe"), pairs)

    def swap_panels(value, bit):
        return along(value, "samp", [(i, i ^ bit) for i in range(panels)])

    def on_line(value, pairs):
        return along(value, "probe", [(2 * i + c, 2 * to + c) for i, to in pairs for c in (0, 1)])

    same = lax.dynamic_index_in_dim(methyl.reshape(line, 2, share, -1), core, 1, False)
    before_mine = to_panel(same.reshape(line * share, -1), 1)
    theirs = to_sibling(methyl)
    parts, panel, other = project(core[None], panel_ids, atlas, methyl, shares)
    parts = lax.all_to_all(parts, "probe", 0, 0)
    scores, copies = descend(parts)
    design = lax.all_to_all(copies, "probe", 0, 0)
    part = cross_products(design, methyl, panel)
    bit = panels // 2
    while bit > 1:
        part = part + swap_panels(part, bit)
        bit //= 2
    peer = swap_panels(part, 1)
    half = lax.dynamic_index_in_dim(design.reshape(line, 2, K, share), core, 1, False)
    design_before = to_panel(half, 1)
    before_theirs = to_panel_sibling(other, 1)
    facts = solve(part, peer, panel, 0.0001 * samples, samples)
    more = to_sibling(facts)

    rounds, onward, table = line_rounds(line)
    slots = jnp.take(jnp.array(table, jnp.int32), place, axis=0)

    def arrivals(sends):
        parts, relay = [], None
        if onward:
            relay = on_line(sends[0], rounds[0])
        for j in range(1, line):
            parts.append(on_line(sends[j], rounds[j]))
        if onward:
            joined = (sends[0].astype(F32) + relay.astype(F32)).astype(BF16)
            parts.append(on_line(joined, onward))
        return parts

    zscore, *sends, own_keep = own_tile(slots, at, line, design, methyl, theirs, facts, more)
    own_parts = arrivals(sends)
    partial = pair_tile(slots, at, line, design_before, before_mine, facts, zscore, 0, None)
    *sends, keep = pair_tile(slots, at, line, design_before, before_theirs, more, zscore, 1, partial)
    left, same, other = fold(at, line, keep, arrivals(sends))
    same, other = to_panel(same, -1), to_panel_sibling(other, -1)
    shifted = [
        on_line(jnp.stack([same[j], other[j]]), rounds_of_shift(line, j)) for j in range(1, line)
    ]
    total = finish(at, line, probes, own_keep, own_parts, left, same, other, shifted)
    return total, scores


def rounds_of_shift(line, by):
    return [(i, (i + by) % line) for i in range(line)]


def solution(mesh):
    placed = (P("samp", "probe"), P(None, "probe"), P())
    return jax.shard_map(
        body,
        mesh=mesh,
        in_specs=placed,
        out_specs=(P(None, "samp", "probe"), P(None, ("samp", "probe"))),
        check_vma=False,
    )
```

```python
import functools

import jax
import jax.numpy as jnp
from jax import lax
from jax.experimental import pallas as pl
from jax.experimental.pallas import tpu as pltpu
from jax.sharding import PartitionSpec as P


K = 32
ITERS = 128
F32, BF16 = jnp.float32, jnp.bfloat16
HIGHEST = lax.Precision.HIGHEST
LANES = 128
VMEM_LIMIT = 60 * 1024 * 1024


def nt(a, b):
    return lax.dot_general(a, b, (((1,), (1,)), ((), ())), preferred_element_type=F32)


def tn(a, b):
    return lax.dot_general(a, b, (((0,), (0,)), ((), ())), preferred_element_type=F32)


def params(*semantics):
    return pltpu.CompilerParams(dimension_semantics=semantics, vmem_limit_bytes=VMEM_LIMIT)


def cost(flops, nbytes):
    return pl.CostEstimate(flops=int(flops), bytes_accessed=int(nbytes), transcendentals=0)


def three_terms(value):
    high = value.astype(BF16)
    rest = value - high.astype(F32)
    mid = rest.astype(BF16)
    low = (rest - mid.astype(F32)).astype(BF16)
    return jnp.concatenate([high, mid, low], axis=0)


def project_kernel(core_ref, ids_ref, atlas_ref, methyl_ref, out_ref, panel_ref, other_ref, gram_ref):
    kk = panel_ref.shape[0]
    blocks, _, share = out_ref.shape
    core = core_ref[0]

    @pl.when(pl.program_id(0) == 0)
    def _():
        rows = atlas_ref.shape[0]
        row = lax.broadcasted_iota(jnp.int32, (kk, rows), 0)
        wanted = jnp.zeros((kk, rows), jnp.int32)
        for k in range(kk):
            wanted = jnp.where(row == k, ids_ref[k], wanted)
        pick = wanted == lax.broadcasted_iota(jnp.int32, (kk, rows), 1)
        chosen = jnp.where(pick, 1.0, 0.0).astype(BF16)
        panel = jnp.dot(chosen, atlas_ref[...], preferred_element_type=F32).astype(BF16)
        panel_ref[...] = panel
        gram_ref[...] = nt(panel, panel)

    proj = nt(methyl_ref[...], panel_ref[...]).T
    for b in range(blocks):
        out_ref[b, :kk, :] = proj[:, b * share : (b + 1) * share]
        out_ref[b, kk:, :] = jnp.zeros((kk, share), F32)
        out_ref[b, kk:, :kk] = gram_ref[...]
    for b in range(blocks // 2):
        other = pl.multiple_of((2 * b + 1 - core) * share, share)
        other_ref[b * share : (b + 1) * share, :] = methyl_ref[pl.ds(other, share), :]


def project(core, panel_ids, atlas, methyl, shares):
    rows, probes = methyl.shape
    share = rows // shares
    chunk = row_chunk(share)
    half = pl.BlockSpec((chunk // 2, probes), lambda i: (i, 0))
    return pl.pallas_call(
        project_kernel,
        grid=(rows // chunk,),
        in_specs=[
            pl.BlockSpec(memory_space=pltpu.SMEM),
            pl.BlockSpec(memory_space=pltpu.SMEM),
            pl.BlockSpec(atlas.shape, lambda i: (0, 0)),
            pl.BlockSpec((chunk, probes), lambda i: (i, 0)),
        ],
        out_specs=(
            pl.BlockSpec((chunk // share, 2 * K, share), lambda i: (i, 0, 0)),
            pl.BlockSpec((K, probes), lambda i: (0, 0)),
            half,
        ),
        out_shape=(
            jax.ShapeDtypeStruct((shares, 2 * K, share), F32),
            jax.ShapeDtypeStruct((K, probes), BF16),
            jax.ShapeDtypeStruct((rows // 2, probes), BF16),
        ),
        scratch_shapes=[pltpu.VMEM((K, K), F32)],
        compiler_params=params("arbitrary"),
        cost_estimate=cost(2 * K * rows * probes, 4 * rows * probes),
        name="project",
    )(core, panel_ids, atlas, methyl)


def row_chunk(share):
    return 2 * share * max(1, 128 // share)


def descend_kernel(parts_ref, scores_ref, design_ref, spread_ref, w_ref):
    kk, share = w_ref.shape
    total = parts_ref[0]
    for peer in range(1, parts_ref.shape[0]):
        total = total + parts_ref[peer]
    gram = total[kk:, :kk]
    row = lax.broadcasted_iota(jnp.int32, (kk, kk), 0)
    col = lax.broadcasted_iota(jnp.int32, (kk, kk), 1)
    trace = jnp.sum(jnp.where(row == col, gram, 0.0), axis=(0, 1), keepdims=True)
    rate = 1.0 / trace
    step = jnp.where(row == col, 1.0, 0.0) - rate * gram
    pull = rate * total[:kk, :]
    for k in range(kk):
        spread_ref[k] = jnp.broadcast_to(step[:, k : k + 1], (kk, share))
    w_ref[...] = jnp.full((kk, share), 1.0 / kk, F32)

    def descend(_, carry):
        acc = [pull, None, None, None]
        for k in range(kk):
            term = spread_ref[k] * w_ref[k : k + 1, :]
            acc[k % 4] = term if acc[k % 4] is None else acc[k % 4] + term
        w_ref[...] = jnp.maximum((acc[0] + acc[1]) + (acc[2] + acc[3]), 0.0)
        return carry

    lax.fori_loop(0, ITERS, descend, 0)
    weights = w_ref[...]
    scores_ref[...] = kk * weights
    design = weights.astype(BF16)
    for peer in range(design_ref.shape[0]):
        design_ref[peer] = design


def descend(parts):
    shares, _, share = parts.shape
    return pl.pallas_call(
        descend_kernel,
        out_shape=(
            jax.ShapeDtypeStruct((K, share), F32),
            jax.ShapeDtypeStruct((shares, K, share), BF16),
        ),
        scratch_shapes=[pltpu.VMEM((K, K, share), F32), pltpu.VMEM((K, share), F32)],
        compiler_params=params(),
        cost_estimate=cost(2 * ITERS * K * K * share, 4 * K * share),
        name="descend",
    )(parts)


def cross_kernel(design_ref, methyl_ref, panel_ref, out_ref):
    blocks, kk, _ = design_ref.shape
    probes = methyl_ref.shape[1]
    design = jnp.concatenate([design_ref[b] for b in range(blocks)], axis=1)

    @pl.when(pl.program_id(0) == 0)
    def _():
        out_ref[...] = jnp.zeros_like(out_ref)

    out_ref[:, probes : probes + kk] += nt(design, design)
    width = min(probes, 512)
    for at in range(0, probes, width):
        cols = slice(at, at + width)
        out_ref[:, cols] += jnp.dot(design, methyl_ref[:, cols], preferred_element_type=F32)
        left = methyl_ref[:, cols].astype(F32) - tn(design, panel_ref[:, cols])
        squares = jnp.sum(left * left, axis=0, keepdims=True)
        for b in range(0, width, LANES):
            row = (at + b) // LANES
            out_ref[row : row + 1, probes + LANES :] += squares[:, b : b + LANES]


def cross_products(design, methyl, panel):
    _, _, share = design.shape
    rows, probes = methyl.shape
    chunk = row_chunk(share)
    return pl.pallas_call(
        cross_kernel,
        grid=(rows // chunk,),
        in_specs=[
            pl.BlockSpec((chunk // share, K, share), lambda i: (i, 0, 0)),
            pl.BlockSpec((chunk, probes), lambda i: (i, 0)),
            pl.BlockSpec((K, probes), lambda i: (0, 0)),
        ],
        out_specs=pl.BlockSpec((K, probes + 2 * LANES), lambda i: (0, 0)),
        out_shape=jax.ShapeDtypeStruct((K, probes + 2 * LANES), F32),
        compiler_params=params("arbitrary"),
        cost_estimate=cost(4 * K * rows * probes, 2 * rows * probes),
        name="cross",
    )(design, methyl, panel)


def ridge_inverse(matrix):
    kk = matrix.shape[0]
    row = lax.broadcasted_iota(jnp.int32, (kk, kk), 0)
    col = lax.broadcasted_iota(jnp.int32, (kk, kk), 1)
    work = jnp.concatenate([matrix, jnp.where(row == col, 1.0, 0.0)], axis=1)
    which = lax.broadcasted_iota(jnp.int32, (kk, 1), 0)
    for k in range(kk):
        pivot_row = work[k : k + 1, :] / work[k : k + 1, k : k + 1]
        factor = jnp.where(which == k, 0.0, work[:, k : k + 1])
        work = jnp.where(which == k, pivot_row, work - factor * pivot_row)
    return work[:, kk:]


def solve_kernel(ridge, samples, mine_ref, peer_ref, panel_ref, out_ref):
    kk, probes = panel_ref.shape
    total = mine_ref[...] + peer_ref[...]
    cross = total[:, :probes]
    wgram = total[:, probes : probes + kk]
    start = jnp.concatenate(
        [total[r : r + 1, probes + LANES :] for r in range(probes // LANES)], axis=1
    )
    row = lax.broadcasted_iota(jnp.int32, (kk, kk), 0)
    col = lax.broadcasted_iota(jnp.int32, (kk, kk), 1)
    system = wgram + jnp.where(row == col, ridge, 0.0)
    inverse = ridge_inverse(system)
    loadings = jnp.dot(inverse, cross, precision=HIGHEST)
    short = cross - jnp.dot(system, loadings, precision=HIGHEST)
    loadings = loadings + jnp.dot(inverse, short, precision=HIGHEST)
    panel = panel_ref[...].astype(F32)
    slope = jnp.dot(wgram, loadings + panel, precision=HIGHEST) - 2.0 * cross
    spread = start + jnp.sum((loadings - panel) * slope, axis=0, keepdims=True)
    rate = lax.rsqrt(jnp.maximum(spread, 0.0) / samples + 1e-06)
    out_ref[:kk, :] = loadings
    out_ref[kk:, :] = jnp.broadcast_to(rate, (out_ref.shape[0] - kk, probes))


def solve(mine, peer, panel, ridge, samples):
    probes = panel.shape[1]
    return pl.pallas_call(
        functools.partial(solve_kernel, ridge, samples),
        out_shape=jax.ShapeDtypeStruct((K + 8, probes), F32),
        compiler_params=params(),
        cost_estimate=cost(50 * K * K * probes, 20 * K * probes),
        name="solve",
    )(mine, peer, panel)


def standardise(design, methyl_ref, terms_ref, rate, store):
    probes = methyl_ref.shape[1]
    stacked = jnp.concatenate([design] * 3, axis=0)
    width = min(probes, 512)
    for at in range(0, probes, width):
        cols = slice(at, at + width)
        fitted = tn(stacked, terms_ref[:, cols])
        left = methyl_ref[:, cols].astype(F32) - fitted
        store(at, width, (left * rate[:, cols]).astype(BF16))


def put_tile(part, sends, keep_ref):
    share = keep_ref.shape[1]
    keep_ref[...] = part[:, :share]
    for j, ref in enumerate(sends, 1):
        ref[...] = part[:, j * share : (j + 1) * share].astype(BF16)


def own_kernel(
    steps, line, place_ref, core_ref, design_ref, mine_ref, theirs_ref, facts_ref, more_ref, *refs
):
    (zscore_ref, *sends), (keep_ref, z_ref, half_ref, terms_ref, moreterms_ref) = (
        refs[:line],
        refs[line:],
    )
    step = pl.program_id(0)
    blocks, kk, share = design_ref.shape
    chunk, probes = mine_ref.shape
    place, core = place_ref[0], core_ref[0]

    @pl.when(step == 0)
    def _():
        terms_ref[...] = three_terms(facts_ref[:kk, :])
        moreterms_ref[...] = three_terms(more_ref[:kk, :])

    @pl.when(step < steps)
    def _():
        design = jnp.concatenate([design_ref[b] for b in range(blocks)], axis=1)
        rows = pl.ds(pl.multiple_of(step * chunk, chunk), chunk)

        def store(base, at, width, value):
            zscore_ref[:, base + at : base + at + width] = value
            z_ref[rows, base + at : base + at + width] = value

        standardise(design, mine_ref, terms_ref, facts_ref[kk : kk + 1, :], functools.partial(store, 0))
        standardise(
            design, theirs_ref, moreterms_ref, more_ref[kk : kk + 1, :], functools.partial(store, probes)
        )
        for b in range(blocks // 2):
            here = pl.ds(pl.multiple_of((2 * b + core) * share, share), share)
            slot = lax.rem(step * (blocks // 2) + b - place + line, line)
            half_ref[pl.ds(pl.multiple_of(slot * share, share), share), :] = zscore_ref[here, :]

    @pl.when(step >= steps)
    def _():
        tall = keep_ref.shape[0]
        rows = pl.ds(pl.multiple_of((step - steps) * tall, tall), tall)
        put_tile(nt(z_ref[rows, :], half_ref[...]), sends, keep_ref)


def own_tile(at, line, design, mine, theirs, facts, more):
    _, _, share = design.shape
    rows, probes = mine.shape
    chunk = row_chunk(share)
    steps, tall = rows // chunk, 2 * chunk

    def first(i, *_):
        return (jnp.minimum(i, steps - 1), 0)

    def second(i, *_):
        return (jnp.maximum(i - steps, 0), 0)

    whole = pl.BlockSpec((K + 8, probes), lambda i, *_: (0, 0))
    return pl.pallas_call(
        functools.partial(own_kernel, steps, line),
        grid_spec=pltpu.PrefetchScalarGridSpec(
            num_scalar_prefetch=2,
            grid=(steps + rows // tall,),
            in_specs=[
                pl.BlockSpec((chunk // share, K, share), lambda i, *_: (*first(i), 0)),
                pl.BlockSpec((chunk, probes), first),
                pl.BlockSpec((chunk, probes), first),
                whole,
                whole,
            ],
            out_specs=[pl.BlockSpec((chunk, 2 * probes), first)]
            + [pl.BlockSpec((tall, share), second)] * line,
            scratch_shapes=[
                pltpu.VMEM((rows, 2 * probes), BF16),
                pltpu.VMEM((rows // 2, 2 * probes), BF16),
                pltpu.VMEM((3 * K, probes), BF16),
                pltpu.VMEM((3 * K, probes), BF16),
            ],
        ),
        out_shape=[jax.ShapeDtypeStruct((rows, 2 * probes), BF16)]
        + [jax.ShapeDtypeStruct((rows, share), BF16)] * (line - 1)
        + [jax.ShapeDtypeStruct((rows, share), F32)],
        compiler_params=params("arbitrary"),
        cost_estimate=cost(2 * rows * rows * probes, 12 * rows * probes),
        name="own",
    )(*at, design, mine, theirs, facts, more)


def pair_kernel(steps, line, last, place_ref, design_ref, raw_ref, facts_ref, zscore_ref, *refs):
    refs, (z_ref, terms_ref) = refs[:-2], refs[-2:]
    step = pl.program_id(0)
    blocks, kk, share = design_ref.shape

    @pl.when(step == 0)
    def _():
        terms_ref[...] = three_terms(facts_ref[:kk, :])

    @pl.when(step < steps)
    def _():
        design = jnp.concatenate([design_ref[b] for b in range(blocks)], axis=1)

        def store(at, width, value):
            for b in range(blocks):
                slot = lax.rem(step * blocks + b - place_ref[0] + line, line)
                rows = pl.ds(pl.multiple_of(slot * share, share), share)
                z_ref[rows, at : at + width] = value[b * share : (b + 1) * share, :]

        standardise(design, raw_ref, terms_ref, facts_ref[kk : kk + 1, :], store)

    @pl.when(step >= steps)
    def _():
        part = nt(zscore_ref[...], z_ref[...])
        if last:
            put_tile(part + refs[0][...], refs[1:-1], refs[-1])
        else:
            refs[0][...] = part


def pair_tile(at, line, design, raw, facts, zscore, which, partial):
    _, _, share = design.shape
    half, probes = raw.shape
    rows = zscore.shape[0]
    chunk = row_chunk(share)
    steps, tall = half // chunk, 2 * chunk
    last = partial is not None

    def first(i, *_):
        return (jnp.minimum(i, steps - 1), 0)

    def second(i, *_):
        return (jnp.maximum(i - steps, 0), 0)

    total = pl.BlockSpec((tall, half), second)
    if last:
        out_specs = [pl.BlockSpec((tall, share), second)] * line
        out_shape = [jax.ShapeDtypeStruct((rows, share), BF16)] * (line - 1)
        out_shape += [jax.ShapeDtypeStruct((rows, share), F32)]
    else:
        out_specs = total
        out_shape = jax.ShapeDtypeStruct((rows, half), F32)
    return pl.pallas_call(
        functools.partial(pair_kernel, steps, line, last),
        grid_spec=pltpu.PrefetchScalarGridSpec(
            num_scalar_prefetch=1,
            grid=(steps + rows // tall,),
            in_specs=[
                pl.BlockSpec((chunk // share, K, share), lambda i, *_: (*first(i), 0)),
                pl.BlockSpec((chunk, probes), first),
                pl.BlockSpec((K + 8, probes), lambda i, *_: (0, 0)),
                pl.BlockSpec((tall, probes), lambda i, *_: (second(i)[0], which)),
            ]
            + [total] * last,
            out_specs=out_specs,
            scratch_shapes=[pltpu.VMEM((half, probes), BF16), pltpu.VMEM((3 * K, probes), BF16)],
        ),
        out_shape=out_shape,
        compiler_params=params("arbitrary"),
        cost_estimate=cost(rows * rows * probes, 8 * rows * probes),
        name="pair_last" if last else "pair_first",
    )(at[0], design, raw, facts, zscore, *([partial] * last))


def fold_kernel(line, place_ref, core_ref, keep_ref, *refs):
    parts, (total_ref, same_ref, other_ref) = refs[:-3], refs[-3:]
    place, core = place_ref[0], core_ref[0]
    share = same_ref.shape[1]
    total = keep_ref[...]
    for ref in parts:
        total = total + ref[...].astype(F32)
    total_ref[...] = total
    for j in range(line):
        block = 2 * lax.rem(place + j, line)
        same = pl.ds(pl.multiple_of((block + core) * share, share), share)
        other = pl.ds(pl.multiple_of((block + 1 - core) * share, share), share)
        same_ref[j] = total_ref[same, :].astype(BF16)
        other_ref[j] = total_ref[other, :].astype(BF16)


def fold(at, line, keep, parts):
    rows, share = keep.shape
    blocks = jax.ShapeDtypeStruct((line, share, share), BF16)
    vmem = pl.BlockSpec(memory_space=pltpu.VMEM)
    return pl.pallas_call(
        functools.partial(fold_kernel, line),
        in_specs=[pl.BlockSpec(memory_space=pltpu.SMEM)] * 2 + [vmem] * (1 + len(parts)),
        out_shape=(jax.ShapeDtypeStruct((rows, share), F32), blocks, blocks),
        compiler_params=params(),
        cost_estimate=cost(rows * share * 8, rows * share * 16),
        name="fold",
    )(*at, keep, *parts)


def scale_kernel(probes, own_ref, *refs):
    parts, (left_ref, out_ref) = refs[:-2], refs[-2:]
    total = own_ref[...]
    for ref in parts:
        total = total + ref[...].astype(F32)
    out_ref[0] = total * (1.0 / probes)
    out_ref[1] = left_ref[...] * (1.0 / probes)


def scale(probes, keep, parts, left):
    rows, share = keep.shape
    vmem = pl.BlockSpec((rows, share), lambda i: (0, 0))
    return pl.pallas_call(
        functools.partial(scale_kernel, probes),
        grid=(1,),
        in_specs=[vmem] * (2 + len(parts)),
        out_specs=pl.BlockSpec((2, rows, share), lambda i: (0, 0, 0)),
        out_shape=jax.ShapeDtypeStruct((3, rows, share), F32),
        compiler_params=params("arbitrary"),
        cost_estimate=cost(rows * share * 16, rows * share * 30),
        name="scale",
    )(keep, *parts, left)


def finish_kernel(line, probes, place_ref, core_ref, _, same_ref, other_ref, *refs):
    shifted, out_ref = refs[:-1], refs[-1]
    place, core = place_ref[0], core_ref[0]
    share = same_ref.shape[1]
    for j in range(line):
        block = 2 * lax.rem(place - j + line, line)
        for side in range(2):
            piece = (same_ref, other_ref)[side][0] if j == 0 else shifted[j - 1][side]
            to = block + (core if side == 0 else 1 - core)
            rows = pl.ds(pl.multiple_of(to * share, share), share)
            out_ref[0, rows, :] = piece.astype(F32).T * (1.0 / probes)


def finish(at, line, probes, tiles, same, other, shifted):
    _, rows, share = tiles.shape
    first = pl.BlockSpec((1, share, share), lambda i: (0, 0, 0))
    pair = pl.BlockSpec((2, share, share), lambda i: (0, 0, 0))
    return pl.pallas_call(
        functools.partial(finish_kernel, line, probes),
        grid=(1,),
        in_specs=[pl.BlockSpec(memory_space=pltpu.SMEM)] * 2
        + [pl.BlockSpec(memory_space=pl.ANY), first, first]
        + [pair] * len(shifted),
        out_specs=pl.BlockSpec((1, rows, share), lambda i: (2, 0, 0)),
        out_shape=jax.ShapeDtypeStruct(tiles.shape, F32),
        input_output_aliases={2: 0},
        compiler_params=params("arbitrary"),
        cost_estimate=cost(rows * share * 4, rows * share * 8),
        name="finish",
    )(*at, tiles, same, other, *shifted)


def body(methyl, atlas, panel_ids):
    panels, shares = lax.axis_size("samp"), lax.axis_size("probe")
    rows = methyl.shape[0]
    samples = rows * panels
    probes = methyl.shape[1] * shares
    share = rows // shares
    line = shares // 2
    position = lax.axis_index("probe")
    place, core = position // 2, position % 2
    at = (place[None], core[None])

    def along(value, axis, pairs):
        return lax.ppermute(value, axis, pairs)

    def to_sibling(value):
        return along(value, "probe", [(i, i ^ 1) for i in range(shares)])

    def to_panel(value, by):
        return along(value, "samp", [(i, (i + by) % panels) for i in range(panels)])

    def to_panel_sibling(value, by):
        pairs = [
            (s * shares + i, ((s + by) % panels) * shares + (i ^ 1))
            for s in range(panels)
            for i in range(shares)
        ]
        return along(value, ("samp", "probe"), pairs)

    def swap_panels(value, bit):
        return along(value, "samp", [(i, i ^ bit) for i in range(panels)])

    def on_line(value, pairs):
        return along(value, "probe", [(2 * i + c, 2 * to + c) for i, to in pairs for c in (0, 1)])

    same = lax.dynamic_index_in_dim(methyl.reshape(line, 2, share, -1), core, 1, False)
    before_mine = to_panel(same.reshape(line * share, -1), 1)
    theirs = to_sibling(methyl)
    parts, panel, other = project(core[None], panel_ids, atlas, methyl, shares)
    parts = lax.all_to_all(parts, "probe", 0, 0)
    scores, copies = descend(parts)
    design = lax.all_to_all(copies, "probe", 0, 0)
    part = cross_products(design, methyl, panel)
    bit = panels // 2
    while bit > 1:
        part = part + swap_panels(part, bit)
        bit //= 2
    peer = swap_panels(part, 1)
    half = lax.dynamic_index_in_dim(design.reshape(line, 2, K, share), core, 1, False)
    design_before = to_panel(half, 1)
    before_theirs = to_panel_sibling(other, 1)
    facts = solve(part, peer, panel, 0.0001 * samples, samples)
    more = to_sibling(facts)

    def round_of(by):
        return [(i, (i + by) % line) for i in range(line)]

    def arrivals(sends):
        return [on_line(value, round_of(j)) for j, value in enumerate(sends, 1)]

    zscore, *sends, own_keep = own_tile(at, line, design, methyl, theirs, facts, more)
    own_parts = arrivals(sends)
    partial = pair_tile(at, line, design_before, before_mine, facts, zscore, 0, None)
    *sends, keep = pair_tile(at, line, design_before, before_theirs, more, zscore, 1, partial)
    left, same, other = fold(at, line, keep, arrivals(sends))
    same, other = to_panel(same, -1), to_panel_sibling(other, -1)
    shifted = [on_line(jnp.stack([same[j], other[j]]), round_of(j)) for j in range(1, line)]
    tiles = scale(probes, own_keep, own_parts, left)
    return finish(at, line, probes, tiles, same, other, shifted), scores


def solution(mesh):
    placed = (P("samp", "probe"), P(None, "probe"), P())
    return jax.shard_map(
        body,
        mesh=mesh,
        in_specs=placed,
        out_specs=(P(None, "samp", "probe"), P(None, ("samp", "probe"))),
        check_vma=False,
    )
```

```python
import functools

import jax
import jax.numpy as jnp
from jax import lax
from jax.experimental import pallas as pl
from jax.experimental.pallas import tpu as pltpu
from jax.sharding import PartitionSpec as P


K = 32
ITERS = 128
F32, BF16 = jnp.float32, jnp.bfloat16
HIGHEST = lax.Precision.HIGHEST
LANES = 128
VMEM_LIMIT = 40 * 1024 * 1024


def nt(a, b):
    return lax.dot_general(a, b, (((1,), (1,)), ((), ())), preferred_element_type=F32)


def tn(a, b):
    return lax.dot_general(a, b, (((0,), (0,)), ((), ())), preferred_element_type=F32)


def params(*semantics):
    return pltpu.CompilerParams(dimension_semantics=semantics, vmem_limit_bytes=VMEM_LIMIT)


def cost(flops, nbytes):
    return pl.CostEstimate(flops=int(flops), bytes_accessed=int(nbytes), transcendentals=0)


def three_terms(value):
    high = value.astype(BF16)
    rest = value - high.astype(F32)
    mid = rest.astype(BF16)
    low = (rest - mid.astype(F32)).astype(BF16)
    return jnp.concatenate([high, mid, low], axis=0)


def project_kernel(core_ref, ids_ref, atlas_ref, methyl_ref, out_ref, panel_ref, other_ref, gram_ref):
    kk = panel_ref.shape[0]
    blocks, _, share = out_ref.shape
    core = core_ref[0]

    @pl.when(pl.program_id(0) == 0)
    def _():
        rows = atlas_ref.shape[0]
        row = lax.broadcasted_iota(jnp.int32, (kk, rows), 0)
        wanted = jnp.zeros((kk, rows), jnp.int32)
        for k in range(kk):
            wanted = jnp.where(row == k, ids_ref[k], wanted)
        pick = wanted == lax.broadcasted_iota(jnp.int32, (kk, rows), 1)
        chosen = jnp.where(pick, 1.0, 0.0).astype(BF16)
        panel = jnp.dot(chosen, atlas_ref[...], preferred_element_type=F32).astype(BF16)
        panel_ref[...] = panel
        gram_ref[...] = nt(panel, panel)

    proj = nt(methyl_ref[...], panel_ref[...]).T
    for b in range(blocks):
        out_ref[b, :kk, :] = proj[:, b * share : (b + 1) * share]
        out_ref[b, kk:, :] = jnp.zeros((kk, share), F32)
        out_ref[b, kk:, :kk] = gram_ref[...]
    for b in range(blocks // 2):
        other = pl.multiple_of((2 * b + 1 - core) * share, share)
        other_ref[b * share : (b + 1) * share, :] = methyl_ref[pl.ds(other, share), :]


def project(core, panel_ids, atlas, methyl, shares):
    rows, probes = methyl.shape
    share = rows // shares
    chunk = row_chunk(share)
    half = pl.BlockSpec((chunk // 2, probes), lambda i: (i, 0))
    return pl.pallas_call(
        project_kernel,
        grid=(rows // chunk,),
        in_specs=[
            pl.BlockSpec(memory_space=pltpu.SMEM),
            pl.BlockSpec(memory_space=pltpu.SMEM),
            pl.BlockSpec(atlas.shape, lambda i: (0, 0)),
            pl.BlockSpec((chunk, probes), lambda i: (i, 0)),
        ],
        out_specs=(
            pl.BlockSpec((chunk // share, 2 * K, share), lambda i: (i, 0, 0)),
            pl.BlockSpec((K, probes), lambda i: (0, 0)),
            half,
        ),
        out_shape=(
            jax.ShapeDtypeStruct((shares, 2 * K, share), F32),
            jax.ShapeDtypeStruct((K, probes), BF16),
            jax.ShapeDtypeStruct((rows // 2, probes), BF16),
        ),
        scratch_shapes=[pltpu.VMEM((K, K), F32)],
        compiler_params=params("arbitrary"),
        cost_estimate=cost(2 * K * rows * probes, 4 * rows * probes),
        name="project",
    )(core, panel_ids, atlas, methyl)


def row_chunk(share):
    return 2 * share * max(1, 128 // share)


def descend_kernel(parts_ref, scores_ref, design_ref, spread_ref, w_ref):
    kk, share = w_ref.shape
    total = parts_ref[0]
    for peer in range(1, parts_ref.shape[0]):
        total = total + parts_ref[peer]
    gram = total[kk:, :kk]
    row = lax.broadcasted_iota(jnp.int32, (kk, kk), 0)
    col = lax.broadcasted_iota(jnp.int32, (kk, kk), 1)
    trace = jnp.sum(jnp.where(row == col, gram, 0.0), axis=(0, 1), keepdims=True)
    rate = 1.0 / trace
    step = jnp.where(row == col, 1.0, 0.0) - rate * gram
    pull = rate * total[:kk, :]
    for k in range(kk):
        spread_ref[k] = jnp.broadcast_to(step[:, k : k + 1], (kk, share))
    w_ref[...] = jnp.full((kk, share), 1.0 / kk, F32)

    def descend(_, carry):
        acc = [pull, None, None, None]
        for k in range(kk):
            term = spread_ref[k] * w_ref[k : k + 1, :]
            acc[k % 4] = term if acc[k % 4] is None else acc[k % 4] + term
        w_ref[...] = jnp.maximum((acc[0] + acc[1]) + (acc[2] + acc[3]), 0.0)
        return carry

    lax.fori_loop(0, ITERS, descend, 0)
    weights = w_ref[...]
    scores_ref[...] = kk * weights
    design = weights.astype(BF16)
    for peer in range(design_ref.shape[0]):
        design_ref[peer] = design


def descend(parts):
    shares, _, share = parts.shape
    return pl.pallas_call(
        descend_kernel,
        out_shape=(
            jax.ShapeDtypeStruct((K, share), F32),
            jax.ShapeDtypeStruct((shares, K, share), BF16),
        ),
        scratch_shapes=[pltpu.VMEM((K, K, share), F32), pltpu.VMEM((K, share), F32)],
        compiler_params=params(),
        cost_estimate=cost(2 * ITERS * K * K * share, 4 * K * share),
        name="descend",
    )(parts)


def cross_kernel(design_ref, methyl_ref, panel_ref, out_ref):
    blocks, kk, _ = design_ref.shape
    probes = methyl_ref.shape[1]
    design = jnp.concatenate([design_ref[b] for b in range(blocks)], axis=1)

    @pl.when(pl.program_id(0) == 0)
    def _():
        out_ref[...] = jnp.zeros_like(out_ref)

    out_ref[:, probes : probes + kk] += nt(design, design)
    width = min(probes, 512)
    for at in range(0, probes, width):
        cols = slice(at, at + width)
        out_ref[:, cols] += jnp.dot(design, methyl_ref[:, cols], preferred_element_type=F32)
        left = methyl_ref[:, cols].astype(F32) - tn(design, panel_ref[:, cols])
        squares = jnp.sum(left * left, axis=0, keepdims=True)
        for b in range(0, width, LANES):
            row = (at + b) // LANES
            out_ref[row : row + 1, probes + LANES :] += squares[:, b : b + LANES]


def cross_products(design, methyl, panel):
    _, _, share = design.shape
    rows, probes = methyl.shape
    chunk = row_chunk(share)
    return pl.pallas_call(
        cross_kernel,
        grid=(rows // chunk,),
        in_specs=[
            pl.BlockSpec((chunk // share, K, share), lambda i: (i, 0, 0)),
            pl.BlockSpec((chunk, probes), lambda i: (i, 0)),
            pl.BlockSpec((K, probes), lambda i: (0, 0)),
        ],
        out_specs=pl.BlockSpec((K, probes + 2 * LANES), lambda i: (0, 0)),
        out_shape=jax.ShapeDtypeStruct((K, probes + 2 * LANES), F32),
        compiler_params=params("arbitrary"),
        cost_estimate=cost(4 * K * rows * probes, 2 * rows * probes),
        name="cross",
    )(design, methyl, panel)


def ridge_inverse(matrix):
    kk = matrix.shape[0]
    row = lax.broadcasted_iota(jnp.int32, (kk, kk), 0)
    col = lax.broadcasted_iota(jnp.int32, (kk, kk), 1)
    work = jnp.concatenate([matrix, jnp.where(row == col, 1.0, 0.0)], axis=1)
    which = lax.broadcasted_iota(jnp.int32, (kk, 1), 0)
    for k in range(kk):
        pivot_row = work[k : k + 1, :] / work[k : k + 1, k : k + 1]
        factor = jnp.where(which == k, 0.0, work[:, k : k + 1])
        work = jnp.where(which == k, pivot_row, work - factor * pivot_row)
    return work[:, kk:]


def solve_kernel(ridge, samples, mine_ref, peer_ref, panel_ref, out_ref):
    kk, probes = panel_ref.shape
    total = mine_ref[...] + peer_ref[...]
    cross = total[:, :probes]
    wgram = total[:, probes : probes + kk]
    start = jnp.concatenate(
        [total[r : r + 1, probes + LANES :] for r in range(probes // LANES)], axis=1
    )
    row = lax.broadcasted_iota(jnp.int32, (kk, kk), 0)
    col = lax.broadcasted_iota(jnp.int32, (kk, kk), 1)
    system = wgram + jnp.where(row == col, ridge, 0.0)
    inverse = ridge_inverse(system)
    loadings = jnp.dot(inverse, cross, precision=HIGHEST)
    short = cross - jnp.dot(system, loadings, precision=HIGHEST)
    loadings = loadings + jnp.dot(inverse, short, precision=HIGHEST)
    panel = panel_ref[...].astype(F32)
    slope = jnp.dot(wgram, loadings + panel, precision=HIGHEST) - 2.0 * cross
    spread = start + jnp.sum((loadings - panel) * slope, axis=0, keepdims=True)
    rate = lax.rsqrt(jnp.maximum(spread, 0.0) / samples + 1e-06)
    out_ref[:kk, :] = loadings
    out_ref[kk:, :] = jnp.broadcast_to(rate, (out_ref.shape[0] - kk, probes))


def solve(mine, peer, panel, ridge, samples):
    probes = panel.shape[1]
    return pl.pallas_call(
        functools.partial(solve_kernel, ridge, samples),
        out_shape=jax.ShapeDtypeStruct((K + 8, probes), F32),
        compiler_params=params(),
        cost_estimate=cost(50 * K * K * probes, 20 * K * probes),
        name="solve",
    )(mine, peer, panel)


def standardise(design, methyl_ref, terms_ref, rate, store):
    probes = methyl_ref.shape[1]
    stacked = jnp.concatenate([design] * 3, axis=0)
    width = min(probes, 512)
    for at in range(0, probes, width):
        cols = slice(at, at + width)
        fitted = tn(stacked, terms_ref[:, cols])
        left = methyl_ref[:, cols].astype(F32) - fitted
        store(at, width, (left * rate[:, cols]).astype(BF16))


def put_tile(part, sends, keep_ref):
    share = keep_ref.shape[1]
    keep_ref[...] = part[:, :share]
    for j, ref in enumerate(sends, 1):
        ref[...] = part[:, j * share : (j + 1) * share].astype(BF16)


def own_kernel(
    steps, line, place_ref, core_ref, design_ref, mine_ref, theirs_ref, facts_ref, more_ref, *refs
):
    (z_ref, *sends), (keep_ref, half_ref, terms_ref, moreterms_ref) = refs[:line], refs[line:]
    step = pl.program_id(0)
    blocks, kk, share = design_ref.shape
    chunk, probes = mine_ref.shape
    place, core = place_ref[0], core_ref[0]

    @pl.when(step == 0)
    def _():
        terms_ref[...] = three_terms(facts_ref[:kk, :])
        moreterms_ref[...] = three_terms(more_ref[:kk, :])

    @pl.when(step < steps)
    def _():
        design = jnp.concatenate([design_ref[b] for b in range(blocks)], axis=1)
        rows = pl.ds(pl.multiple_of(step * chunk, chunk), chunk)

        def store(base, at, width, value):
            z_ref[rows, base + at : base + at + width] = value

        standardise(design, mine_ref, terms_ref, facts_ref[kk : kk + 1, :], functools.partial(store, 0))
        standardise(
            design, theirs_ref, moreterms_ref, more_ref[kk : kk + 1, :], functools.partial(store, probes)
        )
        for b in range(blocks // 2):
            here = pl.ds(pl.multiple_of(step * chunk + (2 * b + core) * share, share), share)
            slot = lax.rem(step * (blocks // 2) + b - place + line, line)
            half_ref[pl.ds(pl.multiple_of(slot * share, share), share), :] = z_ref[here, :]

    @pl.when(step >= steps)
    def _():
        tall = keep_ref.shape[0]
        rows = pl.ds(pl.multiple_of((step - steps) * tall, tall), tall)
        put_tile(nt(z_ref[rows, :], half_ref[...]), sends, keep_ref)


def own_tile(at, line, design, mine, theirs, facts, more):
    _, _, share = design.shape
    rows, probes = mine.shape
    chunk = row_chunk(share)
    steps, tall = rows // chunk, 2 * chunk

    def first(i, *_):
        return (jnp.minimum(i, steps - 1), 0)

    def second(i, *_):
        return (jnp.maximum(i - steps, 0), 0)

    whole = pl.BlockSpec((K + 8, probes), lambda i, *_: (0, 0))
    return pl.pallas_call(
        functools.partial(own_kernel, steps, line),
        grid_spec=pltpu.PrefetchScalarGridSpec(
            num_scalar_prefetch=2,
            grid=(steps + rows // tall,),
            in_specs=[
                pl.BlockSpec((chunk // share, K, share), lambda i, *_: (*first(i), 0)),
                pl.BlockSpec((chunk, probes), first),
                pl.BlockSpec((chunk, probes), first),
                whole,
                whole,
            ],
            out_specs=[pl.BlockSpec(memory_space=pltpu.VMEM)]
            + [pl.BlockSpec((tall, share), second)] * line,
            scratch_shapes=[
                pltpu.VMEM((rows // 2, 2 * probes), BF16),
                pltpu.VMEM((3 * K, probes), BF16),
                pltpu.VMEM((3 * K, probes), BF16),
            ],
        ),
        out_shape=[pltpu.VMEM((rows, 2 * probes), BF16)]
        + [jax.ShapeDtypeStruct((rows, share), BF16)] * (line - 1)
        + [jax.ShapeDtypeStruct((rows, share), F32)],
        compiler_params=params("arbitrary"),
        cost_estimate=cost(2 * rows * rows * probes, 12 * rows * probes),
        name="own",
    )(*at, design, mine, theirs, facts, more)


def pair_kernel(steps, line, last, tall, which, place_ref, design_ref, raw_ref, facts_ref, zscore_ref, *refs):
    refs, (z_ref, terms_ref) = refs[:-2], refs[-2:]
    step = pl.program_id(0)
    blocks, kk, share = design_ref.shape
    probes = raw_ref.shape[1]

    @pl.when(step == 0)
    def _():
        terms_ref[...] = three_terms(facts_ref[:kk, :])

    @pl.when(step < steps)
    def _():
        design = jnp.concatenate([design_ref[b] for b in range(blocks)], axis=1)

        def store(at, width, value):
            for b in range(blocks):
                slot = lax.rem(step * blocks + b - place_ref[0] + line, line)
                rows = pl.ds(pl.multiple_of(slot * share, share), share)
                z_ref[rows, at : at + width] = value[b * share : (b + 1) * share, :]

        standardise(design, raw_ref, terms_ref, facts_ref[kk : kk + 1, :], store)

    @pl.when(step >= steps)
    def _():
        rows = pl.ds(pl.multiple_of((step - steps) * tall, tall), tall)
        cols = slice(which * probes, (which + 1) * probes)
        part = nt(zscore_ref[rows, cols], z_ref[...])
        if last:
            put_tile(part + refs[0][...], refs[1:-1], refs[-1])
        else:
            refs[0][...] = part


def pair_tile(at, line, design, raw, facts, zscore, which, partial):
    _, _, share = design.shape
    half, probes = raw.shape
    rows = zscore.shape[0]
    chunk = row_chunk(share)
    steps, tall = half // chunk, 2 * chunk
    last = partial is not None

    def first(i, *_):
        return (jnp.minimum(i, steps - 1), 0)

    def second(i, *_):
        return (jnp.maximum(i - steps, 0), 0)

    total = pl.BlockSpec((tall, half), second)
    if last:
        out_specs = [pl.BlockSpec((tall, share), second)] * line
        out_shape = [jax.ShapeDtypeStruct((rows, share), BF16)] * (line - 1)
        out_shape += [jax.ShapeDtypeStruct((rows, share), F32)]
    else:
        out_specs = total
        out_shape = jax.ShapeDtypeStruct((rows, half), F32)
    return pl.pallas_call(
        functools.partial(pair_kernel, steps, line, last, tall, which),
        grid_spec=pltpu.PrefetchScalarGridSpec(
            num_scalar_prefetch=1,
            grid=(steps + rows // tall,),
            in_specs=[
                pl.BlockSpec((chunk // share, K, share), lambda i, *_: (*first(i), 0)),
                pl.BlockSpec((chunk, probes), first),
                pl.BlockSpec((K + 8, probes), lambda i, *_: (0, 0)),
                pl.BlockSpec(memory_space=pltpu.VMEM),
            ]
            + [total] * last,
            out_specs=out_specs,
            scratch_shapes=[pltpu.VMEM((half, probes), BF16), pltpu.VMEM((3 * K, probes), BF16)],
        ),
        out_shape=out_shape,
        compiler_params=params("arbitrary"),
        cost_estimate=cost(rows * rows * probes, 8 * rows * probes),
        name="pair_last" if last else "pair_first",
    )(at[0], design, raw, facts, zscore, *([partial] * last))


def fold_kernel(line, place_ref, core_ref, keep_ref, *refs):
    parts, (total_ref, same_ref, other_ref) = refs[:-3], refs[-3:]
    place, core = place_ref[0], core_ref[0]
    share = same_ref.shape[1]
    total = keep_ref[...]
    for ref in parts:
        total = total + ref[...].astype(F32)
    total_ref[...] = total
    for j in range(line):
        block = 2 * lax.rem(place + j, line)
        same = pl.ds(pl.multiple_of((block + core) * share, share), share)
        other = pl.ds(pl.multiple_of((block + 1 - core) * share, share), share)
        same_ref[j] = total_ref[same, :].astype(BF16)
        other_ref[j] = total_ref[other, :].astype(BF16)


def fold(at, line, keep, parts):
    rows, share = keep.shape
    blocks = jax.ShapeDtypeStruct((line, share, share), BF16)
    vmem = pl.BlockSpec(memory_space=pltpu.VMEM)
    return pl.pallas_call(
        functools.partial(fold_kernel, line),
        in_specs=[pl.BlockSpec(memory_space=pltpu.SMEM)] * 2 + [vmem] * (1 + len(parts)),
        out_shape=(jax.ShapeDtypeStruct((rows, share), F32), blocks, blocks),
        compiler_params=params(),
        cost_estimate=cost(rows * share * 8, rows * share * 16),
        name="fold",
    )(*at, keep, *parts)


def scale_kernel(probes, own_ref, *refs):
    parts, (left_ref, out_ref) = refs[:-2], refs[-2:]
    total = own_ref[...]
    for ref in parts:
        total = total + ref[...].astype(F32)
    out_ref[0] = total * (1.0 / probes)
    out_ref[1] = left_ref[...] * (1.0 / probes)


def scale(probes, keep, parts, left):
    rows, share = keep.shape
    vmem = pl.BlockSpec((rows, share), lambda i: (0, 0))
    return pl.pallas_call(
        functools.partial(scale_kernel, probes),
        grid=(1,),
        in_specs=[vmem] * (2 + len(parts)),
        out_specs=pl.BlockSpec((2, rows, share), lambda i: (0, 0, 0)),
        out_shape=jax.ShapeDtypeStruct((3, rows, share), F32),
        compiler_params=params("arbitrary"),
        cost_estimate=cost(rows * share * 16, rows * share * 30),
        name="scale",
    )(keep, *parts, left)


def finish_kernel(line, probes, place_ref, core_ref, _, same_ref, other_ref, *refs):
    shifted, out_ref = refs[:-1], refs[-1]
    place, core = place_ref[0], core_ref[0]
    share = same_ref.shape[1]
    for j in range(line):
        block = 2 * lax.rem(place - j + line, line)
        for side in range(2):
            piece = (same_ref, other_ref)[side][0] if j == 0 else shifted[j - 1][side]
            to = block + (core if side == 0 else 1 - core)
            rows = pl.ds(pl.multiple_of(to * share, share), share)
            out_ref[0, rows, :] = piece.astype(F32).T * (1.0 / probes)


def finish(at, line, probes, tiles, same, other, shifted):
    _, rows, share = tiles.shape
    first = pl.BlockSpec((1, share, share), lambda i: (0, 0, 0))
    pair = pl.BlockSpec((2, share, share), lambda i: (0, 0, 0))
    return pl.pallas_call(
        functools.partial(finish_kernel, line, probes),
        grid=(1,),
        in_specs=[pl.BlockSpec(memory_space=pltpu.SMEM)] * 2
        + [pl.BlockSpec(memory_space=pl.ANY), first, first]
        + [pair] * len(shifted),
        out_specs=pl.BlockSpec((1, rows, share), lambda i: (2, 0, 0)),
        out_shape=jax.ShapeDtypeStruct(tiles.shape, F32),
        input_output_aliases={2: 0},
        compiler_params=params("arbitrary"),
        cost_estimate=cost(rows * share * 4, rows * share * 8),
        name="finish",
    )(*at, tiles, same, other, *shifted)


def body(methyl, atlas, panel_ids):
    panels, shares = lax.axis_size("samp"), lax.axis_size("probe")
    rows = methyl.shape[0]
    samples = rows * panels
    probes = methyl.shape[1] * shares
    share = rows // shares
    line = shares // 2
    position = lax.axis_index("probe")
    place, core = position // 2, position % 2
    at = (place[None], core[None])

    def along(value, axis, pairs):
        return lax.ppermute(value, axis, pairs)

    def to_sibling(value):
        return along(value, "probe", [(i, i ^ 1) for i in range(shares)])

    def to_panel(value, by):
        return along(value, "samp", [(i, (i + by) % panels) for i in range(panels)])

    def to_panel_sibling(value, by):
        pairs = [
            (s * shares + i, ((s + by) % panels) * shares + (i ^ 1))
            for s in range(panels)
            for i in range(shares)
        ]
        return along(value, ("samp", "probe"), pairs)

    def swap_panels(value, bit):
        return along(value, "samp", [(i, i ^ bit) for i in range(panels)])

    def on_line(value, pairs):
        return along(value, "probe", [(2 * i + c, 2 * to + c) for i, to in pairs for c in (0, 1)])

    same = lax.dynamic_index_in_dim(methyl.reshape(line, 2, share, -1), core, 1, False)
    before_mine = to_panel(same.reshape(line * share, -1), 1)
    theirs = to_sibling(methyl)
    parts, panel, other = project(core[None], panel_ids, atlas, methyl, shares)
    parts = lax.all_to_all(parts, "probe", 0, 0)
    scores, copies = descend(parts)
    design = lax.all_to_all(copies, "probe", 0, 0)
    part = cross_products(design, methyl, panel)
    peer = swap_panels(part, 1)
    bit = 2
    while bit < panels:
        part = part + peer
        peer = swap_panels(part, bit)
        bit *= 2
    half = lax.dynamic_index_in_dim(design.reshape(line, 2, K, share), core, 1, False)
    design_before = to_panel(half, 1)
    before_theirs = to_panel_sibling(other, 1)
    facts = solve(part, peer, panel, 0.0001 * samples, samples)
    more = to_sibling(facts)

    def round_of(by):
        return [(i, (i + by) % line) for i in range(line)]

    def arrivals(sends):
        return [on_line(value, round_of(j)) for j, value in enumerate(sends, 1)]

    zscore, *sends, own_keep = own_tile(at, line, design, methyl, theirs, facts, more)
    own_parts = arrivals(sends)
    partial = pair_tile(at, line, design_before, before_mine, facts, zscore, 0, None)
    *sends, keep = pair_tile(at, line, design_before, before_theirs, more, zscore, 1, partial)
    left, same, other = fold(at, line, keep, arrivals(sends))
    same = to_panel(same, -1)
    other = to_panel_sibling(other, -1)
    shifted = [on_line(jnp.stack([same[j], other[j]]), round_of(j)) for j in range(1, line)]
    tiles = scale(probes, own_keep, own_parts, left)
    return finish(at, line, probes, tiles, same, other, shifted), scores


def solution(mesh):
    placed = (P("samp", "probe"), P(None, "probe"), P())
    return jax.shard_map(
        body,
        mesh=mesh,
        in_specs=placed,
        out_specs=(P(None, "samp", "probe"), P(None, ("samp", "probe"))),
        check_vma=False,
    )
```

```python
import functools

import jax
import jax.numpy as jnp
from jax import lax
from jax.experimental import pallas as pl
from jax.experimental.pallas import tpu as pltpu
from jax.sharding import PartitionSpec as P


K = 32
ITERS = 128
F32, BF16 = jnp.float32, jnp.bfloat16
HIGHEST = lax.Precision.HIGHEST
LANES = 128
VMEM_LIMIT = 40 * 1024 * 1024


def nt(a, b):
    return lax.dot_general(a, b, (((1,), (1,)), ((), ())), preferred_element_type=F32)


def tn(a, b):
    return lax.dot_general(a, b, (((0,), (0,)), ((), ())), preferred_element_type=F32)


def params(*semantics):
    return pltpu.CompilerParams(dimension_semantics=semantics, vmem_limit_bytes=VMEM_LIMIT)


def cost(flops, nbytes):
    return pl.CostEstimate(flops=int(flops), bytes_accessed=int(nbytes), transcendentals=0)


def three_terms(value):
    high = value.astype(BF16)
    rest = value - high.astype(F32)
    mid = rest.astype(BF16)
    low = (rest - mid.astype(F32)).astype(BF16)
    return jnp.concatenate([high, mid, low], axis=0)


def project_kernel(
    quarter, core_ref, ids_ref, atlas_ref, methyl_ref, out_ref, panel_ref, low_ref, high_ref, same_ref,
    other_ref, gram_ref,
):
    kk = panel_ref.shape[0]
    blocks, _, share = out_ref.shape
    core = core_ref[0]

    @pl.when(pl.program_id(0) == 0)
    def _():
        rows = atlas_ref.shape[0]
        row = lax.broadcasted_iota(jnp.int32, (kk, rows), 0)
        wanted = jnp.zeros((kk, rows), jnp.int32)
        for k in range(kk):
            wanted = jnp.where(row == k, ids_ref[k], wanted)
        pick = wanted == lax.broadcasted_iota(jnp.int32, (kk, rows), 1)
        chosen = jnp.where(pick, 1.0, 0.0).astype(BF16)
        panel = jnp.dot(chosen, atlas_ref[...], preferred_element_type=F32).astype(BF16)
        panel_ref[...] = panel
        gram_ref[...] = nt(panel, panel)

    proj = nt(methyl_ref[...], panel_ref[...]).T
    for b in range(blocks):
        out_ref[b, :kk, :] = proj[:, b * share : (b + 1) * share]
        out_ref[b, kk:, :] = jnp.zeros((kk, share), F32)
        out_ref[b, kk:, :kk] = gram_ref[...]

    def put(ref, side):
        for b in range(blocks // 2):
            start = pl.multiple_of((2 * b + side) * share, share)
            ref[b * share : (b + 1) * share, :] = methyl_ref[pl.ds(start, share), :]

    step, steps = pl.program_id(0), pl.num_programs(0)

    @pl.when(step < quarter)
    def _():
        put(low_ref, 1 - core)

    @pl.when(step >= steps - quarter)
    def _():
        put(high_ref, 1 - core)

    @pl.when((step >= quarter) & (step < steps - quarter))
    def _():
        put(same_ref, core)
        put(other_ref, 1 - core)


def project(core, panel_ids, atlas, methyl, shares):
    rows, probes = methyl.shape
    share = rows // shares
    chunk = row_chunk(share)
    steps = rows // chunk
    quarter = steps // 4

    def half(first, count):
        return pl.BlockSpec((chunk // 2, probes), lambda i: (jnp.clip(i - first, 0, count - 1), 0))

    def rows_of(count):
        return jax.ShapeDtypeStruct((count * chunk // 2, probes), BF16)

    return pl.pallas_call(
        functools.partial(project_kernel, quarter),
        grid=(steps,),
        in_specs=[
            pl.BlockSpec(memory_space=pltpu.SMEM),
            pl.BlockSpec(memory_space=pltpu.SMEM),
            pl.BlockSpec(atlas.shape, lambda i: (0, 0)),
            pl.BlockSpec((chunk, probes), lambda i: (i, 0)),
        ],
        out_specs=(
            pl.BlockSpec((chunk // share, 2 * K, share), lambda i: (i, 0, 0)),
            pl.BlockSpec((K, probes), lambda i: (0, 0)),
            half(0, quarter),
            half(steps - quarter, quarter),
            half(quarter, steps - 2 * quarter),
            half(quarter, steps - 2 * quarter),
        ),
        out_shape=(
            jax.ShapeDtypeStruct((shares, 2 * K, share), F32),
            jax.ShapeDtypeStruct((K, probes), BF16),
            rows_of(quarter),
            rows_of(quarter),
            rows_of(steps - 2 * quarter),
            rows_of(steps - 2 * quarter),
        ),
        scratch_shapes=[pltpu.VMEM((K, K), F32)],
        compiler_params=params("arbitrary"),
        cost_estimate=cost(2 * K * rows * probes, 4 * rows * probes),
        name="project",
    )(core, panel_ids, atlas, methyl)


def row_chunk(share):
    return 2 * share * max(1, 128 // share)


def descend_kernel(parts_ref, scores_ref, design_ref, spread_ref, w_ref):
    kk, share = w_ref.shape
    total = parts_ref[0]
    for peer in range(1, parts_ref.shape[0]):
        total = total + parts_ref[peer]
    gram = total[kk:, :kk]
    row = lax.broadcasted_iota(jnp.int32, (kk, kk), 0)
    col = lax.broadcasted_iota(jnp.int32, (kk, kk), 1)
    trace = jnp.sum(jnp.where(row == col, gram, 0.0), axis=(0, 1), keepdims=True)
    rate = 1.0 / trace
    step = jnp.where(row == col, 1.0, 0.0) - rate * gram
    pull = rate * total[:kk, :]
    for k in range(kk):
        spread_ref[k] = jnp.broadcast_to(step[:, k : k + 1], (kk, share))
    w_ref[...] = jnp.full((kk, share), 1.0 / kk, F32)

    def descend(_, carry):
        acc = [pull, None, None, None]
        for k in range(kk):
            term = spread_ref[k] * w_ref[k : k + 1, :]
            acc[k % 4] = term if acc[k % 4] is None else acc[k % 4] + term
        w_ref[...] = jnp.maximum((acc[0] + acc[1]) + (acc[2] + acc[3]), 0.0)
        return carry

    lax.fori_loop(0, ITERS, descend, 0)
    weights = w_ref[...]
    scores_ref[...] = kk * weights
    design = weights.astype(BF16)
    for peer in range(design_ref.shape[0]):
        design_ref[peer] = design


def descend(parts):
    shares, _, share = parts.shape
    return pl.pallas_call(
        descend_kernel,
        out_shape=(
            jax.ShapeDtypeStruct((K, share), F32),
            jax.ShapeDtypeStruct((shares, K, share), BF16),
        ),
        scratch_shapes=[pltpu.VMEM((K, K, share), F32), pltpu.VMEM((K, share), F32)],
        compiler_params=params(),
        cost_estimate=cost(2 * ITERS * K * K * share, 4 * K * share),
        name="descend",
    )(parts)


def cross_kernel(design_ref, methyl_ref, panel_ref, out_ref):
    blocks, kk, _ = design_ref.shape
    probes = methyl_ref.shape[1]
    design = jnp.concatenate([design_ref[b] for b in range(blocks)], axis=1)

    @pl.when(pl.program_id(0) == 0)
    def _():
        out_ref[...] = jnp.zeros_like(out_ref)

    out_ref[:, probes : probes + kk] += nt(design, design)
    width = min(probes, 512)
    for at in range(0, probes, width):
        cols = slice(at, at + width)
        out_ref[:, cols] += jnp.dot(design, methyl_ref[:, cols], preferred_element_type=F32)
        left = methyl_ref[:, cols].astype(F32) - tn(design, panel_ref[:, cols])
        squares = jnp.sum(left * left, axis=0, keepdims=True)
        for b in range(0, width, LANES):
            row = (at + b) // LANES
            out_ref[row : row + 1, probes + LANES :] += squares[:, b : b + LANES]


def cross_products(design, methyl, panel):
    _, _, share = design.shape
    rows, probes = methyl.shape
    chunk = row_chunk(share)
    return pl.pallas_call(
        cross_kernel,
        grid=(rows // chunk,),
        in_specs=[
            pl.BlockSpec((chunk // share, K, share), lambda i: (i, 0, 0)),
            pl.BlockSpec((chunk, probes), lambda i: (i, 0)),
            pl.BlockSpec((K, probes), lambda i: (0, 0)),
        ],
        out_specs=pl.BlockSpec((K, probes + 2 * LANES), lambda i: (0, 0)),
        out_shape=jax.ShapeDtypeStruct((K, probes + 2 * LANES), F32),
        compiler_params=params("arbitrary"),
        cost_estimate=cost(4 * K * rows * probes, 2 * rows * probes),
        name="cross",
    )(design, methyl, panel)


def ridge_inverse(matrix):
    kk = matrix.shape[0]
    row = lax.broadcasted_iota(jnp.int32, (kk, kk), 0)
    col = lax.broadcasted_iota(jnp.int32, (kk, kk), 1)
    work = jnp.concatenate([matrix, jnp.where(row == col, 1.0, 0.0)], axis=1)
    which = lax.broadcasted_iota(jnp.int32, (kk, 1), 0)
    for k in range(kk):
        pivot_row = work[k : k + 1, :] / work[k : k + 1, k : k + 1]
        factor = jnp.where(which == k, 0.0, work[:, k : k + 1])
        work = jnp.where(which == k, pivot_row, work - factor * pivot_row)
    return work[:, kk:]


def solve_kernel(ridge, samples, mine_ref, peer_ref, panel_ref, out_ref):
    kk, probes = panel_ref.shape
    total = mine_ref[...] + peer_ref[...]
    cross = total[:, :probes]
    wgram = total[:, probes : probes + kk]
    start = jnp.concatenate(
        [total[r : r + 1, probes + LANES :] for r in range(probes // LANES)], axis=1
    )
    row = lax.broadcasted_iota(jnp.int32, (kk, kk), 0)
    col = lax.broadcasted_iota(jnp.int32, (kk, kk), 1)
    system = wgram + jnp.where(row == col, ridge, 0.0)
    inverse = ridge_inverse(system)
    loadings = jnp.dot(inverse, cross, precision=HIGHEST)
    short = cross - jnp.dot(system, loadings, precision=HIGHEST)
    loadings = loadings + jnp.dot(inverse, short, precision=HIGHEST)
    panel = panel_ref[...].astype(F32)
    slope = jnp.dot(wgram, loadings + panel, precision=HIGHEST) - 2.0 * cross
    spread = start + jnp.sum((loadings - panel) * slope, axis=0, keepdims=True)
    rate = lax.rsqrt(jnp.maximum(spread, 0.0) / samples + 1e-06)
    out_ref[:kk, :] = loadings
    out_ref[kk:, :] = jnp.broadcast_to(rate, (out_ref.shape[0] - kk, probes))


def solve(mine, peer, panel, ridge, samples):
    probes = panel.shape[1]
    return pl.pallas_call(
        functools.partial(solve_kernel, ridge, samples),
        out_shape=jax.ShapeDtypeStruct((K + 8, probes), F32),
        compiler_params=params(),
        cost_estimate=cost(50 * K * K * probes, 20 * K * probes),
        name="solve",
    )(mine, peer, panel)


def standardise(design, methyl_ref, terms_ref, rate, store):
    probes = methyl_ref.shape[1]
    stacked = jnp.concatenate([design] * 3, axis=0)
    width = min(probes, 512)
    for at in range(0, probes, width):
        cols = slice(at, at + width)
        fitted = tn(stacked, terms_ref[:, cols])
        left = methyl_ref[:, cols].astype(F32) - fitted
        store(at, width, (left * rate[:, cols]).astype(BF16))


def put_tile(part, sends, keep_ref):
    share = keep_ref.shape[1]
    keep_ref[...] = part[:, :share]
    for j, ref in enumerate(sends, 1):
        ref[...] = part[:, j * share : (j + 1) * share].astype(BF16)


def own_kernel(
    steps, line, place_ref, core_ref, design_ref, mine_ref, theirs_ref, facts_ref, more_ref, *refs
):
    (z_ref, *sends), (keep_ref, half_ref, terms_ref, moreterms_ref) = refs[:line], refs[line:]
    step = pl.program_id(0)
    blocks, kk, share = design_ref.shape
    chunk, probes = mine_ref.shape
    place, core = place_ref[0], core_ref[0]

    @pl.when(step == 0)
    def _():
        terms_ref[...] = three_terms(facts_ref[:kk, :])
        moreterms_ref[...] = three_terms(more_ref[:kk, :])

    @pl.when(step < steps)
    def _():
        design = jnp.concatenate([design_ref[b] for b in range(blocks)], axis=1)
        rows = pl.ds(pl.multiple_of(step * chunk, chunk), chunk)

        def store(base, at, width, value):
            z_ref[rows, base + at : base + at + width] = value

        standardise(design, mine_ref, terms_ref, facts_ref[kk : kk + 1, :], functools.partial(store, 0))
        standardise(
            design, theirs_ref, moreterms_ref, more_ref[kk : kk + 1, :], functools.partial(store, probes)
        )
        for b in range(blocks // 2):
            here = pl.ds(pl.multiple_of(step * chunk + (2 * b + core) * share, share), share)
            slot = lax.rem(step * (blocks // 2) + b - place + line, line)
            half_ref[pl.ds(pl.multiple_of(slot * share, share), share), :] = z_ref[here, :]

    @pl.when(step >= steps)
    def _():
        tall = keep_ref.shape[0]
        rows = pl.ds(pl.multiple_of((step - steps) * tall, tall), tall)
        put_tile(nt(z_ref[rows, :], half_ref[...]), sends, keep_ref)


def own_tile(at, line, design, mine, theirs, facts, more):
    _, _, share = design.shape
    rows, probes = mine.shape
    chunk = row_chunk(share)
    steps, tall = rows // chunk, 2 * chunk

    def first(i, *_):
        return (jnp.minimum(i, steps - 1), 0)

    def second(i, *_):
        return (jnp.maximum(i - steps, 0), 0)

    whole = pl.BlockSpec((K + 8, probes), lambda i, *_: (0, 0))
    return pl.pallas_call(
        functools.partial(own_kernel, steps, line),
        grid_spec=pltpu.PrefetchScalarGridSpec(
            num_scalar_prefetch=2,
            grid=(steps + rows // tall,),
            in_specs=[
                pl.BlockSpec((chunk // share, K, share), lambda i, *_: (*first(i), 0)),
                pl.BlockSpec((chunk, probes), first),
                pl.BlockSpec((chunk, probes), first),
                whole,
                whole,
            ],
            out_specs=[pl.BlockSpec(memory_space=pltpu.VMEM)]
            + [pl.BlockSpec((tall, share), second)] * line,
            scratch_shapes=[
                pltpu.VMEM((rows // 2, 2 * probes), BF16),
                pltpu.VMEM((3 * K, probes), BF16),
                pltpu.VMEM((3 * K, probes), BF16),
            ],
        ),
        out_shape=[pltpu.VMEM((rows, 2 * probes), BF16)]
        + [jax.ShapeDtypeStruct((rows, share), BF16)] * (line - 1)
        + [jax.ShapeDtypeStruct((rows, share), F32)],
        compiler_params=params("arbitrary"),
        cost_estimate=cost(2 * rows * rows * probes, 12 * rows * probes),
        name="own",
    )(*at, design, mine, theirs, facts, more)


def pair_kernel(index_of, line, count, place_ref, design_ref, facts_ref, more_ref, zscore_ref, *refs):
    mine, theirs, refs = refs[: count[0]], refs[count[0] : sum(count)], refs[sum(count) :]
    (*sends, keep_ref), (z_ref, terms_ref, moreterms_ref) = refs[:-3], refs[-3:]
    blocks, kk, share = design_ref.shape
    probes = facts_ref.shape[1]
    tall = keep_ref.shape[0]
    step, place = pl.program_id(0), place_ref[0]

    @pl.when(step == 0)
    def _():
        terms_ref[...] = three_terms(facts_ref[:kk, :])
        moreterms_ref[...] = three_terms(more_ref[:kk, :])
        design = jnp.concatenate([design_ref[b] for b in range(blocks)], axis=1)
        for base, pieces, facts, terms in (
            (0, mine, facts_ref, terms_ref),
            (probes, theirs, more_ref, moreterms_ref),
        ):
            top = 0
            for piece in pieces:
                rows = slice(top, top + piece.shape[0])

                def store(at, width, value):
                    z_ref[rows, base + at : base + at + width] = value

                standardise(design[:, rows], piece, terms, facts[kk : kk + 1, :], store)
                top += piece.shape[0]

    @pl.when(step > 0)
    def _():
        rows = pl.ds(pl.multiple_of((step - 1) * tall, tall), tall)
        part = nt(zscore_ref[rows, :], z_ref[...])
        for j, ref in enumerate([keep_ref, *sends]):
            index, inside = index_of(lax.rem(place + j, line))
            block = part[:, :share]
            for b in range(1, blocks):
                block = jnp.where(index == b, part[:, b * share : (b + 1) * share], block)
            if j == 0:
                block = jnp.where(inside, block, 0.0)
            ref[...] = block.astype(ref.dtype)


def pair_tile(index_of, at, line, design, mine, theirs, facts, more, zscore):
    blocks, _, share = design.shape
    rows, depth = zscore.shape
    probes = depth // 2
    tall = 2 * row_chunk(share)
    vmem = pl.BlockSpec(memory_space=pltpu.VMEM)
    column = pl.BlockSpec((tall, share), lambda i, *_: (jnp.maximum(i - 1, 0), 0))
    return pl.pallas_call(
        functools.partial(pair_kernel, index_of, line, (len(mine), len(theirs))),
        grid_spec=pltpu.PrefetchScalarGridSpec(
            num_scalar_prefetch=1,
            grid=(1 + rows // tall,),
            in_specs=[vmem] * (4 + len(mine) + len(theirs)),
            out_specs=[column] * line,
            scratch_shapes=[
                pltpu.VMEM((blocks * share, depth), BF16),
                pltpu.VMEM((3 * K, probes), BF16),
                pltpu.VMEM((3 * K, probes), BF16),
            ],
        ),
        out_shape=[jax.ShapeDtypeStruct((rows, share), BF16)] * (line - 1)
        + [jax.ShapeDtypeStruct((rows, share), F32)],
        compiler_params=params("arbitrary"),
        cost_estimate=cost(2 * rows * blocks * share * depth, 8 * rows * probes),
    )(at[0], design, facts, more, zscore, *mine, *theirs)


def fold_kernel(line, place_ref, core_ref, *refs):
    (keep_ref, *parts), (total_ref, same_ref, other_ref) = refs[:-3], refs[-3:]
    place, core = place_ref[0], core_ref[0]
    share = same_ref.shape[1]
    total = keep_ref[...]
    for ref in parts:
        total = total + ref[...].astype(F32)
    total_ref[...] = total
    for j in range(line):
        block = 2 * lax.rem(place + j, line)
        same = pl.ds(pl.multiple_of((block + core) * share, share), share)
        other = pl.ds(pl.multiple_of((block + 1 - core) * share, share), share)
        same_ref[j] = total_ref[same, :].astype(BF16)
        other_ref[j] = total_ref[other, :].astype(BF16)


def fold(at, line, parts):
    rows, share = parts[0].shape
    blocks = jax.ShapeDtypeStruct((line, share, share), BF16)
    vmem = pl.BlockSpec(memory_space=pltpu.VMEM)
    return pl.pallas_call(
        functools.partial(fold_kernel, line),
        in_specs=[pl.BlockSpec(memory_space=pltpu.SMEM)] * 2 + [vmem] * len(parts),
        out_shape=(jax.ShapeDtypeStruct((rows, share), F32), blocks, blocks),
        compiler_params=params(),
        cost_estimate=cost(rows * share * 8, rows * share * 16),
        name="fold",
    )(*at, *parts)


def scale_kernel(probes, own_ref, *refs):
    parts, (left_ref, out_ref) = refs[:-2], refs[-2:]
    total = own_ref[...]
    for ref in parts:
        total = total + ref[...].astype(F32)
    out_ref[0] = total * (1.0 / probes)
    out_ref[1] = left_ref[...] * (1.0 / probes)


def scale(probes, keep, parts, left):
    rows, share = keep.shape
    vmem = pl.BlockSpec((rows, share), lambda i: (0, 0))
    return pl.pallas_call(
        functools.partial(scale_kernel, probes),
        grid=(1,),
        in_specs=[vmem] * (2 + len(parts)),
        out_specs=pl.BlockSpec((2, rows, share), lambda i: (0, 0, 0)),
        out_shape=jax.ShapeDtypeStruct((3, rows, share), F32),
        compiler_params=params("arbitrary"),
        cost_estimate=cost(rows * share * 16, rows * share * 30),
        name="scale",
    )(keep, *parts, left)


def finish_kernel(line, probes, place_ref, core_ref, _, same_ref, other_ref, *refs):
    shifted, out_ref = refs[:-1], refs[-1]
    place, core = place_ref[0], core_ref[0]
    share = same_ref.shape[1]
    for j in range(line):
        block = 2 * lax.rem(place - j + line, line)
        for side in range(2):
            piece = (same_ref, other_ref)[side][0] if j == 0 else shifted[j - 1][side]
            to = block + (core if side == 0 else 1 - core)
            rows = pl.ds(pl.multiple_of(to * share, share), share)
            out_ref[0, rows, :] = piece.astype(F32).T * (1.0 / probes)


def finish(at, line, probes, tiles, same, other, shifted):
    _, rows, share = tiles.shape
    first = pl.BlockSpec((1, share, share), lambda i: (0, 0, 0))
    pair = pl.BlockSpec((2, share, share), lambda i: (0, 0, 0))
    return pl.pallas_call(
        functools.partial(finish_kernel, line, probes),
        grid=(1,),
        in_specs=[pl.BlockSpec(memory_space=pltpu.SMEM)] * 2
        + [pl.BlockSpec(memory_space=pl.ANY), first, first]
        + [pair] * len(shifted),
        out_specs=pl.BlockSpec((1, rows, share), lambda i: (2, 0, 0)),
        out_shape=jax.ShapeDtypeStruct(tiles.shape, F32),
        input_output_aliases={2: 0},
        compiler_params=params("arbitrary"),
        cost_estimate=cost(rows * share * 4, rows * share * 8),
        name="finish",
    )(*at, tiles, same, other, *shifted)


def body(methyl, atlas, panel_ids):
    panels, shares = lax.axis_size("samp"), lax.axis_size("probe")
    rows = methyl.shape[0]
    samples = rows * panels
    probes = methyl.shape[1] * shares
    share = rows // shares
    line = shares // 2
    position = lax.axis_index("probe")
    place, core = position // 2, position % 2
    at = (place[None], core[None])

    def along(value, axis, pairs):
        return lax.ppermute(value, axis, pairs)

    def to_sibling(value):
        return along(value, "probe", [(i, i ^ 1) for i in range(shares)])

    def to_panel(value, by):
        return along(value, "samp", [(i, (i + by) % panels) for i in range(panels)])

    def to_panel_sibling(value, by):
        pairs = [
            (s * shares + i, ((s + by) % panels) * shares + (i ^ 1))
            for s in range(panels)
            for i in range(shares)
        ]
        return along(value, ("samp", "probe"), pairs)

    def swap_panels(value, bit):
        return along(value, "samp", [(i, i ^ bit) for i in range(panels)])

    def on_line(value, pairs):
        return along(value, "probe", [(2 * i + c, 2 * to + c) for i, to in pairs for c in (0, 1)])

    quarter = line // 4
    ends = [*range(quarter), *range(line - quarter, line)]
    inner = [*range(quarter, line - quarter)]

    def among_ends(to):
        high = to >= line - quarter
        return jnp.where(high, to - (line - 2 * quarter), to), (to < quarter) | high

    def among_inner(to):
        return to - quarter, (to >= quarter) & (to < line - quarter)

    halves = methyl.reshape(line, 2, share, -1)
    first = jnp.concatenate(
        [
            lax.dynamic_index_in_dim(halves[:quarter], core, 1, False),
            lax.dynamic_index_in_dim(halves[line - quarter :], core, 1, False),
        ]
    )
    ends_mine = to_panel(first.reshape(len(ends) * share, -1), 1)
    theirs = to_sibling(methyl)
    parts, panel, low, high, same, other = project(core[None], panel_ids, atlas, methyl, shares)
    ends_low = to_panel_sibling(low, 1)
    parts = lax.all_to_all(parts, "probe", 0, 0)
    scores, copies = descend(parts)
    design = lax.all_to_all(copies, "probe", 0, 0)
    part = cross_products(design, methyl, panel)
    peer = swap_panels(part, 1)
    bit = 2
    while bit < panels:
        part = part + peer
        peer = swap_panels(part, bit)
        bit *= 2
    half = lax.dynamic_index_in_dim(design.reshape(line, 2, K, share), core, 1, False)
    design_before = to_panel(half, 1)
    ends_high = to_panel_sibling(high, 1)
    inner_mine = to_panel(same, 1)
    inner_theirs = to_panel_sibling(other, 1)
    facts = solve(part, peer, panel, 0.0001 * samples, samples)
    more = to_sibling(facts)

    def round_of(by, among=None):
        pairs = [(i, (i + by) % line) for i in range(line)]
        return pairs if among is None else [(i, to) for i, to in pairs if to in among]

    def arrivals(sends, among=None):
        return [on_line(value, round_of(j, among)) for j, value in enumerate(sends, 1)]

    zscore, *sends, own_keep = own_tile(at, line, design, methyl, theirs, facts, more)
    own_parts = arrivals(sends)
    design_ends = jnp.concatenate([design_before[:quarter], design_before[line - quarter :]])
    *sends, keep = pair_tile(
        among_ends, at, line, design_ends, [ends_mine], [ends_low, ends_high],
        facts, more, zscore,
    )
    pair_parts = [keep] + arrivals(sends, ends)
    *sends, keep = pair_tile(
        among_inner, at, line, design_before[quarter : line - quarter],
        [inner_mine], [inner_theirs], facts, more, zscore,
    )
    pair_parts += [keep] + arrivals(sends, inner)
    left, same, other = fold(at, line, pair_parts)
    same = to_panel(same, -1)
    other = to_panel_sibling(other, -1)
    shifted = [on_line(jnp.stack([same[j], other[j]]), round_of(j)) for j in range(1, line)]
    tiles = scale(probes, own_keep, own_parts, left)
    return finish(at, line, probes, tiles, same, other, shifted), scores


def solution(mesh):
    placed = (P("samp", "probe"), P(None, "probe"), P())
    return jax.shard_map(
        body,
        mesh=mesh,
        in_specs=placed,
        out_specs=(P(None, "samp", "probe"), P(None, ("samp", "probe"))),
        check_vma=False,
    )
```

```python
import functools

import jax
import jax.numpy as jnp
from jax import lax
from jax.experimental import pallas as pl
from jax.experimental.pallas import tpu as pltpu
from jax.sharding import PartitionSpec as P


K = 32
ITERS = 128
F32, BF16 = jnp.float32, jnp.bfloat16
HIGHEST = lax.Precision.HIGHEST
LANES = 128
VMEM_LIMIT = 40 * 1024 * 1024


def nt(a, b):
    return lax.dot_general(a, b, (((1,), (1,)), ((), ())), preferred_element_type=F32)


def tn(a, b):
    return lax.dot_general(a, b, (((0,), (0,)), ((), ())), preferred_element_type=F32)


def params(*semantics):
    return pltpu.CompilerParams(dimension_semantics=semantics, vmem_limit_bytes=VMEM_LIMIT)


def cost(flops, nbytes):
    return pl.CostEstimate(flops=int(flops), bytes_accessed=int(nbytes), transcendentals=0)


def three_terms(value):
    high = value.astype(BF16)
    rest = value - high.astype(F32)
    mid = rest.astype(BF16)
    low = (rest - mid.astype(F32)).astype(BF16)
    return jnp.concatenate([high, mid, low], axis=0)


def project_kernel(
    quarter, core_ref, ids_ref, atlas_ref, methyl_ref, out_ref, panel_ref, outer_ref, same_ref, other_ref,
    gram_ref,
):
    kk = panel_ref.shape[0]
    blocks, _, share = out_ref.shape
    core = core_ref[0]

    @pl.when(pl.program_id(0) == 0)
    def _():
        rows = atlas_ref.shape[0]
        row = lax.broadcasted_iota(jnp.int32, (kk, rows), 0)
        wanted = jnp.zeros((kk, rows), jnp.int32)
        for k in range(kk):
            wanted = jnp.where(row == k, ids_ref[k], wanted)
        pick = wanted == lax.broadcasted_iota(jnp.int32, (kk, rows), 1)
        chosen = jnp.where(pick, 1.0, 0.0).astype(BF16)
        panel = jnp.dot(chosen, atlas_ref[...], preferred_element_type=F32).astype(BF16)
        panel_ref[...] = panel
        gram_ref[...] = nt(panel, panel)

    proj = nt(methyl_ref[...], panel_ref[...]).T
    for b in range(blocks):
        out_ref[b, :kk, :] = proj[:, b * share : (b + 1) * share]
        out_ref[b, kk:, :] = jnp.zeros((kk, share), F32)
        out_ref[b, kk:, :kk] = gram_ref[...]

    def put(ref, side):
        for b in range(blocks // 2):
            start = pl.multiple_of((2 * b + side) * share, share)
            ref[b * share : (b + 1) * share, :] = methyl_ref[pl.ds(start, share), :]

    step, steps = pl.program_id(0), pl.num_programs(0)

    @pl.when((step < quarter) | (step >= steps - quarter))
    def _():
        put(outer_ref, 1 - core)

    @pl.when((step >= quarter) & (step < steps - quarter))
    def _():
        put(same_ref, core)
        put(other_ref, 1 - core)


def project(core, panel_ids, atlas, methyl, shares):
    rows, probes = methyl.shape
    share = rows // shares
    chunk = row_chunk(share)
    steps = rows // chunk
    quarter = steps // 4

    def outer(i):
        return (jnp.where(i < steps - quarter, jnp.minimum(i, quarter - 1), i - steps + 2 * quarter), 0)

    def inner(i):
        return (jnp.clip(i - quarter, 0, steps - 2 * quarter - 1), 0)

    def rows_of(count):
        return jax.ShapeDtypeStruct((count * chunk // 2, probes), BF16)

    return pl.pallas_call(
        functools.partial(project_kernel, quarter),
        grid=(steps,),
        in_specs=[
            pl.BlockSpec(memory_space=pltpu.SMEM),
            pl.BlockSpec(memory_space=pltpu.SMEM),
            pl.BlockSpec(atlas.shape, lambda i: (0, 0)),
            pl.BlockSpec((chunk, probes), lambda i: (i, 0)),
        ],
        out_specs=(
            pl.BlockSpec((chunk // share, 2 * K, share), lambda i: (i, 0, 0)),
            pl.BlockSpec((K, probes), lambda i: (0, 0)),
            pl.BlockSpec((chunk // 2, probes), outer),
            pl.BlockSpec((chunk // 2, probes), inner),
            pl.BlockSpec((chunk // 2, probes), inner),
        ),
        out_shape=(
            jax.ShapeDtypeStruct((shares, 2 * K, share), F32),
            jax.ShapeDtypeStruct((K, probes), BF16),
            rows_of(2 * quarter),
            rows_of(steps - 2 * quarter),
            rows_of(steps - 2 * quarter),
        ),
        scratch_shapes=[pltpu.VMEM((K, K), F32)],
        compiler_params=params("arbitrary"),
        cost_estimate=cost(2 * K * rows * probes, 4 * rows * probes),
        name="project",
    )(core, panel_ids, atlas, methyl)


def copy_kernel(_, from_ref, to_ref):
    to_ref[...] = from_ref[...]


def pick_ends(core, methyl, line, share):
    probes = methyl.shape[1]
    quarter = line // 4

    def block(i, core):
        return (2 * jnp.where(i < quarter, i, i + line - 2 * quarter) + core[0], 0)

    return pl.pallas_call(
        copy_kernel,
        grid_spec=pltpu.PrefetchScalarGridSpec(
            num_scalar_prefetch=1,
            grid=(2 * quarter,),
            in_specs=[pl.BlockSpec((share, probes), block)],
            out_specs=pl.BlockSpec((share, probes), lambda i, core: (i, 0)),
        ),
        out_shape=jax.ShapeDtypeStruct((2 * quarter * share, probes), BF16),
        compiler_params=params("arbitrary"),
        cost_estimate=cost(0, 8 * quarter * share * probes),
        name="pick_ends",
    )(core, methyl)


def row_chunk(share):
    return 2 * share * max(1, 128 // share)


def descend_kernel(parts_ref, scores_ref, design_ref, spread_ref, w_ref):
    kk, share = w_ref.shape
    total = parts_ref[0]
    for peer in range(1, parts_ref.shape[0]):
        total = total + parts_ref[peer]
    gram = total[kk:, :kk]
    row = lax.broadcasted_iota(jnp.int32, (kk, kk), 0)
    col = lax.broadcasted_iota(jnp.int32, (kk, kk), 1)
    trace = jnp.sum(jnp.where(row == col, gram, 0.0), axis=(0, 1), keepdims=True)
    rate = 1.0 / trace
    step = jnp.where(row == col, 1.0, 0.0) - rate * gram
    pull = rate * total[:kk, :]
    for k in range(kk):
        spread_ref[k] = jnp.broadcast_to(step[:, k : k + 1], (kk, share))
    w_ref[...] = jnp.full((kk, share), 1.0 / kk, F32)

    def descend(_, carry):
        acc = [pull, None, None, None]
        for k in range(kk):
            term = spread_ref[k] * w_ref[k : k + 1, :]
            acc[k % 4] = term if acc[k % 4] is None else acc[k % 4] + term
        w_ref[...] = jnp.maximum((acc[0] + acc[1]) + (acc[2] + acc[3]), 0.0)
        return carry

    lax.fori_loop(0, ITERS, descend, 0)
    weights = w_ref[...]
    scores_ref[...] = kk * weights
    design = weights.astype(BF16)
    for peer in range(design_ref.shape[0]):
        design_ref[peer] = design


def descend(parts):
    shares, _, share = parts.shape
    return pl.pallas_call(
        descend_kernel,
        out_shape=(
            jax.ShapeDtypeStruct((K, share), F32),
            jax.ShapeDtypeStruct((shares, K, share), BF16),
        ),
        scratch_shapes=[pltpu.VMEM((K, K, share), F32), pltpu.VMEM((K, share), F32)],
        compiler_params=params(),
        cost_estimate=cost(2 * ITERS * K * K * share, 4 * K * share),
        name="descend",
    )(parts)


def cross_kernel(design_ref, methyl_ref, panel_ref, out_ref):
    blocks, kk, _ = design_ref.shape
    probes = methyl_ref.shape[1]
    design = jnp.concatenate([design_ref[b] for b in range(blocks)], axis=1)

    @pl.when(pl.program_id(0) == 0)
    def _():
        out_ref[...] = jnp.zeros_like(out_ref)

    out_ref[:, probes : probes + kk] += nt(design, design)
    width = min(probes, 512)
    for at in range(0, probes, width):
        cols = slice(at, at + width)
        out_ref[:, cols] += jnp.dot(design, methyl_ref[:, cols], preferred_element_type=F32)
        left = methyl_ref[:, cols].astype(F32) - tn(design, panel_ref[:, cols])
        squares = jnp.sum(left * left, axis=0, keepdims=True)
        for b in range(0, width, LANES):
            row = (at + b) // LANES
            out_ref[row : row + 1, probes + LANES :] += squares[:, b : b + LANES]


def cross_products(design, methyl, panel):
    _, _, share = design.shape
    rows, probes = methyl.shape
    chunk = row_chunk(share)
    return pl.pallas_call(
        cross_kernel,
        grid=(rows // chunk,),
        in_specs=[
            pl.BlockSpec((chunk // share, K, share), lambda i: (i, 0, 0)),
            pl.BlockSpec((chunk, probes), lambda i: (i, 0)),
            pl.BlockSpec((K, probes), lambda i: (0, 0)),
        ],
        out_specs=pl.BlockSpec((K, probes + 2 * LANES), lambda i: (0, 0)),
        out_shape=jax.ShapeDtypeStruct((K, probes + 2 * LANES), F32),
        compiler_params=params("arbitrary"),
        cost_estimate=cost(4 * K * rows * probes, 2 * rows * probes),
        name="cross",
    )(design, methyl, panel)


def ridge_inverse(matrix):
    kk = matrix.shape[0]
    row = lax.broadcasted_iota(jnp.int32, (kk, kk), 0)
    col = lax.broadcasted_iota(jnp.int32, (kk, kk), 1)
    work = jnp.concatenate([matrix, jnp.where(row == col, 1.0, 0.0)], axis=1)
    which = lax.broadcasted_iota(jnp.int32, (kk, 1), 0)
    for k in range(kk):
        pivot_row = work[k : k + 1, :] / work[k : k + 1, k : k + 1]
        factor = jnp.where(which == k, 0.0, work[:, k : k + 1])
        work = jnp.where(which == k, pivot_row, work - factor * pivot_row)
    return work[:, kk:]


def solve_kernel(ridge, samples, mine_ref, peer_ref, panel_ref, out_ref):
    kk, probes = panel_ref.shape
    total = mine_ref[...] + peer_ref[...]
    cross = total[:, :probes]
    wgram = total[:, probes : probes + kk]
    start = jnp.concatenate(
        [total[r : r + 1, probes + LANES :] for r in range(probes // LANES)], axis=1
    )
    row = lax.broadcasted_iota(jnp.int32, (kk, kk), 0)
    col = lax.broadcasted_iota(jnp.int32, (kk, kk), 1)
    system = wgram + jnp.where(row == col, ridge, 0.0)
    inverse = ridge_inverse(system)
    loadings = jnp.dot(inverse, cross, precision=HIGHEST)
    short = cross - jnp.dot(system, loadings, precision=HIGHEST)
    loadings = loadings + jnp.dot(inverse, short, precision=HIGHEST)
    panel = panel_ref[...].astype(F32)
    slope = jnp.dot(wgram, loadings + panel, precision=HIGHEST) - 2.0 * cross
    spread = start + jnp.sum((loadings - panel) * slope, axis=0, keepdims=True)
    rate = lax.rsqrt(jnp.maximum(spread, 0.0) / samples + 1e-06)
    out_ref[:kk, :] = loadings
    out_ref[kk:, :] = jnp.broadcast_to(rate, (out_ref.shape[0] - kk, probes))


def solve(mine, peer, panel, ridge, samples):
    probes = panel.shape[1]
    return pl.pallas_call(
        functools.partial(solve_kernel, ridge, samples),
        out_shape=jax.ShapeDtypeStruct((K + 8, probes), F32),
        compiler_params=params(),
        cost_estimate=cost(50 * K * K * probes, 20 * K * probes),
        name="solve",
    )(mine, peer, panel)


def standardise(design, methyl_ref, terms_ref, rate, store):
    probes = methyl_ref.shape[1]
    stacked = jnp.concatenate([design] * 3, axis=0)
    width = min(probes, 512)
    for at in range(0, probes, width):
        cols = slice(at, at + width)
        fitted = tn(stacked, terms_ref[:, cols])
        left = methyl_ref[:, cols].astype(F32) - fitted
        store(at, width, (left * rate[:, cols]).astype(BF16))


def put_tile(part, sends, keep_ref):
    share = keep_ref.shape[1]
    keep_ref[...] = part[:, :share]
    for j, ref in enumerate(sends, 1):
        ref[...] = part[:, j * share : (j + 1) * share].astype(BF16)


def own_kernel(
    steps, line, place_ref, core_ref, design_ref, mine_ref, theirs_ref, facts_ref, more_ref, *refs
):
    (z_ref, *sends), (keep_ref, half_ref, terms_ref, moreterms_ref) = refs[:line], refs[line:]
    step = pl.program_id(0)
    blocks, kk, share = design_ref.shape
    chunk, probes = mine_ref.shape
    place, core = place_ref[0], core_ref[0]

    @pl.when(step == 0)
    def _():
        terms_ref[...] = three_terms(facts_ref[:kk, :])
        moreterms_ref[...] = three_terms(more_ref[:kk, :])

    @pl.when(step < steps)
    def _():
        design = jnp.concatenate([design_ref[b] for b in range(blocks)], axis=1)
        rows = pl.ds(pl.multiple_of(step * chunk, chunk), chunk)

        def store(base, at, width, value):
            z_ref[rows, base + at : base + at + width] = value

        standardise(design, mine_ref, terms_ref, facts_ref[kk : kk + 1, :], functools.partial(store, 0))
        standardise(
            design, theirs_ref, moreterms_ref, more_ref[kk : kk + 1, :], functools.partial(store, probes)
        )
        for b in range(blocks // 2):
            here = pl.ds(pl.multiple_of(step * chunk + (2 * b + core) * share, share), share)
            slot = lax.rem(step * (blocks // 2) + b - place + line, line)
            half_ref[pl.ds(pl.multiple_of(slot * share, share), share), :] = z_ref[here, :]

    @pl.when(step >= steps)
    def _():
        tall = keep_ref.shape[0]
        rows = pl.ds(pl.multiple_of((step - steps) * tall, tall), tall)
        put_tile(nt(z_ref[rows, :], half_ref[...]), sends, keep_ref)


def own_tile(at, line, design, mine, theirs, facts, more):
    _, _, share = design.shape
    rows, probes = mine.shape
    chunk = row_chunk(share)
    steps, tall = rows // chunk, 2 * chunk

    def first(i, *_):
        return (jnp.minimum(i, steps - 1), 0)

    def second(i, *_):
        return (jnp.maximum(i - steps, 0), 0)

    whole = pl.BlockSpec((K + 8, probes), lambda i, *_: (0, 0))
    return pl.pallas_call(
        functools.partial(own_kernel, steps, line),
        grid_spec=pltpu.PrefetchScalarGridSpec(
            num_scalar_prefetch=2,
            grid=(steps + rows // tall,),
            in_specs=[
                pl.BlockSpec((chunk // share, K, share), lambda i, *_: (*first(i), 0)),
                pl.BlockSpec((chunk, probes), first),
                pl.BlockSpec((chunk, probes), first),
                whole,
                whole,
            ],
            out_specs=[pl.BlockSpec(memory_space=pltpu.VMEM)]
            + [pl.BlockSpec((tall, share), second)] * line,
            scratch_shapes=[
                pltpu.VMEM((rows // 2, 2 * probes), BF16),
                pltpu.VMEM((3 * K, probes), BF16),
                pltpu.VMEM((3 * K, probes), BF16),
            ],
        ),
        out_shape=[pltpu.VMEM((rows, 2 * probes), BF16)]
        + [jax.ShapeDtypeStruct((rows, share), BF16)] * (line - 1)
        + [jax.ShapeDtypeStruct((rows, share), F32)],
        compiler_params=params("arbitrary"),
        cost_estimate=cost(2 * rows * rows * probes, 12 * rows * probes),
        name="own",
    )(*at, design, mine, theirs, facts, more)


def pair_kernel(index_of, line, count, place_ref, design_ref, facts_ref, more_ref, zscore_ref, *refs):
    mine, theirs, refs = refs[: count[0]], refs[count[0] : sum(count)], refs[sum(count) :]
    (*sends, keep_ref), (z_ref, terms_ref, moreterms_ref) = refs[:-3], refs[-3:]
    blocks, kk, share = design_ref.shape
    probes = facts_ref.shape[1]
    tall = keep_ref.shape[0]
    step, place = pl.program_id(0), place_ref[0]

    @pl.when(step == 0)
    def _():
        terms_ref[...] = three_terms(facts_ref[:kk, :])
        moreterms_ref[...] = three_terms(more_ref[:kk, :])
        design = jnp.concatenate([design_ref[b] for b in range(blocks)], axis=1)
        for base, pieces, facts, terms in (
            (0, mine, facts_ref, terms_ref),
            (probes, theirs, more_ref, moreterms_ref),
        ):
            top = 0
            for piece in pieces:
                rows = slice(top, top + piece.shape[0])

                def store(at, width, value):
                    z_ref[rows, base + at : base + at + width] = value

                standardise(design[:, rows], piece, terms, facts[kk : kk + 1, :], store)
                top += piece.shape[0]

    @pl.when(step > 0)
    def _():
        rows = pl.ds(pl.multiple_of((step - 1) * tall, tall), tall)
        part = nt(zscore_ref[rows, :], z_ref[...])
        for j, ref in enumerate([keep_ref, *sends]):
            index, inside = index_of(lax.rem(place + j, line))
            block = part[:, :share]
            for b in range(1, blocks):
                block = jnp.where(index == b, part[:, b * share : (b + 1) * share], block)
            if j == 0:
                block = jnp.where(inside, block, 0.0)
            ref[...] = block.astype(ref.dtype)


def pair_tile(index_of, at, line, design, mine, theirs, facts, more, zscore):
    blocks, _, share = design.shape
    rows, depth = zscore.shape
    probes = depth // 2
    tall = 2 * row_chunk(share)
    vmem = pl.BlockSpec(memory_space=pltpu.VMEM)
    column = pl.BlockSpec((tall, share), lambda i, *_: (jnp.maximum(i - 1, 0), 0))
    return pl.pallas_call(
        functools.partial(pair_kernel, index_of, line, (len(mine), len(theirs))),
        grid_spec=pltpu.PrefetchScalarGridSpec(
            num_scalar_prefetch=1,
            grid=(1 + rows // tall,),
            in_specs=[vmem] * (4 + len(mine) + len(theirs)),
            out_specs=[column] * line,
            scratch_shapes=[
                pltpu.VMEM((blocks * share, depth), BF16),
                pltpu.VMEM((3 * K, probes), BF16),
                pltpu.VMEM((3 * K, probes), BF16),
            ],
        ),
        out_shape=[jax.ShapeDtypeStruct((rows, share), BF16)] * (line - 1)
        + [jax.ShapeDtypeStruct((rows, share), F32)],
        compiler_params=params("arbitrary"),
        cost_estimate=cost(2 * rows * blocks * share * depth, 8 * rows * probes),
    )(at[0], design, facts, more, zscore, *mine, *theirs)


def fold_kernel(line, place_ref, core_ref, *refs):
    (keep_ref, *parts), (total_ref, same_ref, other_ref) = refs[:-3], refs[-3:]
    place, core = place_ref[0], core_ref[0]
    share = same_ref.shape[1]
    total = keep_ref[...]
    for ref in parts:
        total = total + ref[...].astype(F32)
    total_ref[...] = total
    for j in range(line):
        block = 2 * lax.rem(place + j, line)
        same = pl.ds(pl.multiple_of((block + core) * share, share), share)
        other = pl.ds(pl.multiple_of((block + 1 - core) * share, share), share)
        same_ref[j] = total_ref[same, :].astype(BF16)
        other_ref[j] = total_ref[other, :].astype(BF16)


def fold(at, line, parts):
    rows, share = parts[0].shape
    blocks = jax.ShapeDtypeStruct((line, share, share), BF16)
    vmem = pl.BlockSpec(memory_space=pltpu.VMEM)
    return pl.pallas_call(
        functools.partial(fold_kernel, line),
        in_specs=[pl.BlockSpec(memory_space=pltpu.SMEM)] * 2 + [vmem] * len(parts),
        out_shape=(jax.ShapeDtypeStruct((rows, share), F32), blocks, blocks),
        compiler_params=params(),
        cost_estimate=cost(rows * share * 8, rows * share * 16),
        name="fold",
    )(*at, *parts)


def scale_kernel(probes, own_ref, *refs):
    parts, (left_ref, out_ref) = refs[:-2], refs[-2:]
    total = own_ref[...]
    for ref in parts:
        total = total + ref[...].astype(F32)
    out_ref[0] = total * (1.0 / probes)
    out_ref[1] = left_ref[...] * (1.0 / probes)


def scale(probes, keep, parts, left):
    rows, share = keep.shape
    vmem = pl.BlockSpec((rows, share), lambda i: (0, 0))
    return pl.pallas_call(
        functools.partial(scale_kernel, probes),
        grid=(1,),
        in_specs=[vmem] * (2 + len(parts)),
        out_specs=pl.BlockSpec((2, rows, share), lambda i: (0, 0, 0)),
        out_shape=jax.ShapeDtypeStruct((3, rows, share), F32),
        compiler_params=params("arbitrary"),
        cost_estimate=cost(rows * share * 16, rows * share * 30),
        name="scale",
    )(keep, *parts, left)


def finish_kernel(line, probes, place_ref, core_ref, _, same_ref, other_ref, *refs):
    shifted, out_ref = refs[:-1], refs[-1]
    place, core = place_ref[0], core_ref[0]
    share = same_ref.shape[1]
    for j in range(line):
        block = 2 * lax.rem(place - j + line, line)
        for side in range(2):
            piece = (same_ref, other_ref)[side][0] if j == 0 else shifted[j - 1][side]
            to = block + (core if side == 0 else 1 - core)
            rows = pl.ds(pl.multiple_of(to * share, share), share)
            out_ref[0, rows, :] = piece.astype(F32).T * (1.0 / probes)


def finish(at, line, probes, tiles, same, other, shifted):
    _, rows, share = tiles.shape
    first = pl.BlockSpec((1, share, share), lambda i: (0, 0, 0))
    pair = pl.BlockSpec((2, share, share), lambda i: (0, 0, 0))
    return pl.pallas_call(
        functools.partial(finish_kernel, line, probes),
        grid=(1,),
        in_specs=[pl.BlockSpec(memory_space=pltpu.SMEM)] * 2
        + [pl.BlockSpec(memory_space=pl.ANY), first, first]
        + [pair] * len(shifted),
        out_specs=pl.BlockSpec((1, rows, share), lambda i: (2, 0, 0)),
        out_shape=jax.ShapeDtypeStruct(tiles.shape, F32),
        input_output_aliases={2: 0},
        compiler_params=params("arbitrary"),
        cost_estimate=cost(rows * share * 4, rows * share * 8),
        name="finish",
    )(*at, tiles, same, other, *shifted)


def body(methyl, atlas, panel_ids):
    panels, shares = lax.axis_size("samp"), lax.axis_size("probe")
    rows = methyl.shape[0]
    samples = rows * panels
    probes = methyl.shape[1] * shares
    share = rows // shares
    line = shares // 2
    position = lax.axis_index("probe")
    place, core = position // 2, position % 2
    at = (place[None], core[None])

    def along(value, axis, pairs):
        return lax.ppermute(value, axis, pairs)

    def to_sibling(value):
        return along(value, "probe", [(i, i ^ 1) for i in range(shares)])

    def to_panel(value, by):
        return along(value, "samp", [(i, (i + by) % panels) for i in range(panels)])

    def to_panel_sibling(value, by):
        pairs = [
            (s * shares + i, ((s + by) % panels) * shares + (i ^ 1))
            for s in range(panels)
            for i in range(shares)
        ]
        return along(value, ("samp", "probe"), pairs)

    def swap_panels(value, bit):
        return along(value, "samp", [(i, i ^ bit) for i in range(panels)])

    def on_line(value, pairs):
        return along(value, "probe", [(2 * i + c, 2 * to + c) for i, to in pairs for c in (0, 1)])

    quarter = line // 4
    ends = [*range(quarter), *range(line - quarter, line)]
    inner = [*range(quarter, line - quarter)]

    def among_ends(to):
        high = to >= line - quarter
        return jnp.where(high, to - (line - 2 * quarter), to), (to < quarter) | high

    def among_inner(to):
        return to - quarter, (to >= quarter) & (to < line - quarter)

    ends_mine = to_panel(pick_ends(core[None], methyl, line, share), 1)
    theirs = to_sibling(methyl)
    parts, panel, outer, same, other = project(core[None], panel_ids, atlas, methyl, shares)
    ends_theirs = to_panel_sibling(outer, 1)
    parts = lax.all_to_all(parts, "probe", 0, 0)
    scores, copies = descend(parts)
    design = lax.all_to_all(copies, "probe", 0, 0)
    part = cross_products(design, methyl, panel)
    bit = panels // 2
    while bit > 1:
        part = part + swap_panels(part, bit)
        bit //= 2
    peer = swap_panels(part, 1)
    half = lax.dynamic_index_in_dim(design.reshape(line, 2, K, share), core, 1, False)
    design_before = to_panel(half, 1)
    inner_mine = to_panel(same, 1)
    inner_theirs = to_panel_sibling(other, 1)
    facts = solve(part, peer, panel, 0.0001 * samples, samples)
    more = to_sibling(facts)

    def round_of(by, among=None):
        pairs = [(i, (i + by) % line) for i in range(line)]
        return pairs if among is None else [(i, to) for i, to in pairs if to in among]

    def arrivals(sends, among=None, rounds=None):
        return [
            on_line(value, round_of(j, among))
            for j, value in enumerate(sends, 1)
            if rounds is None or j in rounds
        ]

    early = {1, line - 1}
    late = set(range(1, line)) - early

    zscore, *own_sends, own_keep = own_tile(at, line, design, methyl, theirs, facts, more)
    own_parts = arrivals(own_sends, rounds=early)
    design_ends = jnp.concatenate([design_before[:quarter], design_before[line - quarter :]])
    *sends, keep = pair_tile(
        among_ends, at, line, design_ends, [ends_mine], [ends_theirs],
        facts, more, zscore,
    )
    pair_parts = [keep] + arrivals(sends, ends)
    *sends, keep = pair_tile(
        among_inner, at, line, design_before[quarter : line - quarter],
        [inner_mine], [inner_theirs], facts, more, zscore,
    )
    pair_parts += [keep] + arrivals(sends, inner)
    own_parts += arrivals(own_sends, rounds=late)
    left, same, other = fold(at, line, pair_parts)
    same = to_panel(same, -1)
    other = to_panel_sibling(other, -1)
    shifted = [on_line(jnp.stack([same[j], other[j]]), round_of(j)) for j in range(1, line)]
    tiles = scale(probes, own_keep, own_parts, left)
    return finish(at, line, probes, tiles, same, other, shifted), scores


def solution(mesh):
    placed = (P("samp", "probe"), P(None, "probe"), P())
    return jax.shard_map(
        body,
        mesh=mesh,
        in_specs=placed,
        out_specs=(P(None, "samp", "probe"), P(None, ("samp", "probe"))),
        check_vma=False,
    )
```

```python
import functools

import jax
import jax.numpy as jnp
from jax import lax
from jax.experimental import pallas as pl
from jax.experimental.pallas import tpu as pltpu
from jax.sharding import PartitionSpec as P


K = 32
ITERS = 128
F32, BF16 = jnp.float32, jnp.bfloat16
HIGHEST = lax.Precision.HIGHEST
LANES = 128
VMEM_LIMIT = 40 * 1024 * 1024


def nt(a, b):
    return lax.dot_general(a, b, (((1,), (1,)), ((), ())), preferred_element_type=F32)


def tn(a, b):
    return lax.dot_general(a, b, (((0,), (0,)), ((), ())), preferred_element_type=F32)


def params(*semantics):
    return pltpu.CompilerParams(dimension_semantics=semantics, vmem_limit_bytes=VMEM_LIMIT)


def cost(flops, nbytes):
    return pl.CostEstimate(flops=int(flops), bytes_accessed=int(nbytes), transcendentals=0)


def three_terms(value):
    high = value.astype(BF16)
    rest = value - high.astype(F32)
    mid = rest.astype(BF16)
    low = (rest - mid.astype(F32)).astype(BF16)
    return jnp.concatenate([high, mid, low], axis=0)


def project_kernel(
    quarter, core_ref, ids_ref, atlas_ref, methyl_ref, out_ref, panel_ref, outer_ref, same_ref, other_ref,
    gram_ref,
):
    kk = panel_ref.shape[0]
    blocks, _, share = out_ref.shape
    core = core_ref[0]

    @pl.when(pl.program_id(0) == 0)
    def _():
        rows = atlas_ref.shape[0]
        row = lax.broadcasted_iota(jnp.int32, (kk, rows), 0)
        wanted = jnp.zeros((kk, rows), jnp.int32)
        for k in range(kk):
            wanted = jnp.where(row == k, ids_ref[k], wanted)
        pick = wanted == lax.broadcasted_iota(jnp.int32, (kk, rows), 1)
        chosen = jnp.where(pick, 1.0, 0.0).astype(BF16)
        panel = jnp.dot(chosen, atlas_ref[...], preferred_element_type=F32).astype(BF16)
        panel_ref[...] = panel
        gram_ref[...] = nt(panel, panel)

    proj = nt(methyl_ref[...], panel_ref[...]).T
    for b in range(blocks):
        out_ref[b, :kk, :] = proj[:, b * share : (b + 1) * share]
        out_ref[b, kk:, :] = jnp.zeros((kk, share), F32)
        out_ref[b, kk:, :kk] = gram_ref[...]

    def put(ref, side):
        for b in range(blocks // 2):
            start = pl.multiple_of((2 * b + side) * share, share)
            ref[b * share : (b + 1) * share, :] = methyl_ref[pl.ds(start, share), :]

    step, steps = pl.program_id(0), pl.num_programs(0)

    @pl.when((step < quarter) | (step >= steps - quarter))
    def _():
        put(outer_ref, 1 - core)

    @pl.when((step >= quarter) & (step < steps - quarter))
    def _():
        put(same_ref, core)
        put(other_ref, 1 - core)


def project(core, panel_ids, atlas, methyl, shares):
    rows, probes = methyl.shape
    share = rows // shares
    chunk = row_chunk(share)
    steps = rows // chunk
    quarter = steps // 4

    def outer(i):
        return (jnp.where(i < steps - quarter, jnp.minimum(i, quarter - 1), i - steps + 2 * quarter), 0)

    def inner(i):
        return (jnp.clip(i - quarter, 0, steps - 2 * quarter - 1), 0)

    def rows_of(count):
        return jax.ShapeDtypeStruct((count * chunk // 2, probes), BF16)

    return pl.pallas_call(
        functools.partial(project_kernel, quarter),
        grid=(steps,),
        in_specs=[
            pl.BlockSpec(memory_space=pltpu.SMEM),
            pl.BlockSpec(memory_space=pltpu.SMEM),
            pl.BlockSpec(atlas.shape, lambda i: (0, 0)),
            pl.BlockSpec((chunk, probes), lambda i: (i, 0)),
        ],
        out_specs=(
            pl.BlockSpec((chunk // share, 2 * K, share), lambda i: (i, 0, 0)),
            pl.BlockSpec((K, probes), lambda i: (0, 0)),
            pl.BlockSpec((chunk // 2, probes), outer),
            pl.BlockSpec((chunk // 2, probes), inner),
            pl.BlockSpec((chunk // 2, probes), inner),
        ),
        out_shape=(
            jax.ShapeDtypeStruct((shares, 2 * K, share), F32),
            jax.ShapeDtypeStruct((K, probes), BF16),
            rows_of(2 * quarter),
            rows_of(steps - 2 * quarter),
            rows_of(steps - 2 * quarter),
        ),
        scratch_shapes=[pltpu.VMEM((K, K), F32)],
        compiler_params=params("arbitrary"),
        cost_estimate=cost(2 * K * rows * probes, 4 * rows * probes),
        name="project",
    )(core, panel_ids, atlas, methyl)


def copy_kernel(_, from_ref, to_ref):
    to_ref[...] = from_ref[...]


def pick_ends(core, methyl, line, share):
    probes = methyl.shape[1]
    quarter = line // 4

    def block(i, core):
        return (2 * jnp.where(i < quarter, i, i + line - 2 * quarter) + core[0], 0)

    return pl.pallas_call(
        copy_kernel,
        grid_spec=pltpu.PrefetchScalarGridSpec(
            num_scalar_prefetch=1,
            grid=(2 * quarter,),
            in_specs=[pl.BlockSpec((share, probes), block)],
            out_specs=pl.BlockSpec((share, probes), lambda i, core: (i, 0)),
        ),
        out_shape=jax.ShapeDtypeStruct((2 * quarter * share, probes), BF16),
        compiler_params=params("arbitrary"),
        cost_estimate=cost(0, 8 * quarter * share * probes),
        name="pick_ends",
    )(core, methyl)


def row_chunk(share):
    return 2 * share * max(1, 128 // share)


def descend_kernel(parts_ref, scores_ref, design_ref, spread_ref, w_ref):
    kk, share = w_ref.shape
    total = parts_ref[0]
    for peer in range(1, parts_ref.shape[0]):
        total = total + parts_ref[peer]
    gram = total[kk:, :kk]
    row = lax.broadcasted_iota(jnp.int32, (kk, kk), 0)
    col = lax.broadcasted_iota(jnp.int32, (kk, kk), 1)
    trace = jnp.sum(jnp.where(row == col, gram, 0.0), axis=(0, 1), keepdims=True)
    rate = 1.0 / trace
    step = jnp.where(row == col, 1.0, 0.0) - rate * gram
    pull = rate * total[:kk, :]
    for k in range(kk):
        spread_ref[k] = jnp.broadcast_to(step[:, k : k + 1], (kk, share))
    w_ref[...] = jnp.full((kk, share), 1.0 / kk, F32)

    def descend(_, carry):
        acc = [pull, None, None, None]
        for k in range(kk):
            term = spread_ref[k] * w_ref[k : k + 1, :]
            acc[k % 4] = term if acc[k % 4] is None else acc[k % 4] + term
        w_ref[...] = jnp.maximum((acc[0] + acc[1]) + (acc[2] + acc[3]), 0.0)
        return carry

    lax.fori_loop(0, ITERS, descend, 0)
    weights = w_ref[...]
    scores_ref[...] = kk * weights
    design = weights.astype(BF16)
    for peer in range(design_ref.shape[0]):
        design_ref[peer] = design


def descend(parts):
    shares, _, share = parts.shape
    return pl.pallas_call(
        descend_kernel,
        out_shape=(
            jax.ShapeDtypeStruct((K, share), F32),
            jax.ShapeDtypeStruct((shares, K, share), BF16),
        ),
        scratch_shapes=[pltpu.VMEM((K, K, share), F32), pltpu.VMEM((K, share), F32)],
        compiler_params=params(),
        cost_estimate=cost(2 * ITERS * K * K * share, 4 * K * share),
        name="descend",
    )(parts)


def cross_kernel(design_ref, methyl_ref, panel_ref, out_ref):
    blocks, kk, _ = design_ref.shape
    probes = methyl_ref.shape[1]
    design = jnp.concatenate([design_ref[b] for b in range(blocks)], axis=1)

    @pl.when(pl.program_id(0) == 0)
    def _():
        out_ref[...] = jnp.zeros_like(out_ref)

    out_ref[:, probes : probes + kk] += nt(design, design)
    width = min(probes, 512)
    for at in range(0, probes, width):
        cols = slice(at, at + width)
        out_ref[:, cols] += jnp.dot(design, methyl_ref[:, cols], preferred_element_type=F32)
        left = methyl_ref[:, cols].astype(F32) - tn(design, panel_ref[:, cols])
        squares = jnp.sum(left * left, axis=0, keepdims=True)
        for b in range(0, width, LANES):
            row = (at + b) // LANES
            out_ref[row : row + 1, probes + LANES :] += squares[:, b : b + LANES]


def cross_products(design, methyl, panel):
    _, _, share = design.shape
    rows, probes = methyl.shape
    chunk = row_chunk(share)
    return pl.pallas_call(
        cross_kernel,
        grid=(rows // chunk,),
        in_specs=[
            pl.BlockSpec((chunk // share, K, share), lambda i: (i, 0, 0)),
            pl.BlockSpec((chunk, probes), lambda i: (i, 0)),
            pl.BlockSpec((K, probes), lambda i: (0, 0)),
        ],
        out_specs=pl.BlockSpec((K, probes + 2 * LANES), lambda i: (0, 0)),
        out_shape=jax.ShapeDtypeStruct((K, probes + 2 * LANES), F32),
        compiler_params=params("arbitrary"),
        cost_estimate=cost(4 * K * rows * probes, 2 * rows * probes),
        name="cross",
    )(design, methyl, panel)


def ridge_inverse(matrix):
    kk = matrix.shape[0]
    row = lax.broadcasted_iota(jnp.int32, (kk, kk), 0)
    col = lax.broadcasted_iota(jnp.int32, (kk, kk), 1)
    work = jnp.concatenate([matrix, jnp.where(row == col, 1.0, 0.0)], axis=1)
    which = lax.broadcasted_iota(jnp.int32, (kk, 1), 0)
    for k in range(kk):
        pivot_row = work[k : k + 1, :] / work[k : k + 1, k : k + 1]
        factor = jnp.where(which == k, 0.0, work[:, k : k + 1])
        work = jnp.where(which == k, pivot_row, work - factor * pivot_row)
    return work[:, kk:]


def solve_kernel(ridge, samples, mine_ref, peer_ref, panel_ref, out_ref):
    kk, probes = panel_ref.shape
    total = mine_ref[...] + peer_ref[...]
    cross = total[:, :probes]
    wgram = total[:, probes : probes + kk]
    start = jnp.concatenate(
        [total[r : r + 1, probes + LANES :] for r in range(probes // LANES)], axis=1
    )
    row = lax.broadcasted_iota(jnp.int32, (kk, kk), 0)
    col = lax.broadcasted_iota(jnp.int32, (kk, kk), 1)
    system = wgram + jnp.where(row == col, ridge, 0.0)
    inverse = ridge_inverse(system)
    loadings = jnp.dot(inverse, cross, precision=HIGHEST)
    short = cross - jnp.dot(system, loadings, precision=HIGHEST)
    loadings = loadings + jnp.dot(inverse, short, precision=HIGHEST)
    panel = panel_ref[...].astype(F32)
    slope = jnp.dot(wgram, loadings + panel, precision=HIGHEST) - 2.0 * cross
    spread = start + jnp.sum((loadings - panel) * slope, axis=0, keepdims=True)
    rate = lax.rsqrt(jnp.maximum(spread, 0.0) / samples + 1e-06)
    out_ref[:kk, :] = loadings
    out_ref[kk:, :] = jnp.broadcast_to(rate, (out_ref.shape[0] - kk, probes))


def solve(mine, peer, panel, ridge, samples):
    probes = panel.shape[1]
    return pl.pallas_call(
        functools.partial(solve_kernel, ridge, samples),
        out_shape=jax.ShapeDtypeStruct((K + 8, probes), F32),
        compiler_params=params(),
        cost_estimate=cost(50 * K * K * probes, 20 * K * probes),
        name="solve",
    )(mine, peer, panel)


def standardise(design, methyl_ref, terms_ref, rate, store):
    probes = methyl_ref.shape[1]
    stacked = jnp.concatenate([design] * 3, axis=0)
    width = min(probes, 512)
    for at in range(0, probes, width):
        cols = slice(at, at + width)
        fitted = tn(stacked, terms_ref[:, cols])
        left = methyl_ref[:, cols].astype(F32) - fitted
        store(at, width, (left * rate[:, cols]).astype(BF16))


def own_kernel(
    steps, line, place_ref, core_ref, design_ref, mine_ref, theirs_ref, facts_ref, more_ref, *refs
):
    z_ref, swap_ref, keep_ref, half_ref, terms_ref, moreterms_ref = refs
    step = pl.program_id(0)
    blocks, kk, share = design_ref.shape
    chunk, probes = mine_ref.shape
    place, core = place_ref[0], core_ref[0]

    @pl.when(step == 0)
    def _():
        terms_ref[...] = three_terms(facts_ref[:kk, :])
        moreterms_ref[...] = three_terms(more_ref[:kk, :])

    @pl.when(step < steps)
    def _():
        design = jnp.concatenate([design_ref[b] for b in range(blocks)], axis=1)
        rows = pl.ds(pl.multiple_of(step * chunk, chunk), chunk)

        def store(base, at, width, value):
            z_ref[rows, base + at : base + at + width] = value

        standardise(design, mine_ref, terms_ref, facts_ref[kk : kk + 1, :], functools.partial(store, 0))
        standardise(
            design, theirs_ref, moreterms_ref, more_ref[kk : kk + 1, :], functools.partial(store, probes)
        )
        for b in range(blocks // 2):
            here = pl.ds(pl.multiple_of(step * chunk + (2 * b + core) * share, share), share)
            slot = jnp.bitwise_xor(step * (blocks // 2) + b, place)
            half_ref[pl.ds(pl.multiple_of(slot * share, share), share), :] = z_ref[here, :]

    @pl.when(step >= steps)
    def _():
        tall = keep_ref.shape[1]
        rows = pl.ds(pl.multiple_of((step - steps) * tall, tall), tall)
        part = nt(z_ref[rows, :], half_ref[...])
        for slot in range(0, line, 2):
            keep_ref[slot // 2] = part[:, slot * share : (slot + 1) * share]
            swap_ref[slot // 2] = part[:, (slot + 1) * share : (slot + 2) * share].astype(BF16)


def own_tile(at, line, design, mine, theirs, facts, more):
    _, _, share = design.shape
    rows, probes = mine.shape
    chunk = row_chunk(share)
    steps, tall = rows // chunk, 2 * chunk

    def first(i, *_):
        return (jnp.minimum(i, steps - 1), 0)

    def second(i, *_):
        return (jnp.maximum(i - steps, 0), 0)

    whole = pl.BlockSpec((K + 8, probes), lambda i, *_: (0, 0))
    return pl.pallas_call(
        functools.partial(own_kernel, steps, line),
        grid_spec=pltpu.PrefetchScalarGridSpec(
            num_scalar_prefetch=2,
            grid=(steps + rows // tall,),
            in_specs=[
                pl.BlockSpec((chunk // share, K, share), lambda i, *_: (*first(i), 0)),
                pl.BlockSpec((chunk, probes), first),
                pl.BlockSpec((chunk, probes), first),
                whole,
                whole,
            ],
            out_specs=[pl.BlockSpec(memory_space=pltpu.VMEM)]
            + [pl.BlockSpec((line // 2, tall, share), lambda i, *_: (0, *second(i)))] * 2,
            scratch_shapes=[
                pltpu.VMEM((rows // 2, 2 * probes), BF16),
                pltpu.VMEM((3 * K, probes), BF16),
                pltpu.VMEM((3 * K, probes), BF16),
            ],
        ),
        out_shape=[pltpu.VMEM((rows, 2 * probes), BF16)]
        + [jax.ShapeDtypeStruct((line // 2, rows, share), dtype) for dtype in (BF16, F32)],
        compiler_params=params("arbitrary"),
        cost_estimate=cost(2 * rows * rows * probes, 12 * rows * probes),
        name="own",
    )(*at, design, mine, theirs, facts, more)


def pair_kernel(index_of, line, first, sides, given, last, place_ref, design_ref, zscore_ref, *refs):
    facts, raws, refs = refs[:sides], refs[sides : 2 * sides], refs[2 * sides :]
    given_ref, refs = (refs[0], refs[1:]) if given else (None, refs)
    outs, (z_ref, *terms) = refs[: -1 - sides], refs[-1 - sides :]
    blocks, kk, share = design_ref.shape
    probes = facts[0].shape[1]
    tall = outs[0].shape[0]
    step, place = pl.program_id(0), place_ref[0]

    @pl.when(step == 0)
    def _():
        design = jnp.concatenate([design_ref[b] for b in range(blocks)], axis=1)
        for side in range(sides):
            terms[side][...] = three_terms(facts[side][:kk, :])

            def store(at, width, value):
                z_ref[:, side * probes + at : side * probes + at + width] = value

            standardise(design, raws[side], terms[side], facts[side][kk : kk + 1, :], store)

    @pl.when(step > 0)
    def _():
        rows = pl.ds(pl.multiple_of((step - 1) * tall, tall), tall)
        part = nt(zscore_ref[rows, first * probes : (first + sides) * probes], z_ref[...])
        if given:
            part = part + given_ref[rows, :]
        if not last:
            outs[0][...] = part
            return
        *sends, keep_ref = outs
        for j, ref in enumerate([keep_ref, *sends]):
            index, inside = index_of(lax.rem(place + j, line))
            block = part[:, :share]
            for b in range(1, blocks):
                block = jnp.where(index == b, part[:, b * share : (b + 1) * share], block)
            if j == 0:
                block = jnp.where(inside, block, 0.0)
            ref[...] = block.astype(ref.dtype)


def pair_tile(index_of, at, line, design, zscore, first, facts, raws, given=None, last=True):
    blocks, _, share = design.shape
    rows, depth = zscore.shape
    probes, sides = depth // 2, len(facts)
    tall = 2 * row_chunk(share)
    given = [] if given is None else [given]
    width = share if last else blocks * share
    column = pl.BlockSpec((tall, width), lambda i, *_: (jnp.maximum(i - 1, 0), 0))
    whole = jax.ShapeDtypeStruct((rows, width), F32)
    sends = [jax.ShapeDtypeStruct((rows, share), BF16)] * (line - 1)
    return pl.pallas_call(
        functools.partial(pair_kernel, index_of, line, first, sides, bool(given), last),
        grid_spec=pltpu.PrefetchScalarGridSpec(
            num_scalar_prefetch=1,
            grid=(1 + rows // tall,),
            in_specs=[pl.BlockSpec(memory_space=pltpu.VMEM)] * (2 + 2 * sides + len(given)),
            out_specs=[column] * line if last else [column],
            scratch_shapes=[pltpu.VMEM((blocks * share, sides * probes), BF16)]
            + [pltpu.VMEM((3 * K, probes), BF16)] * sides,
        ),
        out_shape=sends + [whole] if last else [whole],
        compiler_params=params("arbitrary"),
        cost_estimate=cost(2 * rows * blocks * share * sides * probes, 4 * rows * probes),
    )(at[0], design, zscore, *facts, *raws, *given)


def fold_kernel(line, place_ref, core_ref, *refs):
    (keep_ref, *parts), (total_ref, same_ref, other_ref) = refs[:-3], refs[-3:]
    place, core = place_ref[0], core_ref[0]
    share = same_ref.shape[1]
    total = keep_ref[...]
    for ref in parts:
        total = total + ref[...].astype(F32)
    total_ref[...] = total
    for j in range(line):
        block = 2 * lax.rem(place + j, line)
        same = pl.ds(pl.multiple_of((block + core) * share, share), share)
        other = pl.ds(pl.multiple_of((block + 1 - core) * share, share), share)
        same_ref[j] = total_ref[same, :].astype(BF16)
        other_ref[j] = total_ref[other, :].astype(BF16)


def fold(at, line, parts):
    rows, share = parts[0].shape
    blocks = jax.ShapeDtypeStruct((line, share, share), BF16)
    vmem = pl.BlockSpec(memory_space=pltpu.VMEM)
    return pl.pallas_call(
        functools.partial(fold_kernel, line),
        in_specs=[pl.BlockSpec(memory_space=pltpu.SMEM)] * 2 + [vmem] * len(parts),
        out_shape=(jax.ShapeDtypeStruct((rows, share), F32), blocks, blocks),
        compiler_params=params(),
        cost_estimate=cost(rows * share * 8, rows * share * 16),
        name="fold",
    )(*at, *parts)


def scale_kernel(probes, own_ref, *refs):
    parts, (left_ref, out_ref) = refs[:-2], refs[-2:]
    total = own_ref[...]
    for ref in parts:
        total = total + ref[...].astype(F32)
    out_ref[0] = total * (1.0 / probes)
    out_ref[1] = left_ref[...] * (1.0 / probes)


def scale(probes, keep, parts, left):
    rows, share = keep.shape
    vmem = pl.BlockSpec((rows, share), lambda i: (0, 0))
    return pl.pallas_call(
        functools.partial(scale_kernel, probes),
        grid=(1,),
        in_specs=[vmem] * (2 + len(parts)),
        out_specs=pl.BlockSpec((2, rows, share), lambda i: (0, 0, 0)),
        out_shape=jax.ShapeDtypeStruct((3, rows, share), F32),
        compiler_params=params("arbitrary"),
        cost_estimate=cost(rows * share * 16, rows * share * 30),
        name="scale",
    )(keep, *parts, left)


def finish_kernel(line, probes, place_ref, core_ref, _, same_ref, other_ref, *refs):
    shifted, out_ref = refs[:-1], refs[-1]
    place, core = place_ref[0], core_ref[0]
    share = same_ref.shape[1]
    for j in range(line):
        block = 2 * lax.rem(place - j + line, line)
        for side in range(2):
            piece = (same_ref, other_ref)[side][0] if j == 0 else shifted[j - 1][side]
            to = block + (core if side == 0 else 1 - core)
            rows = pl.ds(pl.multiple_of(to * share, share), share)
            out_ref[0, rows, :] = piece.astype(F32).T * (1.0 / probes)


def finish(at, line, probes, tiles, same, other, shifted):
    _, rows, share = tiles.shape
    first = pl.BlockSpec((1, share, share), lambda i: (0, 0, 0))
    pair = pl.BlockSpec((2, share, share), lambda i: (0, 0, 0))
    return pl.pallas_call(
        functools.partial(finish_kernel, line, probes),
        grid=(1,),
        in_specs=[pl.BlockSpec(memory_space=pltpu.SMEM)] * 2
        + [pl.BlockSpec(memory_space=pl.ANY), first, first]
        + [pair] * len(shifted),
        out_specs=pl.BlockSpec((1, rows, share), lambda i: (2, 0, 0)),
        out_shape=jax.ShapeDtypeStruct(tiles.shape, F32),
        input_output_aliases={2: 0},
        compiler_params=params("arbitrary"),
        cost_estimate=cost(rows * share * 4, rows * share * 8),
        name="finish",
    )(*at, tiles, same, other, *shifted)


def body(methyl, atlas, panel_ids):
    panels, shares = lax.axis_size("samp"), lax.axis_size("probe")
    rows = methyl.shape[0]
    samples = rows * panels
    probes = methyl.shape[1] * shares
    share = rows // shares
    line = shares // 2
    position = lax.axis_index("probe")
    place, core = position // 2, position % 2
    at = (place[None], core[None])

    def along(value, axis, pairs):
        return lax.ppermute(value, axis, pairs)

    def to_sibling(value):
        return along(value, "probe", [(i, i ^ 1) for i in range(shares)])

    def to_panel(value, by):
        return along(value, "samp", [(i, (i + by) % panels) for i in range(panels)])

    def to_panel_sibling(value, by):
        pairs = [
            (s * shares + i, ((s + by) % panels) * shares + (i ^ 1))
            for s in range(panels)
            for i in range(shares)
        ]
        return along(value, ("samp", "probe"), pairs)

    def swap_panels(value, bit):
        return along(value, "samp", [(i, i ^ bit) for i in range(panels)])

    def on_line(value, pairs):
        return along(value, "probe", [(2 * i + c, 2 * to + c) for i, to in pairs for c in (0, 1)])

    quarter = line // 4
    ends = [*range(quarter), *range(line - quarter, line)]
    inner = [*range(quarter, line - quarter)]

    def among_ends(to):
        high = to >= line - quarter
        return jnp.where(high, to - (line - 2 * quarter), to), (to < quarter) | high

    def among_inner(to):
        return to - quarter, (to >= quarter) & (to < line - quarter)

    ends_mine = to_panel(pick_ends(core[None], methyl, line, share), 1)
    theirs = to_sibling(methyl)
    parts, panel, outer, same, other = project(core[None], panel_ids, atlas, methyl, shares)
    ends_theirs = to_panel_sibling(outer, 1)
    parts = lax.all_to_all(parts, "probe", 0, 0)
    scores, copies = descend(parts)
    design = lax.all_to_all(copies, "probe", 0, 0)
    part = cross_products(design, methyl, panel)
    bit = panels // 2
    while bit > 1:
        part = part + swap_panels(part, bit)
        bit //= 2
    peer = swap_panels(part, 1)
    half = lax.dynamic_index_in_dim(design.reshape(line, 2, K, share), core, 1, False)
    design_before = to_panel(half, 1)
    inner_mine = to_panel(same, 1)
    inner_theirs = to_panel_sibling(other, 1)
    facts = solve(part, peer, panel, 0.0001 * samples, samples)
    more = to_sibling(facts)

    def round_of(by, among=None):
        pairs = [(i, (i + by) % line) for i in range(line)]
        return pairs if among is None else [(i, to) for i, to in pairs if to in among]

    def arrivals(sends, among):
        return [on_line(value, round_of(j, among)) for j, value in enumerate(sends, 1)]


    zscore, swap, keep = own_tile(at, line, design, methyl, theirs, facts, more)
    given = on_line(swap, [(i, i ^ 1) for i in range(line)])
    design_ends = jnp.concatenate([design_before[:quarter], design_before[line - quarter :]])
    *sends, pair_keep = pair_tile(
        among_ends, at, line, design_ends, zscore, 0, [facts, more],
        [ends_mine, ends_theirs],
    )
    pair_parts = [pair_keep] + arrivals(sends, ends)
    bit = 2
    while bit < line:
        swap = keep[1::2] + given[1::2].astype(F32)
        keep = keep[::2] + given[::2].astype(F32)
        given = on_line(swap.astype(BF16), [(i, i ^ bit) for i in range(line)])
        bit *= 2
    own_keep, own_parts = keep[0], [given[0]]
    design_inner = design_before[quarter : line - quarter]
    (partial,) = pair_tile(
        among_inner, at, line, design_inner, zscore, 0, [facts], [inner_mine],
        last=False,
    )
    *sends, pair_keep = pair_tile(
        among_inner, at, line, design_inner, zscore, 1, [more], [inner_theirs],
        given=partial,
    )
    pair_parts.append(pair_keep)
    pair_parts += arrivals(sends, inner)
    left, same, other = fold(at, line, pair_parts)
    same = to_panel(same, -1)
    other = to_panel_sibling(other, -1)
    shifted = [on_line(jnp.stack([same[j], other[j]]), round_of(j)) for j in range(1, line)]
    tiles = scale(probes, own_keep, own_parts, left)
    return finish(at, line, probes, tiles, same, other, shifted), scores


def solution(mesh):
    placed = (P("samp", "probe"), P(None, "probe"), P())
    return jax.shard_map(
        body,
        mesh=mesh,
        in_specs=placed,
        out_specs=(P(None, "samp", "probe"), P(None, ("samp", "probe"))),
        check_vma=False,
    )
```

```python
import functools

import jax
import jax.numpy as jnp
from jax import lax
from jax.experimental import pallas as pl
from jax.experimental.pallas import tpu as pltpu
from jax.sharding import PartitionSpec as P


K = 32
ITERS = 128
F32, BF16 = jnp.float32, jnp.bfloat16
HIGHEST = lax.Precision.HIGHEST
LANES = 128
VMEM_LIMIT = 40 * 1024 * 1024


def nt(a, b):
    return lax.dot_general(a, b, (((1,), (1,)), ((), ())), preferred_element_type=F32)


def tn(a, b):
    return lax.dot_general(a, b, (((0,), (0,)), ((), ())), preferred_element_type=F32)


def params(*semantics):
    return pltpu.CompilerParams(dimension_semantics=semantics, vmem_limit_bytes=VMEM_LIMIT)


def cost(flops, nbytes):
    return pl.CostEstimate(flops=int(flops), bytes_accessed=int(nbytes), transcendentals=0)


def three_terms(value):
    high = value.astype(BF16)
    rest = value - high.astype(F32)
    mid = rest.astype(BF16)
    low = (rest - mid.astype(F32)).astype(BF16)
    return jnp.concatenate([high, mid, low], axis=0)


def project_kernel(
    quarter, core_ref, ids_ref, atlas_ref, methyl_ref, out_ref, panel_ref, outer_ref, same_ref, other_ref,
    gram_ref,
):
    kk = panel_ref.shape[0]
    blocks, _, share = out_ref.shape
    core = core_ref[0]

    @pl.when(pl.program_id(0) == 0)
    def _():
        rows = atlas_ref.shape[0]
        row = lax.broadcasted_iota(jnp.int32, (kk, rows), 0)
        wanted = jnp.zeros((kk, rows), jnp.int32)
        for k in range(kk):
            wanted = jnp.where(row == k, ids_ref[k], wanted)
        pick = wanted == lax.broadcasted_iota(jnp.int32, (kk, rows), 1)
        chosen = jnp.where(pick, 1.0, 0.0).astype(BF16)
        panel = jnp.dot(chosen, atlas_ref[...], preferred_element_type=F32).astype(BF16)
        panel_ref[...] = panel
        gram_ref[...] = nt(panel, panel)

    proj = nt(methyl_ref[...], panel_ref[...]).T
    for b in range(blocks):
        out_ref[b, :kk, :] = proj[:, b * share : (b + 1) * share]
        out_ref[b, kk:, :] = jnp.zeros((kk, share), F32)
        out_ref[b, kk:, :kk] = gram_ref[...]

    def put(ref, side):
        for b in range(blocks // 2):
            start = pl.multiple_of((2 * b + side) * share, share)
            ref[b * share : (b + 1) * share, :] = methyl_ref[pl.ds(start, share), :]

    step, steps = pl.program_id(0), pl.num_programs(0)

    @pl.when((step < quarter) | (step >= steps - quarter))
    def _():
        put(outer_ref, 1 - core)

    @pl.when((step >= quarter) & (step < steps - quarter))
    def _():
        put(same_ref, core)
        put(other_ref, 1 - core)


def project(core, panel_ids, atlas, methyl, shares):
    rows, probes = methyl.shape
    share = rows // shares
    chunk = row_chunk(share)
    steps = rows // chunk
    quarter = steps // 4

    def outer(i):
        return (jnp.where(i < steps - quarter, jnp.minimum(i, quarter - 1), i - steps + 2 * quarter), 0)

    def inner(i):
        return (jnp.clip(i - quarter, 0, steps - 2 * quarter - 1), 0)

    def rows_of(count):
        return jax.ShapeDtypeStruct((count * chunk // 2, probes), BF16)

    return pl.pallas_call(
        functools.partial(project_kernel, quarter),
        grid=(steps,),
        in_specs=[
            pl.BlockSpec(memory_space=pltpu.SMEM),
            pl.BlockSpec(memory_space=pltpu.SMEM),
            pl.BlockSpec(atlas.shape, lambda i: (0, 0)),
            pl.BlockSpec((chunk, probes), lambda i: (i, 0)),
        ],
        out_specs=(
            pl.BlockSpec((chunk // share, 2 * K, share), lambda i: (i, 0, 0)),
            pl.BlockSpec((K, probes), lambda i: (0, 0)),
            pl.BlockSpec((chunk // 2, probes), outer),
            pl.BlockSpec((chunk // 2, probes), inner),
            pl.BlockSpec((chunk // 2, probes), inner),
        ),
        out_shape=(
            jax.ShapeDtypeStruct((shares, 2 * K, share), F32),
            jax.ShapeDtypeStruct((K, probes), BF16),
            rows_of(2 * quarter),
            rows_of(steps - 2 * quarter),
            rows_of(steps - 2 * quarter),
        ),
        scratch_shapes=[pltpu.VMEM((K, K), F32)],
        compiler_params=params("arbitrary"),
        cost_estimate=cost(2 * K * rows * probes, 4 * rows * probes),
        name="project",
    )(core, panel_ids, atlas, methyl)


def copy_kernel(_, from_ref, to_ref):
    to_ref[...] = from_ref[...]


def pick_ends(core, methyl, line, share):
    probes = methyl.shape[1]
    quarter = line // 4

    def block(i, core):
        return (2 * jnp.where(i < quarter, i, i + line - 2 * quarter) + core[0], 0)

    return pl.pallas_call(
        copy_kernel,
        grid_spec=pltpu.PrefetchScalarGridSpec(
            num_scalar_prefetch=1,
            grid=(2 * quarter,),
            in_specs=[pl.BlockSpec((share, probes), block)],
            out_specs=pl.BlockSpec((share, probes), lambda i, core: (i, 0)),
        ),
        out_shape=jax.ShapeDtypeStruct((2 * quarter * share, probes), BF16),
        compiler_params=params("arbitrary"),
        cost_estimate=cost(0, 8 * quarter * share * probes),
        name="pick_ends",
    )(core, methyl)


def row_chunk(share):
    return 2 * share * max(1, 128 // share)


def descend_kernel(parts_ref, scores_ref, design_ref, spread_ref, w_ref):
    kk, share = w_ref.shape
    total = parts_ref[0]
    for peer in range(1, parts_ref.shape[0]):
        total = total + parts_ref[peer]
    gram = total[kk:, :kk]
    row = lax.broadcasted_iota(jnp.int32, (kk, kk), 0)
    col = lax.broadcasted_iota(jnp.int32, (kk, kk), 1)
    trace = jnp.sum(jnp.where(row == col, gram, 0.0), axis=(0, 1), keepdims=True)
    rate = 1.0 / trace
    step = jnp.where(row == col, 1.0, 0.0) - rate * gram
    pull = rate * total[:kk, :]
    for k in range(kk):
        spread_ref[k] = jnp.broadcast_to(step[:, k : k + 1], (kk, share))
    w_ref[...] = jnp.full((kk, share), 1.0 / kk, F32)

    def descend(_, carry):
        acc = [pull, None, None, None]
        for k in range(kk):
            term = spread_ref[k] * w_ref[k : k + 1, :]
            acc[k % 4] = term if acc[k % 4] is None else acc[k % 4] + term
        w_ref[...] = jnp.maximum((acc[0] + acc[1]) + (acc[2] + acc[3]), 0.0)
        return carry

    lax.fori_loop(0, ITERS, descend, 0)
    weights = w_ref[...]
    scores_ref[...] = kk * weights
    design = weights.astype(BF16)
    for peer in range(design_ref.shape[0]):
        design_ref[peer] = design


def descend(parts):
    shares, _, share = parts.shape
    return pl.pallas_call(
        descend_kernel,
        out_shape=(
            jax.ShapeDtypeStruct((K, share), F32),
            jax.ShapeDtypeStruct((shares, K, share), BF16),
        ),
        scratch_shapes=[pltpu.VMEM((K, K, share), F32), pltpu.VMEM((K, share), F32)],
        compiler_params=params(),
        cost_estimate=cost(2 * ITERS * K * K * share, 4 * K * share),
        name="descend",
    )(parts)


def cross_kernel(design_ref, methyl_ref, panel_ref, out_ref):
    blocks, kk, _ = design_ref.shape
    probes = methyl_ref.shape[1]
    design = jnp.concatenate([design_ref[b] for b in range(blocks)], axis=1)

    @pl.when(pl.program_id(0) == 0)
    def _():
        out_ref[...] = jnp.zeros_like(out_ref)

    out_ref[:, probes : probes + kk] += nt(design, design)
    width = min(probes, 512)
    for at in range(0, probes, width):
        cols = slice(at, at + width)
        out_ref[:, cols] += jnp.dot(design, methyl_ref[:, cols], preferred_element_type=F32)
        left = methyl_ref[:, cols].astype(F32) - tn(design, panel_ref[:, cols])
        squares = jnp.sum(left * left, axis=0, keepdims=True)
        for b in range(0, width, LANES):
            row = (at + b) // LANES
            out_ref[row : row + 1, probes + LANES :] += squares[:, b : b + LANES]


def cross_products(design, methyl, panel):
    _, _, share = design.shape
    rows, probes = methyl.shape
    chunk = row_chunk(share)
    return pl.pallas_call(
        cross_kernel,
        grid=(rows // chunk,),
        in_specs=[
            pl.BlockSpec((chunk // share, K, share), lambda i: (i, 0, 0)),
            pl.BlockSpec((chunk, probes), lambda i: (i, 0)),
            pl.BlockSpec((K, probes), lambda i: (0, 0)),
        ],
        out_specs=pl.BlockSpec((K, probes + 2 * LANES), lambda i: (0, 0)),
        out_shape=jax.ShapeDtypeStruct((K, probes + 2 * LANES), F32),
        compiler_params=params("arbitrary"),
        cost_estimate=cost(4 * K * rows * probes, 2 * rows * probes),
        name="cross",
    )(design, methyl, panel)


def ridge_inverse(matrix):
    kk = matrix.shape[0]
    row = lax.broadcasted_iota(jnp.int32, (kk, kk), 0)
    col = lax.broadcasted_iota(jnp.int32, (kk, kk), 1)
    work = jnp.concatenate([matrix, jnp.where(row == col, 1.0, 0.0)], axis=1)
    which = lax.broadcasted_iota(jnp.int32, (kk, 1), 0)
    for k in range(kk):
        pivot_row = work[k : k + 1, :] / work[k : k + 1, k : k + 1]
        factor = jnp.where(which == k, 0.0, work[:, k : k + 1])
        work = jnp.where(which == k, pivot_row, work - factor * pivot_row)
    return work[:, kk:]


def solve_kernel(ridge, samples, mine_ref, peer_ref, panel_ref, out_ref):
    kk, probes = panel_ref.shape
    total = mine_ref[...] + peer_ref[...]
    cross = total[:, :probes]
    wgram = total[:, probes : probes + kk]
    start = jnp.concatenate(
        [total[r : r + 1, probes + LANES :] for r in range(probes // LANES)], axis=1
    )
    row = lax.broadcasted_iota(jnp.int32, (kk, kk), 0)
    col = lax.broadcasted_iota(jnp.int32, (kk, kk), 1)
    system = wgram + jnp.where(row == col, ridge, 0.0)
    inverse = ridge_inverse(system)
    loadings = jnp.dot(inverse, cross, precision=HIGHEST)
    short = cross - jnp.dot(system, loadings, precision=HIGHEST)
    loadings = loadings + jnp.dot(inverse, short, precision=HIGHEST)
    panel = panel_ref[...].astype(F32)
    slope = jnp.dot(wgram, loadings + panel, precision=HIGHEST) - 2.0 * cross
    spread = start + jnp.sum((loadings - panel) * slope, axis=0, keepdims=True)
    rate = lax.rsqrt(jnp.maximum(spread, 0.0) / samples + 1e-06)
    out_ref[:kk, :] = loadings
    out_ref[kk:, :] = jnp.broadcast_to(rate, (out_ref.shape[0] - kk, probes))


def solve(mine, peer, panel, ridge, samples):
    probes = panel.shape[1]
    return pl.pallas_call(
        functools.partial(solve_kernel, ridge, samples),
        out_shape=jax.ShapeDtypeStruct((K + 8, probes), F32),
        compiler_params=params(),
        cost_estimate=cost(50 * K * K * probes, 20 * K * probes),
        name="solve",
    )(mine, peer, panel)


def standardise(design, methyl_ref, terms_ref, rate, store):
    probes = methyl_ref.shape[1]
    stacked = jnp.concatenate([design] * 3, axis=0)
    width = min(probes, 512)
    for at in range(0, probes, width):
        cols = slice(at, at + width)
        fitted = tn(stacked, terms_ref[:, cols])
        left = methyl_ref[:, cols].astype(F32) - fitted
        store(at, width, (left * rate[:, cols]).astype(BF16))


def relayed(place, line):
    far = jnp.where(place <= 1, line - 1, 0)
    return jnp.where((place <= 1) | (place >= line - 2), lax.rem(far - place + line, line), 0)


def put_tile(part, own, sends, keep_ref):
    share = keep_ref.shape[1]
    keep = None
    for j, ref in enumerate(sends):
        block = part[:, j * share : (j + 1) * share]
        ref[...] = block.astype(BF16)
        mine = jnp.where(own == j, block, 0.0)
        keep = mine if keep is None else keep + mine
    keep_ref[...] = keep


def own_kernel(
    steps, line, place_ref, core_ref, design_ref, mine_ref, theirs_ref, facts_ref, more_ref, *refs
):
    (z_ref, *sends), (keep_ref, half_ref, terms_ref, moreterms_ref) = (
        refs[: line + 1],
        refs[line + 1 :],
    )
    step = pl.program_id(0)
    blocks, kk, share = design_ref.shape
    chunk, probes = mine_ref.shape
    place, core = place_ref[0], core_ref[0]

    @pl.when(step == 0)
    def _():
        terms_ref[...] = three_terms(facts_ref[:kk, :])
        moreterms_ref[...] = three_terms(more_ref[:kk, :])

    @pl.when(step < steps)
    def _():
        design = jnp.concatenate([design_ref[b] for b in range(blocks)], axis=1)
        rows = pl.ds(pl.multiple_of(step * chunk, chunk), chunk)

        def store(base, at, width, value):
            z_ref[rows, base + at : base + at + width] = value

        standardise(design, mine_ref, terms_ref, facts_ref[kk : kk + 1, :], functools.partial(store, 0))
        standardise(
            design, theirs_ref, moreterms_ref, more_ref[kk : kk + 1, :], functools.partial(store, probes)
        )
        for b in range(blocks // 2):
            here = pl.ds(pl.multiple_of(step * chunk + (2 * b + core) * share, share), share)
            away = lax.rem(step * (blocks // 2) + b - place + line, line)
            skipped = relayed(place, line)
            slot = jnp.where(away == 0, skipped, jnp.where(away == skipped, 0, away))
            half_ref[pl.ds(pl.multiple_of(slot * share, share), share), :] = z_ref[here, :]

    @pl.when(step >= steps)
    def _():
        tall = keep_ref.shape[0]
        rows = pl.ds(pl.multiple_of((step - steps) * tall, tall), tall)
        put_tile(nt(z_ref[rows, :], half_ref[...]), relayed(place, line), sends, keep_ref)


def own_tile(at, line, design, mine, theirs, facts, more):
    _, _, share = design.shape
    rows, probes = mine.shape
    chunk = row_chunk(share)
    steps, tall = rows // chunk, 2 * chunk

    def first(i, *_):
        return (jnp.minimum(i, steps - 1), 0)

    def second(i, *_):
        return (jnp.maximum(i - steps, 0), 0)

    whole = pl.BlockSpec((K + 8, probes), lambda i, *_: (0, 0))
    return pl.pallas_call(
        functools.partial(own_kernel, steps, line),
        grid_spec=pltpu.PrefetchScalarGridSpec(
            num_scalar_prefetch=2,
            grid=(steps + rows // tall,),
            in_specs=[
                pl.BlockSpec((chunk // share, K, share), lambda i, *_: (*first(i), 0)),
                pl.BlockSpec((chunk, probes), first),
                pl.BlockSpec((chunk, probes), first),
                whole,
                whole,
            ],
            out_specs=[pl.BlockSpec(memory_space=pltpu.VMEM)]
            + [pl.BlockSpec((tall, share), second)] * (line + 1),
            scratch_shapes=[
                pltpu.VMEM((rows // 2, 2 * probes), BF16),
                pltpu.VMEM((3 * K, probes), BF16),
                pltpu.VMEM((3 * K, probes), BF16),
            ],
        ),
        out_shape=[pltpu.VMEM((rows, 2 * probes), BF16)]
        + [jax.ShapeDtypeStruct((rows, share), BF16)] * line
        + [jax.ShapeDtypeStruct((rows, share), F32)],
        compiler_params=params("arbitrary"),
        cost_estimate=cost(2 * rows * rows * probes, 12 * rows * probes),
        name="own",
    )(*at, design, mine, theirs, facts, more)


def pair_kernel(index_of, line, first, sides, given, last, place_ref, design_ref, zscore_ref, *refs):
    facts, raws, refs = refs[:sides], refs[sides : 2 * sides], refs[2 * sides :]
    given_ref, refs = (refs[0], refs[1:]) if given else (None, refs)
    outs, (z_ref, *terms) = refs[: -1 - sides], refs[-1 - sides :]
    blocks, kk, share = design_ref.shape
    probes = facts[0].shape[1]
    tall = outs[0].shape[-2]
    step, place = pl.program_id(0), place_ref[0]

    @pl.when(step == 0)
    def _():
        design = jnp.concatenate([design_ref[b] for b in range(blocks)], axis=1)
        for side in range(sides):
            terms[side][...] = three_terms(facts[side][:kk, :])

            def store(at, width, value):
                z_ref[:, side * probes + at : side * probes + at + width] = value

            standardise(design, raws[side], terms[side], facts[side][kk : kk + 1, :], store)

    @pl.when(step > 0)
    def _():
        rows = pl.ds(pl.multiple_of((step - 1) * tall, tall), tall)
        part = nt(zscore_ref[rows, first * probes : (first + sides) * probes], z_ref[...])
        if given:
            part = part + given_ref[rows, :]
        if not last:
            outs[0][...] = part
            return
        if index_of is None:
            swap_ref, keep_ref = outs
            odd = lax.rem(place, 2) == 1
            for k in range(blocks // 2):
                low = part[:, 2 * k * share : (2 * k + 1) * share]
                high = part[:, (2 * k + 1) * share : (2 * k + 2) * share]
                swap_ref[k] = jnp.where(odd, low, high).astype(BF16)
                keep_ref[k] = jnp.where(odd, high, low)
            return
        *sends, keep_ref = outs
        for j, ref in enumerate([keep_ref, *sends]):
            index, inside = index_of(lax.rem(place + j, line))
            block = part[:, :share]
            for b in range(1, blocks):
                block = jnp.where(index == b, part[:, b * share : (b + 1) * share], block)
            if j == 0:
                block = jnp.where(inside, block, 0.0)
            ref[...] = block.astype(ref.dtype)


def pair_tile(index_of, at, line, design, zscore, first, facts, raws, given=None, last=True):
    blocks, _, share = design.shape
    rows, depth = zscore.shape
    probes, sides = depth // 2, len(facts)
    tall = 2 * row_chunk(share)
    given = [] if given is None else [given]
    width = share if last else blocks * share
    column = pl.BlockSpec((tall, width), lambda i, *_: (jnp.maximum(i - 1, 0), 0))
    whole = jax.ShapeDtypeStruct((rows, width), F32)
    sends = [jax.ShapeDtypeStruct((rows, share), BF16)] * (line - 1)
    out_specs = [column] * line if last else [column]
    out_shape = sends + [whole] if last else [whole]
    if last and index_of is None:
        halves = (blocks // 2, tall, share)
        out_specs = [pl.BlockSpec(halves, lambda i, *_: (0, jnp.maximum(i - 1, 0), 0))] * 2
        out_shape = [jax.ShapeDtypeStruct((blocks // 2, rows, share), t) for t in (BF16, F32)]
    return pl.pallas_call(
        functools.partial(pair_kernel, index_of, line, first, sides, bool(given), last),
        grid_spec=pltpu.PrefetchScalarGridSpec(
            num_scalar_prefetch=1,
            grid=(1 + rows // tall,),
            in_specs=[pl.BlockSpec(memory_space=pltpu.VMEM)] * (2 + 2 * sides + len(given)),
            out_specs=out_specs,
            scratch_shapes=[pltpu.VMEM((blocks * share, sides * probes), BF16)]
            + [pltpu.VMEM((3 * K, probes), BF16)] * sides,
        ),
        out_shape=out_shape,
        compiler_params=params("arbitrary"),
        cost_estimate=cost(2 * rows * blocks * share * sides * probes, 4 * rows * probes),
    )(at[0], design, zscore, *facts, *raws, *given)


def fold_kernel(line, place_ref, core_ref, *refs):
    (keep_ref, *parts), (total_ref, same_ref, other_ref) = refs[:-3], refs[-3:]
    place, core = place_ref[0], core_ref[0]
    share = same_ref.shape[1]
    total = keep_ref[...]
    for ref in parts:
        total = total + ref[...].astype(F32)
    total_ref[...] = total
    for j in range(line):
        block = 2 * lax.rem(place + j, line)
        same = pl.ds(pl.multiple_of((block + core) * share, share), share)
        other = pl.ds(pl.multiple_of((block + 1 - core) * share, share), share)
        same_ref[j] = total_ref[same, :].astype(BF16)
        other_ref[j] = total_ref[other, :].astype(BF16)


def fold(at, line, parts):
    rows, share = parts[0].shape
    blocks = jax.ShapeDtypeStruct((line, share, share), BF16)
    vmem = pl.BlockSpec(memory_space=pltpu.VMEM)
    return pl.pallas_call(
        functools.partial(fold_kernel, line),
        in_specs=[pl.BlockSpec(memory_space=pltpu.SMEM)] * 2 + [vmem] * len(parts),
        out_shape=(jax.ShapeDtypeStruct((rows, share), F32), blocks, blocks),
        compiler_params=params(),
        cost_estimate=cost(rows * share * 8, rows * share * 16),
        name="fold",
    )(*at, *parts)


def scale_kernel(probes, own_ref, *refs):
    parts, (left_ref, out_ref) = refs[:-2], refs[-2:]
    total = own_ref[...]
    for ref in parts:
        total = total + ref[...].astype(F32)
    out_ref[0] = total * (1.0 / probes)
    out_ref[1] = left_ref[...] * (1.0 / probes)


def scale(probes, keep, parts, left):
    rows, share = keep.shape
    vmem = pl.BlockSpec((rows, share), lambda i: (0, 0))
    return pl.pallas_call(
        functools.partial(scale_kernel, probes),
        grid=(1,),
        in_specs=[vmem] * (2 + len(parts)),
        out_specs=pl.BlockSpec((2, rows, share), lambda i: (0, 0, 0)),
        out_shape=jax.ShapeDtypeStruct((3, rows, share), F32),
        compiler_params=params("arbitrary"),
        cost_estimate=cost(rows * share * 16, rows * share * 30),
        name="scale",
    )(keep, *parts, left)


def finish_kernel(line, probes, place_ref, core_ref, _, same_ref, other_ref, *refs):
    shifted, out_ref = refs[:-1], refs[-1]
    place, core = place_ref[0], core_ref[0]
    share = same_ref.shape[1]
    for j in range(line):
        block = 2 * lax.rem(place - j + line, line)
        for side in range(2):
            piece = (same_ref, other_ref)[side][0] if j == 0 else shifted[j - 1][side]
            to = block + (core if side == 0 else 1 - core)
            rows = pl.ds(pl.multiple_of(to * share, share), share)
            out_ref[0, rows, :] = piece.astype(F32).T * (1.0 / probes)


def finish(at, line, probes, tiles, same, other, shifted):
    _, rows, share = tiles.shape
    first = pl.BlockSpec((1, share, share), lambda i: (0, 0, 0))
    pair = pl.BlockSpec((2, share, share), lambda i: (0, 0, 0))
    return pl.pallas_call(
        functools.partial(finish_kernel, line, probes),
        grid=(1,),
        in_specs=[pl.BlockSpec(memory_space=pltpu.SMEM)] * 2
        + [pl.BlockSpec(memory_space=pl.ANY), first, first]
        + [pair] * len(shifted),
        out_specs=pl.BlockSpec((1, rows, share), lambda i: (2, 0, 0)),
        out_shape=jax.ShapeDtypeStruct(tiles.shape, F32),
        input_output_aliases={2: 0},
        compiler_params=params("arbitrary"),
        cost_estimate=cost(rows * share * 4, rows * share * 8),
        name="finish",
    )(*at, tiles, same, other, *shifted)


def body(methyl, atlas, panel_ids):
    panels, shares = lax.axis_size("samp"), lax.axis_size("probe")
    rows = methyl.shape[0]
    samples = rows * panels
    probes = methyl.shape[1] * shares
    share = rows // shares
    line = shares // 2
    position = lax.axis_index("probe")
    place, core = position // 2, position % 2
    at = (place[None], core[None])

    def along(value, axis, pairs):
        return lax.ppermute(value, axis, pairs)

    def to_sibling(value):
        return along(value, "probe", [(i, i ^ 1) for i in range(shares)])

    def to_panel(value, by):
        return along(value, "samp", [(i, (i + by) % panels) for i in range(panels)])

    def to_panel_sibling(value, by):
        pairs = [
            (s * shares + i, ((s + by) % panels) * shares + (i ^ 1))
            for s in range(panels)
            for i in range(shares)
        ]
        return along(value, ("samp", "probe"), pairs)

    def swap_panels(value, bit):
        return along(value, "samp", [(i, i ^ bit) for i in range(panels)])

    def on_line(value, pairs):
        return along(value, "probe", [(2 * i + c, 2 * to + c) for i, to in pairs for c in (0, 1)])

    quarter = line // 4
    ends = [*range(quarter), *range(line - quarter, line)]
    inner = [*range(quarter, line - quarter)]

    def among_inner(to):
        return to - quarter, (to >= quarter) & (to < line - quarter)

    ends_mine = to_panel(pick_ends(core[None], methyl, line, share), 1)
    theirs = to_sibling(methyl)
    parts, panel, outer, same, other = project(core[None], panel_ids, atlas, methyl, shares)
    ends_theirs = to_panel_sibling(outer, 1)
    parts = lax.all_to_all(parts, "probe", 0, 0)
    scores, copies = descend(parts)
    design = lax.all_to_all(copies, "probe", 0, 0)
    part = cross_products(design, methyl, panel)
    bit = panels // 2
    while bit > 1:
        part = part + swap_panels(part, bit)
        bit //= 2
    peer = swap_panels(part, 1)
    half = lax.dynamic_index_in_dim(design.reshape(line, 2, K, share), core, 1, False)
    design_before = to_panel(half, 1)
    inner_mine = to_panel(same, 1)
    inner_theirs = to_panel_sibling(other, 1)
    facts = solve(part, peer, panel, 0.0001 * samples, samples)
    more = to_sibling(facts)

    def round_of(by, among=None):
        pairs = [(i, (i + by) % line) for i in range(line)]
        return pairs if among is None else [(i, to) for i, to in pairs if to in among]

    def arrivals(sends, among):
        return [on_line(value, round_of(j, among)) for j, value in enumerate(sends, 1)]

    def near_round(by):
        return [(i, to) for i, to in round_of(by) if line <= 3 or abs(to - i) < line - 1]

    zscore, *own_sends, own_keep = own_tile(at, line, design, methyl, theirs, facts, more)
    relay = on_line(own_sends[0], [(0, 1), (line - 1, line - 2)])
    late = sorted({2, line - 2})
    own_parts = [
        on_line(own_sends[j], near_round(j)) for j in range(1, line) if j not in late
    ]
    design_ends = jnp.concatenate([design_before[:quarter], design_before[line - quarter :]])
    swap, keep = pair_tile(
        None, at, line, design_ends, zscore, 0, [facts, more],
        [ends_mine, ends_theirs],
    )
    given = on_line(swap, [(i, i ^ 1) for i in range(line)])
    for j in late:
        passing = ((place == 1) & (j == line - 2)) | ((place == line - 2) & (j == 2))
        joined = (own_sends[0].astype(F32) + relay.astype(F32)).astype(BF16)
        own_parts.append(on_line(jnp.where(passing, joined, own_sends[j]), near_round(j)))
    design_inner = design_before[quarter : line - quarter]
    (partial,) = pair_tile(
        among_inner, at, line, design_inner, zscore, 0, [facts], [inner_mine],
        last=False,
    )
    keep = keep + given.astype(F32)

    def sum_for(to):
        if quarter == 1:
            return keep[0]
        which = jnp.where(to >= line - quarter, to - line + 2 * quarter, to) // 2
        return lax.dynamic_index_in_dim(keep, jnp.clip(which, 0, quarter - 1), 0, False)

    pair_parts = [jnp.where((place < quarter) | (place >= line - quarter), sum_for(place), 0.0)]
    for j in range(2, line, 2):
        pair_parts.append(on_line(sum_for((place + j) % line).astype(BF16), round_of(j, ends)))
    *sends, pair_keep = pair_tile(
        among_inner, at, line, design_inner, zscore, 1, [more], [inner_theirs],
        given=partial,
    )
    pair_parts += [pair_keep] + arrivals(sends, inner)
    left, same, other = fold(at, line, pair_parts)
    same = to_panel(same, -1)
    other = to_panel_sibling(other, -1)
    shifted = [on_line(jnp.stack([same[j], other[j]]), round_of(j)) for j in range(1, line)]
    tiles = scale(probes, own_keep, own_parts, left)
    return finish(at, line, probes, tiles, same, other, shifted), scores


def solution(mesh):
    placed = (P("samp", "probe"), P(None, "probe"), P())
    return jax.shard_map(
        body,
        mesh=mesh,
        in_specs=placed,
        out_specs=(P(None, "samp", "probe"), P(None, ("samp", "probe"))),
        check_vma=False,
    )
```

```python
import functools

import jax
import jax.numpy as jnp
from jax import lax
from jax.experimental import pallas as pl
from jax.experimental.pallas import tpu as pltpu
from jax.sharding import PartitionSpec as P


K = 32
ITERS = 128
F32, BF16 = jnp.float32, jnp.bfloat16
HIGHEST = lax.Precision.HIGHEST
LANES = 128
VMEM_LIMIT = 40 * 1024 * 1024


def nt(a, b):
    return lax.dot_general(a, b, (((1,), (1,)), ((), ())), preferred_element_type=F32)


def tn(a, b):
    return lax.dot_general(a, b, (((0,), (0,)), ((), ())), preferred_element_type=F32)


def params(*semantics):
    return pltpu.CompilerParams(dimension_semantics=semantics, vmem_limit_bytes=VMEM_LIMIT)


def cost(flops, nbytes):
    return pl.CostEstimate(flops=int(flops), bytes_accessed=int(nbytes), transcendentals=0)


def three_terms(value):
    high = value.astype(BF16)
    rest = value - high.astype(F32)
    mid = rest.astype(BF16)
    low = (rest - mid.astype(F32)).astype(BF16)
    return jnp.concatenate([high, mid, low], axis=0)


def project_kernel(
    quarter, core_ref, ids_ref, atlas_ref, methyl_ref, out_ref, panel_ref, outer_ref, same_ref, other_ref,
    gram_ref,
):
    kk = panel_ref.shape[0]
    blocks, _, share = out_ref.shape
    core = core_ref[0]

    @pl.when(pl.program_id(0) == 0)
    def _():
        rows = atlas_ref.shape[0]
        row = lax.broadcasted_iota(jnp.int32, (kk, rows), 0)
        wanted = jnp.zeros((kk, rows), jnp.int32)
        for k in range(kk):
            wanted = jnp.where(row == k, ids_ref[k], wanted)
        pick = wanted == lax.broadcasted_iota(jnp.int32, (kk, rows), 1)
        chosen = jnp.where(pick, 1.0, 0.0).astype(BF16)
        panel = jnp.dot(chosen, atlas_ref[...], preferred_element_type=F32).astype(BF16)
        panel_ref[...] = panel
        gram_ref[...] = nt(panel, panel)

    proj = nt(methyl_ref[...], panel_ref[...]).T
    for b in range(blocks):
        out_ref[b, :kk, :] = proj[:, b * share : (b + 1) * share]
        out_ref[b, kk:, :] = jnp.zeros((kk, share), F32)
        out_ref[b, kk:, :kk] = gram_ref[...]

    def put(ref, side):
        for b in range(blocks // 2):
            start = pl.multiple_of((2 * b + side) * share, share)
            ref[b * share : (b + 1) * share, :] = methyl_ref[pl.ds(start, share), :]

    step, steps = pl.program_id(0), pl.num_programs(0)

    @pl.when((step < quarter) | (step >= steps - quarter))
    def _():
        put(outer_ref, 1 - core)

    @pl.when((step >= quarter) & (step < steps - quarter))
    def _():
        put(same_ref, core)
        put(other_ref, 1 - core)


def project(core, panel_ids, atlas, methyl, shares):
    rows, probes = methyl.shape
    share = rows // shares
    chunk = row_chunk(share)
    steps = rows // chunk
    quarter = steps // 4

    def outer(i):
        return (jnp.where(i < steps - quarter, jnp.minimum(i, quarter - 1), i - steps + 2 * quarter), 0)

    def inner(i):
        return (jnp.clip(i - quarter, 0, steps - 2 * quarter - 1), 0)

    def rows_of(count):
        return jax.ShapeDtypeStruct((count * chunk // 2, probes), BF16)

    return pl.pallas_call(
        functools.partial(project_kernel, quarter),
        grid=(steps,),
        in_specs=[
            pl.BlockSpec(memory_space=pltpu.SMEM),
            pl.BlockSpec(memory_space=pltpu.SMEM),
            pl.BlockSpec(atlas.shape, lambda i: (0, 0)),
            pl.BlockSpec((chunk, probes), lambda i: (i, 0)),
        ],
        out_specs=(
            pl.BlockSpec((chunk // share, 2 * K, share), lambda i: (i, 0, 0)),
            pl.BlockSpec((K, probes), lambda i: (0, 0)),
            pl.BlockSpec((chunk // 2, probes), outer),
            pl.BlockSpec((chunk // 2, probes), inner),
            pl.BlockSpec((chunk // 2, probes), inner),
        ),
        out_shape=(
            jax.ShapeDtypeStruct((shares, 2 * K, share), F32),
            jax.ShapeDtypeStruct((K, probes), BF16),
            rows_of(2 * quarter),
            rows_of(steps - 2 * quarter),
            rows_of(steps - 2 * quarter),
        ),
        scratch_shapes=[pltpu.VMEM((K, K), F32)],
        compiler_params=params("arbitrary"),
        cost_estimate=cost(2 * K * rows * probes, 4 * rows * probes),
        name="project",
    )(core, panel_ids, atlas, methyl)


def copy_kernel(_, from_ref, to_ref):
    to_ref[...] = from_ref[...]


def pick_ends(core, methyl, line, share):
    probes = methyl.shape[1]
    quarter = line // 4

    def block(i, core):
        return (2 * jnp.where(i < quarter, i, i + line - 2 * quarter) + core[0], 0)

    return pl.pallas_call(
        copy_kernel,
        grid_spec=pltpu.PrefetchScalarGridSpec(
            num_scalar_prefetch=1,
            grid=(2 * quarter,),
            in_specs=[pl.BlockSpec((share, probes), block)],
            out_specs=pl.BlockSpec((share, probes), lambda i, core: (i, 0)),
        ),
        out_shape=jax.ShapeDtypeStruct((2 * quarter * share, probes), BF16),
        compiler_params=params("arbitrary"),
        cost_estimate=cost(0, 8 * quarter * share * probes),
        name="pick_ends",
    )(core, methyl)


def row_chunk(share):
    return 2 * share * max(1, 128 // share)


def descend_kernel(parts_ref, scores_ref, design_ref, spread_ref, w_ref):
    kk, share = w_ref.shape
    total = parts_ref[0]
    for peer in range(1, parts_ref.shape[0]):
        total = total + parts_ref[peer]
    gram = total[kk:, :kk]
    row = lax.broadcasted_iota(jnp.int32, (kk, kk), 0)
    col = lax.broadcasted_iota(jnp.int32, (kk, kk), 1)
    trace = jnp.sum(jnp.where(row == col, gram, 0.0), axis=(0, 1), keepdims=True)
    rate = 1.0 / trace
    step = jnp.where(row == col, 1.0, 0.0) - rate * gram
    pull = rate * total[:kk, :]
    for k in range(kk):
        spread_ref[k] = jnp.broadcast_to(step[:, k : k + 1], (kk, share))
    w_ref[...] = jnp.full((kk, share), 1.0 / kk, F32)

    def descend(_, carry):
        acc = [pull, None, None, None]
        for k in range(kk):
            term = spread_ref[k] * w_ref[k : k + 1, :]
            acc[k % 4] = term if acc[k % 4] is None else acc[k % 4] + term
        w_ref[...] = jnp.maximum((acc[0] + acc[1]) + (acc[2] + acc[3]), 0.0)
        return carry

    lax.fori_loop(0, ITERS, descend, 0)
    weights = w_ref[...]
    scores_ref[...] = kk * weights
    design = weights.astype(BF16)
    for peer in range(design_ref.shape[0]):
        design_ref[peer] = design


def descend(parts):
    shares, _, share = parts.shape
    return pl.pallas_call(
        descend_kernel,
        out_shape=(
            jax.ShapeDtypeStruct((K, share), F32),
            jax.ShapeDtypeStruct((shares, K, share), BF16),
        ),
        scratch_shapes=[pltpu.VMEM((K, K, share), F32), pltpu.VMEM((K, share), F32)],
        compiler_params=params(),
        cost_estimate=cost(2 * ITERS * K * K * share, 4 * K * share),
        name="descend",
    )(parts)


def cross_kernel(design_ref, methyl_ref, panel_ref, out_ref):
    blocks, kk, _ = design_ref.shape
    probes = methyl_ref.shape[1]
    design = jnp.concatenate([design_ref[b] for b in range(blocks)], axis=1)

    @pl.when(pl.program_id(0) == 0)
    def _():
        out_ref[...] = jnp.zeros_like(out_ref)

    out_ref[:, probes : probes + kk] += nt(design, design)
    width = min(probes, 512)
    for at in range(0, probes, width):
        cols = slice(at, at + width)
        out_ref[:, cols] += jnp.dot(design, methyl_ref[:, cols], preferred_element_type=F32)
        left = methyl_ref[:, cols].astype(F32) - tn(design, panel_ref[:, cols])
        squares = jnp.sum(left * left, axis=0, keepdims=True)
        for b in range(0, width, LANES):
            row = (at + b) // LANES
            out_ref[row : row + 1, probes + LANES :] += squares[:, b : b + LANES]


def cross_products(design, methyl, panel):
    _, _, share = design.shape
    rows, probes = methyl.shape
    chunk = row_chunk(share)
    return pl.pallas_call(
        cross_kernel,
        grid=(rows // chunk,),
        in_specs=[
            pl.BlockSpec((chunk // share, K, share), lambda i: (i, 0, 0)),
            pl.BlockSpec((chunk, probes), lambda i: (i, 0)),
            pl.BlockSpec((K, probes), lambda i: (0, 0)),
        ],
        out_specs=pl.BlockSpec((K, probes + 2 * LANES), lambda i: (0, 0)),
        out_shape=jax.ShapeDtypeStruct((K, probes + 2 * LANES), F32),
        compiler_params=params("arbitrary"),
        cost_estimate=cost(4 * K * rows * probes, 2 * rows * probes),
        name="cross",
    )(design, methyl, panel)


def ridge_inverse(matrix):
    kk = matrix.shape[0]
    row = lax.broadcasted_iota(jnp.int32, (kk, kk), 0)
    col = lax.broadcasted_iota(jnp.int32, (kk, kk), 1)
    work = jnp.concatenate([matrix, jnp.where(row == col, 1.0, 0.0)], axis=1)
    which = lax.broadcasted_iota(jnp.int32, (kk, 1), 0)
    for k in range(kk):
        pivot_row = work[k : k + 1, :] / work[k : k + 1, k : k + 1]
        factor = jnp.where(which == k, 0.0, work[:, k : k + 1])
        work = jnp.where(which == k, pivot_row, work - factor * pivot_row)
    return work[:, kk:]


def solve_kernel(ridge, samples, mine_ref, peer_ref, panel_ref, out_ref):
    kk, probes = panel_ref.shape
    total = mine_ref[...] + peer_ref[...]
    cross = total[:, :probes]
    wgram = total[:, probes : probes + kk]
    start = jnp.concatenate(
        [total[r : r + 1, probes + LANES :] for r in range(probes // LANES)], axis=1
    )
    row = lax.broadcasted_iota(jnp.int32, (kk, kk), 0)
    col = lax.broadcasted_iota(jnp.int32, (kk, kk), 1)
    system = wgram + jnp.where(row == col, ridge, 0.0)
    inverse = ridge_inverse(system)
    loadings = jnp.dot(inverse, cross, precision=HIGHEST)
    short = cross - jnp.dot(system, loadings, precision=HIGHEST)
    loadings = loadings + jnp.dot(inverse, short, precision=HIGHEST)
    panel = panel_ref[...].astype(F32)
    slope = jnp.dot(wgram, loadings + panel, precision=HIGHEST) - 2.0 * cross
    spread = start + jnp.sum((loadings - panel) * slope, axis=0, keepdims=True)
    rate = lax.rsqrt(jnp.maximum(spread, 0.0) / samples + 1e-06)
    out_ref[:kk, :] = loadings
    out_ref[kk:, :] = jnp.broadcast_to(rate, (out_ref.shape[0] - kk, probes))


def solve(mine, peer, panel, ridge, samples):
    probes = panel.shape[1]
    return pl.pallas_call(
        functools.partial(solve_kernel, ridge, samples),
        out_shape=jax.ShapeDtypeStruct((K + 8, probes), F32),
        compiler_params=params(),
        cost_estimate=cost(50 * K * K * probes, 20 * K * probes),
        name="solve",
    )(mine, peer, panel)


def standardise(design, methyl_ref, terms_ref, rate, store):
    probes = methyl_ref.shape[1]
    stacked = jnp.concatenate([design] * 3, axis=0)
    width = min(probes, 512)
    for at in range(0, probes, width):
        cols = slice(at, at + width)
        fitted = tn(stacked, terms_ref[:, cols])
        left = methyl_ref[:, cols].astype(F32) - fitted
        store(at, width, (left * rate[:, cols]).astype(BF16))


def put_tile(part, sends, keep_ref):
    share = keep_ref.shape[1]
    keep_ref[...] = part[:, :share]
    for j, ref in enumerate(sends, 1):
        ref[...] = part[:, j * share : (j + 1) * share].astype(BF16)


def own_kernel(
    steps, line, place_ref, core_ref, design_ref, mine_ref, theirs_ref, facts_ref, more_ref, *refs
):
    (z_ref, *sends), (keep_ref, half_ref, terms_ref, moreterms_ref) = refs[:line], refs[line:]
    step = pl.program_id(0)
    blocks, kk, share = design_ref.shape
    chunk, probes = mine_ref.shape
    place, core = place_ref[0], core_ref[0]

    @pl.when(step == 0)
    def _():
        terms_ref[...] = three_terms(facts_ref[:kk, :])
        moreterms_ref[...] = three_terms(more_ref[:kk, :])

    @pl.when(step < steps)
    def _():
        design = jnp.concatenate([design_ref[b] for b in range(blocks)], axis=1)
        rows = pl.ds(pl.multiple_of(step * chunk, chunk), chunk)

        def store(base, at, width, value):
            z_ref[rows, base + at : base + at + width] = value

        standardise(design, mine_ref, terms_ref, facts_ref[kk : kk + 1, :], functools.partial(store, 0))
        standardise(
            design, theirs_ref, moreterms_ref, more_ref[kk : kk + 1, :], functools.partial(store, probes)
        )
        for b in range(blocks // 2):
            here = pl.ds(pl.multiple_of(step * chunk + (2 * b + core) * share, share), share)
            slot = lax.rem(step * (blocks // 2) + b - place + line, line)
            half_ref[pl.ds(pl.multiple_of(slot * share, share), share), :] = z_ref[here, :]

    @pl.when(step >= steps)
    def _():
        tall = keep_ref.shape[0]
        rows = pl.ds(pl.multiple_of((step - steps) * tall, tall), tall)
        put_tile(nt(z_ref[rows, :], half_ref[...]), sends, keep_ref)


def own_tile(at, line, design, mine, theirs, facts, more):
    _, _, share = design.shape
    rows, probes = mine.shape
    chunk = row_chunk(share)
    steps, tall = rows // chunk, 2 * chunk

    def first(i, *_):
        return (jnp.minimum(i, steps - 1), 0)

    def second(i, *_):
        return (jnp.maximum(i - steps, 0), 0)

    whole = pl.BlockSpec((K + 8, probes), lambda i, *_: (0, 0))
    return pl.pallas_call(
        functools.partial(own_kernel, steps, line),
        grid_spec=pltpu.PrefetchScalarGridSpec(
            num_scalar_prefetch=2,
            grid=(steps + rows // tall,),
            in_specs=[
                pl.BlockSpec((chunk // share, K, share), lambda i, *_: (*first(i), 0)),
                pl.BlockSpec((chunk, probes), first),
                pl.BlockSpec((chunk, probes), first),
                whole,
                whole,
            ],
            out_specs=[pl.BlockSpec(memory_space=pltpu.VMEM)]
            + [pl.BlockSpec((tall, share), second)] * line,
            scratch_shapes=[
                pltpu.VMEM((rows // 2, 2 * probes), BF16),
                pltpu.VMEM((3 * K, probes), BF16),
                pltpu.VMEM((3 * K, probes), BF16),
            ],
        ),
        out_shape=[pltpu.VMEM((rows, 2 * probes), BF16)]
        + [jax.ShapeDtypeStruct((rows, share), BF16)] * (line - 1)
        + [jax.ShapeDtypeStruct((rows, share), F32)],
        compiler_params=params("arbitrary"),
        cost_estimate=cost(2 * rows * rows * probes, 12 * rows * probes),
        name="own",
    )(*at, design, mine, theirs, facts, more)


def pair_kernel(index_of, line, first, sides, given, last, place_ref, design_ref, zscore_ref, *refs):
    facts, raws, refs = refs[:sides], refs[sides : 2 * sides], refs[2 * sides :]
    given_ref, refs = (refs[0], refs[1:]) if given else (None, refs)
    outs, (z_ref, *terms) = refs[: -1 - sides], refs[-1 - sides :]
    blocks, kk, share = design_ref.shape
    probes = facts[0].shape[1]
    tall = outs[0].shape[0]
    step, place = pl.program_id(0), place_ref[0]

    @pl.when(step == 0)
    def _():
        design = jnp.concatenate([design_ref[b] for b in range(blocks)], axis=1)
        for side in range(sides):
            terms[side][...] = three_terms(facts[side][:kk, :])

            def store(at, width, value):
                z_ref[:, side * probes + at : side * probes + at + width] = value

            standardise(design, raws[side], terms[side], facts[side][kk : kk + 1, :], store)

    @pl.when(step > 0)
    def _():
        rows = pl.ds(pl.multiple_of((step - 1) * tall, tall), tall)
        part = nt(zscore_ref[rows, first * probes : (first + sides) * probes], z_ref[...])
        if given:
            part = part + given_ref[rows, :]
        if not last:
            outs[0][...] = part
            return
        *sends, keep_ref = outs
        for j, ref in enumerate([keep_ref, *sends]):
            index, inside = index_of(lax.rem(place + j, line))
            block = part[:, :share]
            for b in range(1, blocks):
                block = jnp.where(index == b, part[:, b * share : (b + 1) * share], block)
            if j == 0:
                block = jnp.where(inside, block, 0.0)
            ref[...] = block.astype(ref.dtype)


def pair_tile(index_of, at, line, design, zscore, first, facts, raws, given=None, last=True):
    blocks, _, share = design.shape
    rows, depth = zscore.shape
    probes, sides = depth // 2, len(facts)
    tall = 2 * row_chunk(share)
    given = [] if given is None else [given]
    width = share if last else blocks * share
    column = pl.BlockSpec((tall, width), lambda i, *_: (jnp.maximum(i - 1, 0), 0))
    whole = jax.ShapeDtypeStruct((rows, width), F32)
    sends = [jax.ShapeDtypeStruct((rows, share), BF16)] * (line - 1)
    return pl.pallas_call(
        functools.partial(pair_kernel, index_of, line, first, sides, bool(given), last),
        grid_spec=pltpu.PrefetchScalarGridSpec(
            num_scalar_prefetch=1,
            grid=(1 + rows // tall,),
            in_specs=[pl.BlockSpec(memory_space=pltpu.VMEM)] * (2 + 2 * sides + len(given)),
            out_specs=[column] * line if last else [column],
            scratch_shapes=[pltpu.VMEM((blocks * share, sides * probes), BF16)]
            + [pltpu.VMEM((3 * K, probes), BF16)] * sides,
        ),
        out_shape=sends + [whole] if last else [whole],
        compiler_params=params("arbitrary"),
        cost_estimate=cost(2 * rows * blocks * share * sides * probes, 4 * rows * probes),
    )(at[0], design, zscore, *facts, *raws, *given)


def fold_kernel(line, place_ref, core_ref, *refs):
    (keep_ref, *parts), (total_ref, same_ref, other_ref) = refs[:-3], refs[-3:]
    place, core = place_ref[0], core_ref[0]
    share = same_ref.shape[1]
    total = keep_ref[...]
    for ref in parts:
        total = total + ref[...].astype(F32)
    total_ref[...] = total
    for j in range(line):
        block = 2 * lax.rem(place + j, line)
        same = pl.ds(pl.multiple_of((block + core) * share, share), share)
        other = pl.ds(pl.multiple_of((block + 1 - core) * share, share), share)
        same_ref[j] = total_ref[same, :].astype(BF16)
        other_ref[j] = total_ref[other, :].astype(BF16)


def fold(at, line, parts):
    rows, share = parts[0].shape
    blocks = jax.ShapeDtypeStruct((line, share, share), BF16)
    vmem = pl.BlockSpec(memory_space=pltpu.VMEM)
    return pl.pallas_call(
        functools.partial(fold_kernel, line),
        in_specs=[pl.BlockSpec(memory_space=pltpu.SMEM)] * 2 + [vmem] * len(parts),
        out_shape=(jax.ShapeDtypeStruct((rows, share), F32), blocks, blocks),
        compiler_params=params(),
        cost_estimate=cost(rows * share * 8, rows * share * 16),
        name="fold",
    )(*at, *parts)


def scale_kernel(probes, own_ref, *refs):
    parts, (left_ref, out_ref) = refs[:-2], refs[-2:]
    total = own_ref[...]
    for ref in parts:
        total = total + ref[...].astype(F32)
    out_ref[0] = total * (1.0 / probes)
    out_ref[1] = left_ref[...] * (1.0 / probes)


def scale(probes, keep, parts, left):
    rows, share = keep.shape
    vmem = pl.BlockSpec((rows, share), lambda i: (0, 0))
    return pl.pallas_call(
        functools.partial(scale_kernel, probes),
        grid=(1,),
        in_specs=[vmem] * (2 + len(parts)),
        out_specs=pl.BlockSpec((2, rows, share), lambda i: (0, 0, 0)),
        out_shape=jax.ShapeDtypeStruct((3, rows, share), F32),
        compiler_params=params("arbitrary"),
        cost_estimate=cost(rows * share * 16, rows * share * 30),
        name="scale",
    )(keep, *parts, left)


def finish_kernel(line, probes, place_ref, core_ref, _, same_ref, other_ref, *refs):
    shifted, out_ref = refs[:-1], refs[-1]
    place, core = place_ref[0], core_ref[0]
    share = same_ref.shape[1]
    for j in range(line):
        block = 2 * lax.rem(place - j + line, line)
        for side in range(2):
            piece = (same_ref, other_ref)[side][0] if j == 0 else shifted[j - 1][side]
            to = block + (core if side == 0 else 1 - core)
            rows = pl.ds(pl.multiple_of(to * share, share), share)
            out_ref[0, rows, :] = piece.astype(F32).T * (1.0 / probes)


def finish(at, line, probes, tiles, same, other, shifted):
    _, rows, share = tiles.shape
    first = pl.BlockSpec((1, share, share), lambda i: (0, 0, 0))
    pair = pl.BlockSpec((2, share, share), lambda i: (0, 0, 0))
    return pl.pallas_call(
        functools.partial(finish_kernel, line, probes),
        grid=(1,),
        in_specs=[pl.BlockSpec(memory_space=pltpu.SMEM)] * 2
        + [pl.BlockSpec(memory_space=pl.ANY), first, first]
        + [pair] * len(shifted),
        out_specs=pl.BlockSpec((1, rows, share), lambda i: (2, 0, 0)),
        out_shape=jax.ShapeDtypeStruct(tiles.shape, F32),
        input_output_aliases={2: 0},
        compiler_params=params("arbitrary"),
        cost_estimate=cost(rows * share * 4, rows * share * 8),
        name="finish",
    )(*at, tiles, same, other, *shifted)


def body(methyl, atlas, panel_ids):
    panels, shares = lax.axis_size("samp"), lax.axis_size("probe")
    rows = methyl.shape[0]
    samples = rows * panels
    probes = methyl.shape[1] * shares
    share = rows // shares
    line = shares // 2
    position = lax.axis_index("probe")
    place, core = position // 2, position % 2
    at = (place[None], core[None])

    def along(value, axis, pairs):
        return lax.ppermute(value, axis, pairs)

    def to_sibling(value):
        return along(value, "probe", [(i, i ^ 1) for i in range(shares)])

    def to_panel(value, by):
        return along(value, "samp", [(i, (i + by) % panels) for i in range(panels)])

    def to_panel_sibling(value, by):
        pairs = [
            (s * shares + i, ((s + by) % panels) * shares + (i ^ 1))
            for s in range(panels)
            for i in range(shares)
        ]
        return along(value, ("samp", "probe"), pairs)

    def swap_panels(value, bit):
        return along(value, "samp", [(i, i ^ bit) for i in range(panels)])

    def on_line(value, pairs):
        return along(value, "probe", [(2 * i + c, 2 * to + c) for i, to in pairs for c in (0, 1)])

    quarter = line // 4
    ends = [*range(quarter), *range(line - quarter, line)]
    inner = [*range(quarter, line - quarter)]

    def among_ends(to):
        high = to >= line - quarter
        return jnp.where(high, to - (line - 2 * quarter), to), (to < quarter) | high

    def among_inner(to):
        return to - quarter, (to >= quarter) & (to < line - quarter)

    ends_mine = to_panel(pick_ends(core[None], methyl, line, share), 1)
    theirs = to_sibling(methyl)
    parts, panel, outer, same, other = project(core[None], panel_ids, atlas, methyl, shares)
    ends_theirs = to_panel_sibling(outer, 1)
    parts = lax.all_to_all(parts, "probe", 0, 0)
    scores, copies = descend(parts)
    design = lax.all_to_all(copies, "probe", 0, 0)
    part = cross_products(design, methyl, panel)
    bit = panels // 2
    while bit > 1:
        part = part + swap_panels(part, bit)
        bit //= 2
    peer = swap_panels(part, 1)
    half = lax.dynamic_index_in_dim(design.reshape(line, 2, K, share), core, 1, False)
    design_before = to_panel(half, 1)
    inner_mine = to_panel(same, 1)
    inner_theirs = to_panel_sibling(other, 1)
    facts = solve(part, peer, panel, 0.0001 * samples, samples)
    more = to_sibling(facts)

    def round_of(by, among=None):
        pairs = [(i, (i + by) % line) for i in range(line)]
        return pairs if among is None else [(i, to) for i, to in pairs if to in among]

    def arrivals(sends, among=None, rounds=None):
        return [
            on_line(value, round_of(j, among))
            for j, value in enumerate(sends, 1)
            if rounds is None or j in rounds
        ]

    early = {1, line - 1}
    late = set(range(1, line)) - early

    zscore, *own_sends, own_keep = own_tile(at, line, design, methyl, theirs, facts, more)
    own_parts = arrivals(own_sends, rounds=early)
    design_ends = jnp.concatenate([design_before[:quarter], design_before[line - quarter :]])
    *sends, keep = pair_tile(
        among_ends, at, line, design_ends, zscore, 0, [facts, more],
        [ends_mine, ends_theirs],
    )
    pair_parts = [keep] + arrivals(sends, ends)
    design_inner = design_before[quarter : line - quarter]
    (partial,) = pair_tile(
        among_inner, at, line, design_inner, zscore, 0, [facts], [inner_mine],
        last=False,
    )
    *sends, keep = pair_tile(
        among_inner, at, line, design_inner, zscore, 1, [more], [inner_theirs],
        given=partial,
    )
    pair_parts.append(keep)
    pair_parts += arrivals(sends, inner, late)
    pair_parts += arrivals(sends, inner, early)
    own_parts += arrivals(own_sends, rounds=late)
    left, same, other = fold(at, line, pair_parts)
    same = to_panel(same, -1)
    other = to_panel_sibling(other, -1)
    shifted = [on_line(jnp.stack([same[j], other[j]]), round_of(j)) for j in range(1, line)]
    tiles = scale(probes, own_keep, own_parts, left)
    return finish(at, line, probes, tiles, same, other, shifted), scores


def solution(mesh):
    placed = (P("samp", "probe"), P(None, "probe"), P())
    return jax.shard_map(
        body,
        mesh=mesh,
        in_specs=placed,
        out_specs=(P(None, "samp", "probe"), P(None, ("samp", "probe"))),
        check_vma=False,
    )
```

```python
import functools

import jax
import jax.numpy as jnp
from jax import lax
from jax.experimental import pallas as pl
from jax.experimental.pallas import tpu as pltpu
from jax.sharding import PartitionSpec as P


K = 32
ITERS = 128
F32, BF16 = jnp.float32, jnp.bfloat16
HIGHEST = lax.Precision.HIGHEST
LANES = 128
VMEM_LIMIT = 40 * 1024 * 1024


def nt(a, b):
    return lax.dot_general(a, b, (((1,), (1,)), ((), ())), preferred_element_type=F32)


def tn(a, b):
    return lax.dot_general(a, b, (((0,), (0,)), ((), ())), preferred_element_type=F32)


def params(*semantics):
    return pltpu.CompilerParams(dimension_semantics=semantics, vmem_limit_bytes=VMEM_LIMIT)


def cost(flops, nbytes):
    return pl.CostEstimate(flops=int(flops), bytes_accessed=int(nbytes), transcendentals=0)


def three_terms(value):
    high = value.astype(BF16)
    rest = value - high.astype(F32)
    mid = rest.astype(BF16)
    low = (rest - mid.astype(F32)).astype(BF16)
    return jnp.concatenate([high, mid, low], axis=0)


def project_kernel(
    quarter, core_ref, ids_ref, atlas_ref, methyl_ref, out_ref, panel_ref, outer_ref, same_ref, other_ref,
    gram_ref,
):
    kk = panel_ref.shape[0]
    blocks, _, share = out_ref.shape
    core = core_ref[0]

    @pl.when(pl.program_id(0) == 0)
    def _():
        rows = atlas_ref.shape[0]
        row = lax.broadcasted_iota(jnp.int32, (kk, rows), 0)
        wanted = jnp.zeros((kk, rows), jnp.int32)
        for k in range(kk):
            wanted = jnp.where(row == k, ids_ref[k], wanted)
        pick = wanted == lax.broadcasted_iota(jnp.int32, (kk, rows), 1)
        chosen = jnp.where(pick, 1.0, 0.0).astype(BF16)
        panel = jnp.dot(chosen, atlas_ref[...], preferred_element_type=F32).astype(BF16)
        panel_ref[...] = panel
        gram_ref[...] = nt(panel, panel)

    proj = nt(methyl_ref[...], panel_ref[...]).T
    for b in range(blocks):
        out_ref[b, :kk, :] = proj[:, b * share : (b + 1) * share]
        out_ref[b, kk:, :] = jnp.zeros((kk, share), F32)
        out_ref[b, kk:, :kk] = gram_ref[...]

    def put(ref, side):
        for b in range(blocks // 2):
            start = pl.multiple_of((2 * b + side) * share, share)
            ref[b * share : (b + 1) * share, :] = methyl_ref[pl.ds(start, share), :]

    step, steps = pl.program_id(0), pl.num_programs(0)

    @pl.when((step < quarter) | (step >= steps - quarter))
    def _():
        put(outer_ref, 1 - core)

    @pl.when((step >= quarter) & (step < steps - quarter))
    def _():
        put(same_ref, core)
        put(other_ref, 1 - core)


def project(core, panel_ids, atlas, methyl, shares):
    rows, probes = methyl.shape
    share = rows // shares
    chunk = row_chunk(share)
    steps = rows // chunk
    quarter = steps // 4

    def outer(i):
        return (jnp.where(i < steps - quarter, jnp.minimum(i, quarter - 1), i - steps + 2 * quarter), 0)

    def inner(i):
        return (jnp.clip(i - quarter, 0, steps - 2 * quarter - 1), 0)

    def rows_of(count):
        return jax.ShapeDtypeStruct((count * chunk // 2, probes), BF16)

    return pl.pallas_call(
        functools.partial(project_kernel, quarter),
        grid=(steps,),
        in_specs=[
            pl.BlockSpec(memory_space=pltpu.SMEM),
            pl.BlockSpec(memory_space=pltpu.SMEM),
            pl.BlockSpec(atlas.shape, lambda i: (0, 0)),
            pl.BlockSpec((chunk, probes), lambda i: (i, 0)),
        ],
        out_specs=(
            pl.BlockSpec((chunk // share, 2 * K, share), lambda i: (i, 0, 0)),
            pl.BlockSpec((K, probes), lambda i: (0, 0)),
            pl.BlockSpec((chunk // 2, probes), outer),
            pl.BlockSpec((chunk // 2, probes), inner),
            pl.BlockSpec((chunk // 2, probes), inner),
        ),
        out_shape=(
            jax.ShapeDtypeStruct((shares, 2 * K, share), F32),
            jax.ShapeDtypeStruct((K, probes), BF16),
            rows_of(2 * quarter),
            rows_of(steps - 2 * quarter),
            rows_of(steps - 2 * quarter),
        ),
        scratch_shapes=[pltpu.VMEM((K, K), F32)],
        compiler_params=params("arbitrary"),
        cost_estimate=cost(2 * K * rows * probes, 4 * rows * probes),
        name="project",
    )(core, panel_ids, atlas, methyl)


def copy_kernel(_, from_ref, to_ref):
    to_ref[...] = from_ref[...]


def pick_ends(core, methyl, line, share):
    probes = methyl.shape[1]
    quarter = line // 4

    def block(i, core):
        return (2 * jnp.where(i < quarter, i, i + line - 2 * quarter) + core[0], 0)

    return pl.pallas_call(
        copy_kernel,
        grid_spec=pltpu.PrefetchScalarGridSpec(
            num_scalar_prefetch=1,
            grid=(2 * quarter,),
            in_specs=[pl.BlockSpec((share, probes), block)],
            out_specs=pl.BlockSpec((share, probes), lambda i, core: (i, 0)),
        ),
        out_shape=jax.ShapeDtypeStruct((2 * quarter * share, probes), BF16),
        compiler_params=params("arbitrary"),
        cost_estimate=cost(0, 8 * quarter * share * probes),
        name="pick_ends",
    )(core, methyl)


def row_chunk(share):
    return 2 * share * max(1, 128 // share)


def descend_kernel(parts_ref, scores_ref, design_ref, spread_ref, w_ref):
    kk, share = w_ref.shape
    total = parts_ref[0]
    for peer in range(1, parts_ref.shape[0]):
        total = total + parts_ref[peer]
    gram = total[kk:, :kk]
    row = lax.broadcasted_iota(jnp.int32, (kk, kk), 0)
    col = lax.broadcasted_iota(jnp.int32, (kk, kk), 1)
    trace = jnp.sum(jnp.where(row == col, gram, 0.0), axis=(0, 1), keepdims=True)
    rate = 1.0 / trace
    step = jnp.where(row == col, 1.0, 0.0) - rate * gram
    pull = rate * total[:kk, :]
    for k in range(kk):
        spread_ref[k] = jnp.broadcast_to(step[:, k : k + 1], (kk, share))
    w_ref[...] = jnp.full((kk, share), 1.0 / kk, F32)

    def descend(_, carry):
        acc = [pull, None, None, None]
        for k in range(kk):
            term = spread_ref[k] * w_ref[k : k + 1, :]
            acc[k % 4] = term if acc[k % 4] is None else acc[k % 4] + term
        w_ref[...] = jnp.maximum((acc[0] + acc[1]) + (acc[2] + acc[3]), 0.0)
        return carry

    lax.fori_loop(0, ITERS, descend, 0)
    weights = w_ref[...]
    scores_ref[...] = kk * weights
    design = weights.astype(BF16)
    for peer in range(design_ref.shape[0]):
        design_ref[peer] = design


def descend(parts):
    shares, _, share = parts.shape
    return pl.pallas_call(
        descend_kernel,
        out_shape=(
            jax.ShapeDtypeStruct((K, share), F32),
            jax.ShapeDtypeStruct((shares, K, share), BF16),
        ),
        scratch_shapes=[pltpu.VMEM((K, K, share), F32), pltpu.VMEM((K, share), F32)],
        compiler_params=params(),
        cost_estimate=cost(2 * ITERS * K * K * share, 4 * K * share),
        name="descend",
    )(parts)


def cross_kernel(design_ref, methyl_ref, panel_ref, out_ref):
    blocks, kk, _ = design_ref.shape
    probes = methyl_ref.shape[1]
    design = jnp.concatenate([design_ref[b] for b in range(blocks)], axis=1)

    @pl.when(pl.program_id(0) == 0)
    def _():
        out_ref[...] = jnp.zeros_like(out_ref)

    out_ref[:, probes : probes + kk] += nt(design, design)
    width = min(probes, 512)
    for at in range(0, probes, width):
        cols = slice(at, at + width)
        out_ref[:, cols] += jnp.dot(design, methyl_ref[:, cols], preferred_element_type=F32)
        left = methyl_ref[:, cols].astype(F32) - tn(design, panel_ref[:, cols])
        squares = jnp.sum(left * left, axis=0, keepdims=True)
        for b in range(0, width, LANES):
            row = (at + b) // LANES
            out_ref[row : row + 1, probes + LANES :] += squares[:, b : b + LANES]


def cross_products(design, methyl, panel):
    _, _, share = design.shape
    rows, probes = methyl.shape
    chunk = row_chunk(share)
    return pl.pallas_call(
        cross_kernel,
        grid=(rows // chunk,),
        in_specs=[
            pl.BlockSpec((chunk // share, K, share), lambda i: (i, 0, 0)),
            pl.BlockSpec((chunk, probes), lambda i: (i, 0)),
            pl.BlockSpec((K, probes), lambda i: (0, 0)),
        ],
        out_specs=pl.BlockSpec((K, probes + 2 * LANES), lambda i: (0, 0)),
        out_shape=jax.ShapeDtypeStruct((K, probes + 2 * LANES), F32),
        compiler_params=params("arbitrary"),
        cost_estimate=cost(4 * K * rows * probes, 2 * rows * probes),
        name="cross",
    )(design, methyl, panel)


def ridge_inverse(matrix):
    kk = matrix.shape[0]
    row = lax.broadcasted_iota(jnp.int32, (kk, kk), 0)
    col = lax.broadcasted_iota(jnp.int32, (kk, kk), 1)
    work = jnp.concatenate([matrix, jnp.where(row == col, 1.0, 0.0)], axis=1)
    which = lax.broadcasted_iota(jnp.int32, (kk, 1), 0)
    for k in range(kk):
        pivot_row = work[k : k + 1, :] / work[k : k + 1, k : k + 1]
        factor = jnp.where(which == k, 0.0, work[:, k : k + 1])
        work = jnp.where(which == k, pivot_row, work - factor * pivot_row)
    return work[:, kk:]


def solve_kernel(ridge, samples, *refs):
    parts, panel_ref, out_ref = refs[:-2], refs[-2], refs[-1]
    kk, probes = panel_ref.shape
    total = parts[0][...]
    for ref in parts[1:]:
        total = total + ref[...]
    cross = total[:, :probes]
    wgram = total[:, probes : probes + kk]
    start = jnp.concatenate(
        [total[r : r + 1, probes + LANES :] for r in range(probes // LANES)], axis=1
    )
    row = lax.broadcasted_iota(jnp.int32, (kk, kk), 0)
    col = lax.broadcasted_iota(jnp.int32, (kk, kk), 1)
    system = wgram + jnp.where(row == col, ridge, 0.0)
    inverse = ridge_inverse(system)
    loadings = jnp.dot(inverse, cross, precision=HIGHEST)
    short = cross - jnp.dot(system, loadings, precision=HIGHEST)
    loadings = loadings + jnp.dot(inverse, short, precision=HIGHEST)
    panel = panel_ref[...].astype(F32)
    slope = jnp.dot(wgram, loadings + panel, precision=HIGHEST) - 2.0 * cross
    spread = start + jnp.sum((loadings - panel) * slope, axis=0, keepdims=True)
    rate = lax.rsqrt(jnp.maximum(spread, 0.0) / samples + 1e-06)
    out_ref[:kk, :] = loadings
    out_ref[kk:, :] = jnp.broadcast_to(rate, (out_ref.shape[0] - kk, probes))


def solve(parts, panel, ridge, samples):
    probes = panel.shape[1]
    return pl.pallas_call(
        functools.partial(solve_kernel, ridge, samples),
        out_shape=jax.ShapeDtypeStruct((K + 8, probes), F32),
        compiler_params=params(),
        cost_estimate=cost(50 * K * K * probes, 20 * K * probes),
        name="solve",
    )(*parts, panel)


def standardise(design, methyl_ref, terms_ref, rate, store):
    probes = methyl_ref.shape[1]
    stacked = jnp.concatenate([design] * 3, axis=0)
    width = min(probes, 512)
    for at in range(0, probes, width):
        cols = slice(at, at + width)
        fitted = tn(stacked, terms_ref[:, cols])
        left = methyl_ref[:, cols].astype(F32) - fitted
        store(at, width, (left * rate[:, cols]).astype(BF16))


def put_tile(part, sends, keep_ref):
    share = keep_ref.shape[1]
    keep_ref[...] = part[:, :share]
    for j, ref in enumerate(sends, 1):
        ref[...] = part[:, j * share : (j + 1) * share].astype(BF16)


def own_kernel(
    steps, line, place_ref, core_ref, design_ref, mine_ref, theirs_ref, facts_ref, more_ref, *refs
):
    (z_ref, *sends), (keep_ref, half_ref, terms_ref, moreterms_ref) = refs[:line], refs[line:]
    step = pl.program_id(0)
    blocks, kk, share = design_ref.shape
    chunk, probes = mine_ref.shape
    place, core = place_ref[0], core_ref[0]

    @pl.when(step == 0)
    def _():
        terms_ref[...] = three_terms(facts_ref[:kk, :])
        moreterms_ref[...] = three_terms(more_ref[:kk, :])

    @pl.when(step < steps)
    def _():
        design = jnp.concatenate([design_ref[b] for b in range(blocks)], axis=1)
        rows = pl.ds(pl.multiple_of(step * chunk, chunk), chunk)

        def store(base, at, width, value):
            z_ref[rows, base + at : base + at + width] = value

        standardise(design, mine_ref, terms_ref, facts_ref[kk : kk + 1, :], functools.partial(store, 0))
        standardise(
            design, theirs_ref, moreterms_ref, more_ref[kk : kk + 1, :], functools.partial(store, probes)
        )
        for b in range(blocks // 2):
            here = pl.ds(pl.multiple_of(step * chunk + (2 * b + core) * share, share), share)
            slot = lax.rem(step * (blocks // 2) + b - place + line, line)
            half_ref[pl.ds(pl.multiple_of(slot * share, share), share), :] = z_ref[here, :]

    @pl.when(step >= steps)
    def _():
        tall = keep_ref.shape[0]
        rows = pl.ds(pl.multiple_of((step - steps) * tall, tall), tall)
        put_tile(nt(z_ref[rows, :], half_ref[...]), sends, keep_ref)


def own_tile(at, line, design, mine, theirs, facts, more):
    _, _, share = design.shape
    rows, probes = mine.shape
    chunk = row_chunk(share)
    steps, tall = rows // chunk, 2 * chunk

    def first(i, *_):
        return (jnp.minimum(i, steps - 1), 0)

    def second(i, *_):
        return (jnp.maximum(i - steps, 0), 0)

    whole = pl.BlockSpec((K + 8, probes), lambda i, *_: (0, 0))
    return pl.pallas_call(
        functools.partial(own_kernel, steps, line),
        grid_spec=pltpu.PrefetchScalarGridSpec(
            num_scalar_prefetch=2,
            grid=(steps + rows // tall,),
            in_specs=[
                pl.BlockSpec((chunk // share, K, share), lambda i, *_: (*first(i), 0)),
                pl.BlockSpec((chunk, probes), first),
                pl.BlockSpec((chunk, probes), first),
                whole,
                whole,
            ],
            out_specs=[pl.BlockSpec(memory_space=pltpu.VMEM)]
            + [pl.BlockSpec((tall, share), second)] * line,
            scratch_shapes=[
                pltpu.VMEM((rows // 2, 2 * probes), BF16),
                pltpu.VMEM((3 * K, probes), BF16),
                pltpu.VMEM((3 * K, probes), BF16),
            ],
        ),
        out_shape=[pltpu.VMEM((rows, 2 * probes), BF16)]
        + [jax.ShapeDtypeStruct((rows, share), BF16)] * (line - 1)
        + [jax.ShapeDtypeStruct((rows, share), F32)],
        compiler_params=params("arbitrary"),
        cost_estimate=cost(2 * rows * rows * probes, 12 * rows * probes),
        name="own",
    )(*at, design, mine, theirs, facts, more)


def pair_kernel(index_of, line, first, sides, given, last, place_ref, design_ref, zscore_ref, *refs):
    facts, raws, refs = refs[:sides], refs[sides : 2 * sides], refs[2 * sides :]
    given_ref, refs = (refs[0], refs[1:]) if given else (None, refs)
    outs, (z_ref, *terms) = refs[: -1 - sides], refs[-1 - sides :]
    blocks, kk, share = design_ref.shape
    probes = facts[0].shape[1]
    tall = outs[0].shape[0]
    step, place = pl.program_id(0), place_ref[0]

    @pl.when(step == 0)
    def _():
        design = jnp.concatenate([design_ref[b] for b in range(blocks)], axis=1)
        for side in range(sides):
            terms[side][...] = three_terms(facts[side][:kk, :])

            def store(at, width, value):
                z_ref[:, side * probes + at : side * probes + at + width] = value

            standardise(design, raws[side], terms[side], facts[side][kk : kk + 1, :], store)

    @pl.when(step > 0)
    def _():
        rows = pl.ds(pl.multiple_of((step - 1) * tall, tall), tall)
        part = nt(zscore_ref[rows, first * probes : (first + sides) * probes], z_ref[...])
        if given:
            part = part + given_ref[rows, :]
        if not last:
            outs[0][...] = part
            return
        *sends, keep_ref = outs
        for j, ref in enumerate([keep_ref, *sends]):
            index, inside = index_of(lax.rem(place + j, line))
            block = part[:, :share]
            for b in range(1, blocks):
                block = jnp.where(index == b, part[:, b * share : (b + 1) * share], block)
            if j == 0:
                block = jnp.where(inside, block, 0.0)
            ref[...] = block.astype(ref.dtype)


def pair_tile(index_of, at, line, design, zscore, first, facts, raws, given=None, last=True):
    blocks, _, share = design.shape
    rows, depth = zscore.shape
    probes, sides = depth // 2, len(facts)
    tall = 2 * row_chunk(share)
    given = [] if given is None else [given]
    width = share if last else blocks * share
    column = pl.BlockSpec((tall, width), lambda i, *_: (jnp.maximum(i - 1, 0), 0))
    whole = jax.ShapeDtypeStruct((rows, width), F32)
    sends = [jax.ShapeDtypeStruct((rows, share), BF16)] * (line - 1)
    return pl.pallas_call(
        functools.partial(pair_kernel, index_of, line, first, sides, bool(given), last),
        grid_spec=pltpu.PrefetchScalarGridSpec(
            num_scalar_prefetch=1,
            grid=(1 + rows // tall,),
            in_specs=[pl.BlockSpec(memory_space=pltpu.VMEM)] * (2 + 2 * sides + len(given)),
            out_specs=[column] * line if last else [column],
            scratch_shapes=[pltpu.VMEM((blocks * share, sides * probes), BF16)]
            + [pltpu.VMEM((3 * K, probes), BF16)] * sides,
        ),
        out_shape=sends + [whole] if last else [whole],
        compiler_params=params("arbitrary"),
        cost_estimate=cost(2 * rows * blocks * share * sides * probes, 4 * rows * probes),
    )(at[0], design, zscore, *facts, *raws, *given)


def fold_kernel(line, place_ref, core_ref, *refs):
    (keep_ref, *parts), (total_ref, same_ref, other_ref) = refs[:-3], refs[-3:]
    place, core = place_ref[0], core_ref[0]
    share = same_ref.shape[1]
    total = keep_ref[...]
    for ref in parts:
        total = total + ref[...].astype(F32)
    total_ref[...] = total
    for j in range(line):
        block = 2 * lax.rem(place + j, line)
        same = pl.ds(pl.multiple_of((block + core) * share, share), share)
        other = pl.ds(pl.multiple_of((block + 1 - core) * share, share), share)
        same_ref[j] = total_ref[same, :].astype(BF16)
        other_ref[j] = total_ref[other, :].astype(BF16)


def fold(at, line, parts):
    rows, share = parts[0].shape
    blocks = jax.ShapeDtypeStruct((line, share, share), BF16)
    vmem = pl.BlockSpec(memory_space=pltpu.VMEM)
    return pl.pallas_call(
        functools.partial(fold_kernel, line),
        in_specs=[pl.BlockSpec(memory_space=pltpu.SMEM)] * 2 + [vmem] * len(parts),
        out_shape=(jax.ShapeDtypeStruct((rows, share), F32), blocks, blocks),
        compiler_params=params(),
        cost_estimate=cost(rows * share * 8, rows * share * 16),
        name="fold",
    )(*at, *parts)


def scale_kernel(probes, wholes, own_ref, *refs):
    parts, halves, (left_ref, out_ref) = refs[:wholes], refs[wholes:-2], refs[-2:]
    total = own_ref[...]
    for ref in parts:
        total = total + ref[...].astype(F32)
    for top, bottom in zip(halves[: len(halves) // 2], halves[len(halves) // 2 :]):
        total = total + jnp.concatenate([top[...], bottom[...]], axis=0).astype(F32)
    out_ref[0] = total * (1.0 / probes)
    out_ref[1] = left_ref[...] * (1.0 / probes)


def scale(probes, keep, parts, tops, bottoms, left):
    rows, share = keep.shape
    whole = pl.BlockSpec((rows, share), lambda i: (0, 0))
    half = pl.BlockSpec((rows // 2, share), lambda i: (0, 0))
    return pl.pallas_call(
        functools.partial(scale_kernel, probes, len(parts)),
        grid=(1,),
        in_specs=[whole] * (1 + len(parts)) + [half] * (2 * len(tops)) + [whole],
        out_specs=pl.BlockSpec((2, rows, share), lambda i: (0, 0, 0)),
        out_shape=jax.ShapeDtypeStruct((3, rows, share), F32),
        compiler_params=params("arbitrary"),
        cost_estimate=cost(rows * share * 16, rows * share * 30),
        name="scale",
    )(keep, *parts, *tops, *bottoms, left)


def finish_kernel(line, probes, place_ref, core_ref, _, same_ref, other_ref, *refs):
    shifted, out_ref = refs[:-1], refs[-1]
    place, core = place_ref[0], core_ref[0]
    share = same_ref.shape[1]
    for j in range(line):
        block = 2 * lax.rem(place - j + line, line)
        for side in range(2):
            piece = (same_ref, other_ref)[side][0] if j == 0 else shifted[j - 1][side]
            to = block + (core if side == 0 else 1 - core)
            rows = pl.ds(pl.multiple_of(to * share, share), share)
            out_ref[0, rows, :] = piece.astype(F32).T * (1.0 / probes)


def finish(at, line, probes, tiles, same, other, shifted):
    _, rows, share = tiles.shape
    first = pl.BlockSpec((1, share, share), lambda i: (0, 0, 0))
    pair = pl.BlockSpec((2, share, share), lambda i: (0, 0, 0))
    return pl.pallas_call(
        functools.partial(finish_kernel, line, probes),
        grid=(1,),
        in_specs=[pl.BlockSpec(memory_space=pltpu.SMEM)] * 2
        + [pl.BlockSpec(memory_space=pl.ANY), first, first]
        + [pair] * len(shifted),
        out_specs=pl.BlockSpec((1, rows, share), lambda i: (2, 0, 0)),
        out_shape=jax.ShapeDtypeStruct(tiles.shape, F32),
        input_output_aliases={2: 0},
        compiler_params=params("arbitrary"),
        cost_estimate=cost(rows * share * 4, rows * share * 8),
        name="finish",
    )(*at, tiles, same, other, *shifted)


def body(methyl, atlas, panel_ids):
    panels, shares = lax.axis_size("samp"), lax.axis_size("probe")
    rows = methyl.shape[0]
    samples = rows * panels
    probes = methyl.shape[1] * shares
    share = rows // shares
    line = shares // 2
    position = lax.axis_index("probe")
    place, core = position // 2, position % 2
    at = (place[None], core[None])

    def along(value, axis, pairs):
        return lax.ppermute(value, axis, pairs)

    def to_sibling(value):
        return along(value, "probe", [(i, i ^ 1) for i in range(shares)])

    def to_panel(value, by):
        return along(value, "samp", [(i, (i + by) % panels) for i in range(panels)])

    def to_panel_sibling(value, by):
        pairs = [
            (s * shares + i, ((s + by) % panels) * shares + (i ^ 1))
            for s in range(panels)
            for i in range(shares)
        ]
        return along(value, ("samp", "probe"), pairs)

    def swap_panels(value, bit):
        return along(value, "samp", [(i, i ^ bit) for i in range(panels)])

    def on_line(value, pairs):
        return along(value, "probe", [(2 * i + c, 2 * to + c) for i, to in pairs for c in (0, 1)])

    quarter = line // 4
    ends = [*range(quarter), *range(line - quarter, line)]
    inner = [*range(quarter, line - quarter)]

    def among_ends(to):
        high = to >= line - quarter
        return jnp.where(high, to - (line - 2 * quarter), to), (to < quarter) | high

    def among_inner(to):
        return to - quarter, (to >= quarter) & (to < line - quarter)

    ends_mine = to_panel(pick_ends(core[None], methyl, line, share), 1)
    theirs = to_sibling(methyl)
    parts, panel, outer, same, other = project(core[None], panel_ids, atlas, methyl, shares)
    ends_theirs = to_panel_sibling(outer, 1)
    parts = lax.all_to_all(parts, "probe", 0, 0)
    scores, copies = descend(parts)
    design = lax.all_to_all(copies, "probe", 0, 0)
    part = cross_products(design, methyl, panel)
    peers = [swap_panels(part, mask) for mask in range(1, panels)]
    half = lax.dynamic_index_in_dim(design.reshape(line, 2, K, share), core, 1, False)
    design_before = to_panel(half, 1)
    inner_mine = to_panel(same, 1)
    inner_theirs = to_panel_sibling(other, 1)
    facts = solve([part, *peers], panel, 0.0001 * samples, samples)
    more = to_sibling(facts)

    def round_of(by, among=None):
        pairs = [(i, (i + by) % line) for i in range(line)]
        return pairs if among is None else [(i, to) for i, to in pairs if to in among]

    def arrivals(sends, among=None, rounds=None):
        return [
            on_line(value, round_of(j, among))
            for j, value in enumerate(sends, 1)
            if rounds is None or j in rounds
        ]

    zscore, *own_sends, own_keep = own_tile(at, line, design, methyl, theirs, facts, more)
    early = {1, line - 1}
    late = set(range(1, line)) - early
    own_parts = arrivals(own_sends, rounds=early)
    tops = arrivals([value[: rows // 2] for value in own_sends], rounds=late)
    design_ends = jnp.concatenate([design_before[:quarter], design_before[line - quarter :]])
    *sends, keep = pair_tile(
        among_ends, at, line, design_ends, zscore, 0, [facts, more],
        [ends_mine, ends_theirs],
    )
    pair_parts = [keep] + arrivals(sends, ends)
    design_inner = design_before[quarter : line - quarter]
    (partial,) = pair_tile(
        among_inner, at, line, design_inner, zscore, 0, [facts], [inner_mine],
        last=False,
    )
    *sends, keep = pair_tile(
        among_inner, at, line, design_inner, zscore, 1, [more], [inner_theirs],
        given=partial,
    )
    pair_parts.append(keep)
    pair_parts += arrivals(sends, inner, late)
    pair_parts += arrivals(sends, inner, early)
    bottoms = arrivals([value[rows // 2 :] for value in own_sends], rounds=late)
    left, same, other = fold(at, line, pair_parts)
    same = to_panel(same, -1)
    other = to_panel_sibling(other, -1)
    shifted = [on_line(jnp.stack([same[j], other[j]]), round_of(j)) for j in range(1, line)]
    tiles = scale(probes, own_keep, own_parts, tops, bottoms, left)
    return finish(at, line, probes, tiles, same, other, shifted), scores


def solution(mesh):
    placed = (P("samp", "probe"), P(None, "probe"), P())
    return jax.shard_map(
        body,
        mesh=mesh,
        in_specs=placed,
        out_specs=(P(None, "samp", "probe"), P(None, ("samp", "probe"))),
        check_vma=False,
    )
```

```python
import functools

import jax
import jax.numpy as jnp
from jax import lax
from jax.experimental import pallas as pl
from jax.experimental.pallas import tpu as pltpu
from jax.sharding import PartitionSpec as P


K = 32
ITERS = 128
F32, BF16 = jnp.float32, jnp.bfloat16
HIGHEST = lax.Precision.HIGHEST
LANES = 128
HALF = LANES // 2
VMEM_LIMIT = 40 * 1024 * 1024


def nt(a, b):
    return lax.dot_general(a, b, (((1,), (1,)), ((), ())), preferred_element_type=F32)


def tn(a, b):
    return lax.dot_general(a, b, (((0,), (0,)), ((), ())), preferred_element_type=F32)


def params(*semantics):
    return pltpu.CompilerParams(dimension_semantics=semantics, vmem_limit_bytes=VMEM_LIMIT)


def cost(flops, nbytes):
    return pl.CostEstimate(flops=int(flops), bytes_accessed=int(nbytes), transcendentals=0)


def three_terms(value):
    high = value.astype(BF16)
    rest = value - high.astype(F32)
    mid = rest.astype(BF16)
    low = (rest - mid.astype(F32)).astype(BF16)
    return jnp.concatenate([high, mid, low], axis=0)


def project_kernel(
    quarter, core_ref, ids_ref, atlas_ref, methyl_ref, out_ref, panel_ref, outer_ref, same_ref, other_ref,
    gram_ref,
):
    kk = panel_ref.shape[0]
    blocks, _, share = out_ref.shape
    core = core_ref[0]

    @pl.when(pl.program_id(0) == 0)
    def _():
        rows = atlas_ref.shape[0]
        row = lax.broadcasted_iota(jnp.int32, (kk, rows), 0)
        wanted = jnp.zeros((kk, rows), jnp.int32)
        for k in range(kk):
            wanted = jnp.where(row == k, ids_ref[k], wanted)
        pick = wanted == lax.broadcasted_iota(jnp.int32, (kk, rows), 1)
        chosen = jnp.where(pick, 1.0, 0.0).astype(BF16)
        panel = jnp.dot(chosen, atlas_ref[...], preferred_element_type=F32).astype(BF16)
        panel_ref[...] = panel
        gram_ref[...] = nt(panel, panel)

    proj = nt(methyl_ref[...], panel_ref[...]).T
    for b in range(blocks):
        out_ref[b, :kk, :] = proj[:, b * share : (b + 1) * share]
        out_ref[b, kk:, :] = jnp.zeros((kk, share), F32)
        out_ref[b, kk:, :kk] = gram_ref[...]

    def put(ref, side):
        for b in range(blocks // 2):
            start = pl.multiple_of((2 * b + side) * share, share)
            ref[b * share : (b + 1) * share, :] = methyl_ref[pl.ds(start, share), :]

    step, steps = pl.program_id(0), pl.num_programs(0)

    @pl.when((step < quarter) | (step >= steps - quarter))
    def _():
        put(outer_ref, 1 - core)

    @pl.when((step >= quarter) & (step < steps - quarter))
    def _():
        put(same_ref, core)
        put(other_ref, 1 - core)


def project(core, panel_ids, atlas, methyl, shares):
    rows, probes = methyl.shape
    share = rows // shares
    chunk = row_chunk(share)
    steps = rows // chunk
    quarter = steps // 4

    def outer(i):
        return (jnp.where(i < steps - quarter, jnp.minimum(i, quarter - 1), i - steps + 2 * quarter), 0)

    def inner(i):
        return (jnp.clip(i - quarter, 0, steps - 2 * quarter - 1), 0)

    def rows_of(count):
        return jax.ShapeDtypeStruct((count * chunk // 2, probes), BF16)

    return pl.pallas_call(
        functools.partial(project_kernel, quarter),
        grid=(steps,),
        in_specs=[
            pl.BlockSpec(memory_space=pltpu.SMEM),
            pl.BlockSpec(memory_space=pltpu.SMEM),
            pl.BlockSpec(atlas.shape, lambda i: (0, 0)),
            pl.BlockSpec((chunk, probes), lambda i: (i, 0)),
        ],
        out_specs=(
            pl.BlockSpec((chunk // share, 2 * K, share), lambda i: (i, 0, 0)),
            pl.BlockSpec((K, probes), lambda i: (0, 0)),
            pl.BlockSpec((chunk // 2, probes), outer),
            pl.BlockSpec((chunk // 2, probes), inner),
            pl.BlockSpec((chunk // 2, probes), inner),
        ),
        out_shape=(
            jax.ShapeDtypeStruct((shares, 2 * K, share), F32),
            jax.ShapeDtypeStruct((K, probes), BF16),
            rows_of(2 * quarter),
            rows_of(steps - 2 * quarter),
            rows_of(steps - 2 * quarter),
        ),
        scratch_shapes=[pltpu.VMEM((K, K), F32)],
        compiler_params=params("arbitrary"),
        cost_estimate=cost(2 * K * rows * probes, 4 * rows * probes),
        name="project",
    )(core, panel_ids, atlas, methyl)


def copy_kernel(_, from_ref, to_ref):
    to_ref[...] = from_ref[...]


def pick_ends(core, methyl, line, share):
    probes = methyl.shape[1]
    quarter = line // 4

    def block(i, core):
        return (2 * jnp.where(i < quarter, i, i + line - 2 * quarter) + core[0], 0)

    return pl.pallas_call(
        copy_kernel,
        grid_spec=pltpu.PrefetchScalarGridSpec(
            num_scalar_prefetch=1,
            grid=(2 * quarter,),
            in_specs=[pl.BlockSpec((share, probes), block)],
            out_specs=pl.BlockSpec((share, probes), lambda i, core: (i, 0)),
        ),
        out_shape=jax.ShapeDtypeStruct((2 * quarter * share, probes), BF16),
        compiler_params=params("arbitrary"),
        cost_estimate=cost(0, 8 * quarter * share * probes),
        name="pick_ends",
    )(core, methyl)


def row_chunk(share):
    return 2 * share * max(1, 128 // share)


def descend_kernel(parts_ref, scores_ref, design_ref, spread_ref, w_ref):
    kk, share = w_ref.shape
    total = parts_ref[0]
    for peer in range(1, parts_ref.shape[0]):
        total = total + parts_ref[peer]
    gram = total[kk:, :kk]
    row = lax.broadcasted_iota(jnp.int32, (kk, kk), 0)
    col = lax.broadcasted_iota(jnp.int32, (kk, kk), 1)
    trace = jnp.sum(jnp.where(row == col, gram, 0.0), axis=(0, 1), keepdims=True)
    rate = 1.0 / trace
    step = jnp.where(row == col, 1.0, 0.0) - rate * gram
    pull = rate * total[:kk, :]
    for k in range(kk):
        spread_ref[k] = jnp.broadcast_to(step[:, k : k + 1], (kk, share))
    w_ref[...] = jnp.full((kk, share), 1.0 / kk, F32)

    def descend(_, carry):
        acc = [pull, None, None, None]
        for k in range(kk):
            term = spread_ref[k] * w_ref[k : k + 1, :]
            acc[k % 4] = term if acc[k % 4] is None else acc[k % 4] + term
        w_ref[...] = jnp.maximum((acc[0] + acc[1]) + (acc[2] + acc[3]), 0.0)
        return carry

    lax.fori_loop(0, ITERS, descend, 0)
    weights = w_ref[...]
    scores_ref[...] = kk * weights
    design = weights.astype(BF16)
    for peer in range(design_ref.shape[0]):
        design_ref[peer] = design


def descend(parts):
    shares, _, share = parts.shape
    return pl.pallas_call(
        descend_kernel,
        out_shape=(
            jax.ShapeDtypeStruct((K, share), F32),
            jax.ShapeDtypeStruct((shares, K, share), BF16),
        ),
        scratch_shapes=[pltpu.VMEM((K, K, share), F32), pltpu.VMEM((K, share), F32)],
        compiler_params=params(),
        cost_estimate=cost(2 * ITERS * K * K * share, 4 * K * share),
        name="descend",
    )(parts)


def cross_kernel(design_ref, methyl_ref, panel_ref, out_ref):
    blocks, kk, _ = design_ref.shape
    probes = methyl_ref.shape[1]
    design = jnp.concatenate([design_ref[b] for b in range(blocks)], axis=1)

    @pl.when(pl.program_id(0) == 0)
    def _():
        out_ref[...] = jnp.zeros_like(out_ref)

    out_ref[:, probes : probes + kk] += nt(design, design)
    width = min(probes, 512)
    for at in range(0, probes, width):
        cols = slice(at, at + width)
        out_ref[:, cols] += jnp.dot(design, methyl_ref[:, cols], preferred_element_type=F32)
        left = methyl_ref[:, cols].astype(F32) - tn(design, panel_ref[:, cols])
        squares = jnp.sum(left * left, axis=0, keepdims=True)
        for b in range(0, width, HALF):
            row = (at + b) // HALF
            out_ref[row : row + 1, probes + HALF :] += squares[:, b : b + HALF]


def cross_products(design, methyl, panel):
    _, _, share = design.shape
    rows, probes = methyl.shape
    chunk = row_chunk(share)
    return pl.pallas_call(
        cross_kernel,
        grid=(rows // chunk,),
        in_specs=[
            pl.BlockSpec((chunk // share, K, share), lambda i: (i, 0, 0)),
            pl.BlockSpec((chunk, probes), lambda i: (i, 0)),
            pl.BlockSpec((K, probes), lambda i: (0, 0)),
        ],
        out_specs=pl.BlockSpec((K, probes + LANES), lambda i: (0, 0)),
        out_shape=jax.ShapeDtypeStruct((K, probes + LANES), F32),
        compiler_params=params("arbitrary"),
        cost_estimate=cost(4 * K * rows * probes, 2 * rows * probes),
        name="cross",
    )(design, methyl, panel)


def ridge_inverse(matrix):
    kk = matrix.shape[0]
    row = lax.broadcasted_iota(jnp.int32, (kk, kk), 0)
    col = lax.broadcasted_iota(jnp.int32, (kk, kk), 1)
    work = jnp.concatenate([matrix, jnp.where(row == col, 1.0, 0.0)], axis=1)
    which = lax.broadcasted_iota(jnp.int32, (kk, 1), 0)
    for k in range(kk):
        pivot_row = work[k : k + 1, :] / work[k : k + 1, k : k + 1]
        factor = jnp.where(which == k, 0.0, work[:, k : k + 1])
        work = jnp.where(which == k, pivot_row, work - factor * pivot_row)
    return work[:, kk:]


def solve_kernel(ridge, samples, *refs):
    parts, panel_ref, out_ref = refs[:-2], refs[-2], refs[-1]
    kk, probes = panel_ref.shape
    total = parts[0][...]
    for ref in parts[1:]:
        total = total + ref[...]
    cross = total[:, :probes]
    wgram = total[:, probes : probes + kk]
    start = jnp.concatenate(
        [total[r : r + 1, probes + HALF :] for r in range(probes // HALF)], axis=1
    )
    row = lax.broadcasted_iota(jnp.int32, (kk, kk), 0)
    col = lax.broadcasted_iota(jnp.int32, (kk, kk), 1)
    system = wgram + jnp.where(row == col, ridge, 0.0)
    inverse = ridge_inverse(system)
    loadings = jnp.dot(inverse, cross, precision=HIGHEST)
    short = cross - jnp.dot(system, loadings, precision=HIGHEST)
    loadings = loadings + jnp.dot(inverse, short, precision=HIGHEST)
    panel = panel_ref[...].astype(F32)
    slope = jnp.dot(wgram, loadings + panel, precision=HIGHEST) - 2.0 * cross
    spread = start + jnp.sum((loadings - panel) * slope, axis=0, keepdims=True)
    rate = lax.rsqrt(jnp.maximum(spread, 0.0) / samples + 1e-06)
    out_ref[:kk, :] = loadings
    out_ref[kk:, :] = jnp.broadcast_to(rate, (out_ref.shape[0] - kk, probes))


def solve(parts, panel, ridge, samples):
    probes = panel.shape[1]
    return pl.pallas_call(
        functools.partial(solve_kernel, ridge, samples),
        out_shape=jax.ShapeDtypeStruct((K + 8, probes), F32),
        compiler_params=params(),
        cost_estimate=cost(50 * K * K * probes, 20 * K * probes),
        name="solve",
    )(*parts, panel)


def standardise(design, methyl_ref, terms_ref, rate, store):
    probes = methyl_ref.shape[1]
    stacked = jnp.concatenate([design] * 3, axis=0)
    width = min(probes, 512)
    for at in range(0, probes, width):
        cols = slice(at, at + width)
        fitted = tn(stacked, terms_ref[:, cols])
        left = methyl_ref[:, cols].astype(F32) - fitted
        store(at, width, (left * rate[:, cols]).astype(BF16))


def put_tile(part, sends, keep_ref):
    share = keep_ref.shape[1]
    keep_ref[...] = part[:, :share]
    for j, ref in enumerate(sends, 1):
        ref[...] = part[:, j * share : (j + 1) * share].astype(BF16)


def own_kernel(
    steps, line, place_ref, core_ref, design_ref, mine_ref, theirs_ref, facts_ref, more_ref, *refs
):
    (z_ref, *sends), (keep_ref, half_ref, terms_ref, moreterms_ref) = refs[:line], refs[line:]
    step = pl.program_id(0)
    blocks, kk, share = design_ref.shape
    chunk, probes = mine_ref.shape
    place, core = place_ref[0], core_ref[0]

    @pl.when(step == 0)
    def _():
        terms_ref[...] = three_terms(facts_ref[:kk, :])
        moreterms_ref[...] = three_terms(more_ref[:kk, :])

    @pl.when(step < steps)
    def _():
        design = jnp.concatenate([design_ref[b] for b in range(blocks)], axis=1)
        rows = pl.ds(pl.multiple_of(step * chunk, chunk), chunk)

        def store(base, at, width, value):
            z_ref[rows, base + at : base + at + width] = value

        standardise(design, mine_ref, terms_ref, facts_ref[kk : kk + 1, :], functools.partial(store, 0))
        standardise(
            design, theirs_ref, moreterms_ref, more_ref[kk : kk + 1, :], functools.partial(store, probes)
        )
        for b in range(blocks // 2):
            here = pl.ds(pl.multiple_of(step * chunk + (2 * b + core) * share, share), share)
            slot = lax.rem(step * (blocks // 2) + b - place + line, line)
            half_ref[pl.ds(pl.multiple_of(slot * share, share), share), :] = z_ref[here, :]

    @pl.when(step >= steps)
    def _():
        tall = keep_ref.shape[0]
        rows = pl.ds(pl.multiple_of((step - steps) * tall, tall), tall)
        put_tile(nt(z_ref[rows, :], half_ref[...]), sends, keep_ref)


def own_tile(at, line, design, mine, theirs, facts, more):
    _, _, share = design.shape
    rows, probes = mine.shape
    chunk = row_chunk(share)
    steps, tall = rows // chunk, 2 * chunk

    def first(i, *_):
        return (jnp.minimum(i, steps - 1), 0)

    def second(i, *_):
        return (jnp.maximum(i - steps, 0), 0)

    whole = pl.BlockSpec((K + 8, probes), lambda i, *_: (0, 0))
    return pl.pallas_call(
        functools.partial(own_kernel, steps, line),
        grid_spec=pltpu.PrefetchScalarGridSpec(
            num_scalar_prefetch=2,
            grid=(steps + rows // tall,),
            in_specs=[
                pl.BlockSpec((chunk // share, K, share), lambda i, *_: (*first(i), 0)),
                pl.BlockSpec((chunk, probes), first),
                pl.BlockSpec((chunk, probes), first),
                whole,
                whole,
            ],
            out_specs=[pl.BlockSpec(memory_space=pltpu.VMEM)]
            + [pl.BlockSpec((tall, share), second)] * line,
            scratch_shapes=[
                pltpu.VMEM((rows // 2, 2 * probes), BF16),
                pltpu.VMEM((3 * K, probes), BF16),
                pltpu.VMEM((3 * K, probes), BF16),
            ],
        ),
        out_shape=[pltpu.VMEM((rows, 2 * probes), BF16)]
        + [jax.ShapeDtypeStruct((rows, share), BF16)] * (line - 1)
        + [jax.ShapeDtypeStruct((rows, share), F32)],
        compiler_params=params("arbitrary"),
        cost_estimate=cost(2 * rows * rows * probes, 12 * rows * probes),
        name="own",
    )(*at, design, mine, theirs, facts, more)


def pair_kernel(index_of, line, first, sides, given, last, place_ref, design_ref, zscore_ref, *refs):
    facts, raws, refs = refs[:sides], refs[sides : 2 * sides], refs[2 * sides :]
    given_ref, refs = (refs[0], refs[1:]) if given else (None, refs)
    outs, (z_ref, *terms) = refs[: -1 - sides], refs[-1 - sides :]
    blocks, kk, share = design_ref.shape
    probes = facts[0].shape[1]
    tall = outs[0].shape[0]
    step, place = pl.program_id(0), place_ref[0]

    @pl.when(step == 0)
    def _():
        design = jnp.concatenate([design_ref[b] for b in range(blocks)], axis=1)
        for side in range(sides):
            terms[side][...] = three_terms(facts[side][:kk, :])

            def store(at, width, value):
                z_ref[:, side * probes + at : side * probes + at + width] = value

            standardise(design, raws[side], terms[side], facts[side][kk : kk + 1, :], store)

    @pl.when(step > 0)
    def _():
        rows = pl.ds(pl.multiple_of((step - 1) * tall, tall), tall)
        part = nt(zscore_ref[rows, first * probes : (first + sides) * probes], z_ref[...])
        if given:
            part = part + given_ref[rows, :]
        if not last:
            outs[0][...] = part
            return
        *sends, keep_ref = outs
        for j, ref in enumerate([keep_ref, *sends]):
            index, inside = index_of(lax.rem(place + j, line))
            block = part[:, :share]
            for b in range(1, blocks):
                block = jnp.where(index == b, part[:, b * share : (b + 1) * share], block)
            if j == 0:
                block = jnp.where(inside, block, 0.0)
            ref[...] = block.astype(ref.dtype)


def pair_tile(index_of, at, line, design, zscore, first, facts, raws, given=None, last=True):
    blocks, _, share = design.shape
    rows, depth = zscore.shape
    probes, sides = depth // 2, len(facts)
    tall = 2 * row_chunk(share)
    given = [] if given is None else [given]
    width = share if last else blocks * share
    column = pl.BlockSpec((tall, width), lambda i, *_: (jnp.maximum(i - 1, 0), 0))
    whole = jax.ShapeDtypeStruct((rows, width), F32)
    sends = [jax.ShapeDtypeStruct((rows, share), BF16)] * (line - 1)
    return pl.pallas_call(
        functools.partial(pair_kernel, index_of, line, first, sides, bool(given), last),
        grid_spec=pltpu.PrefetchScalarGridSpec(
            num_scalar_prefetch=1,
            grid=(1 + rows // tall,),
            in_specs=[pl.BlockSpec(memory_space=pltpu.VMEM)] * (2 + 2 * sides + len(given)),
            out_specs=[column] * line if last else [column],
            scratch_shapes=[pltpu.VMEM((blocks * share, sides * probes), BF16)]
            + [pltpu.VMEM((3 * K, probes), BF16)] * sides,
        ),
        out_shape=sends + [whole] if last else [whole],
        compiler_params=params("arbitrary"),
        cost_estimate=cost(2 * rows * blocks * share * sides * probes, 4 * rows * probes),
    )(at[0], design, zscore, *facts, *raws, *given)


def fold_kernel(line, place_ref, core_ref, *refs):
    (keep_ref, *parts), (total_ref, same_ref, other_ref) = refs[:-3], refs[-3:]
    place, core = place_ref[0], core_ref[0]
    share = same_ref.shape[1]
    total = keep_ref[...]
    for ref in parts:
        total = total + ref[...].astype(F32)
    total_ref[...] = total
    for j in range(line):
        block = 2 * lax.rem(place + j, line)
        same = pl.ds(pl.multiple_of((block + core) * share, share), share)
        other = pl.ds(pl.multiple_of((block + 1 - core) * share, share), share)
        same_ref[j] = total_ref[same, :].astype(BF16)
        other_ref[j] = total_ref[other, :].astype(BF16)


def fold(at, line, parts):
    rows, share = parts[0].shape
    blocks = jax.ShapeDtypeStruct((line, share, share), BF16)
    vmem = pl.BlockSpec(memory_space=pltpu.VMEM)
    return pl.pallas_call(
        functools.partial(fold_kernel, line),
        in_specs=[pl.BlockSpec(memory_space=pltpu.SMEM)] * 2 + [vmem] * len(parts),
        out_shape=(jax.ShapeDtypeStruct((rows, share), F32), blocks, blocks),
        compiler_params=params(),
        cost_estimate=cost(rows * share * 8, rows * share * 16),
        name="fold",
    )(*at, *parts)


def scale_kernel(probes, wholes, own_ref, *refs):
    parts, halves, (left_ref, out_ref) = refs[:wholes], refs[wholes:-2], refs[-2:]
    total = own_ref[...]
    for ref in parts:
        total = total + ref[...].astype(F32)
    for top, bottom in zip(halves[: len(halves) // 2], halves[len(halves) // 2 :]):
        total = total + jnp.concatenate([top[...], bottom[...]], axis=0).astype(F32)
    out_ref[0] = total * (1.0 / probes)
    out_ref[1] = left_ref[...] * (1.0 / probes)


def scale(probes, keep, parts, tops, bottoms, left):
    rows, share = keep.shape
    whole = pl.BlockSpec((rows, share), lambda i: (0, 0))
    half = pl.BlockSpec((rows // 2, share), lambda i: (0, 0))
    return pl.pallas_call(
        functools.partial(scale_kernel, probes, len(parts)),
        grid=(1,),
        in_specs=[whole] * (1 + len(parts)) + [half] * (2 * len(tops)) + [whole],
        out_specs=pl.BlockSpec((2, rows, share), lambda i: (0, 0, 0)),
        out_shape=jax.ShapeDtypeStruct((3, rows, share), F32),
        compiler_params=params("arbitrary"),
        cost_estimate=cost(rows * share * 16, rows * share * 30),
        name="scale",
    )(keep, *parts, *tops, *bottoms, left)


def finish_kernel(line, probes, place_ref, core_ref, _, same_ref, other_ref, *refs):
    shifted, out_ref = refs[:-1], refs[-1]
    place, core = place_ref[0], core_ref[0]
    share = same_ref.shape[1]
    for j in range(line):
        block = 2 * lax.rem(place - j + line, line)
        for side in range(2):
            piece = (same_ref, other_ref)[side][0] if j == 0 else shifted[j - 1][side]
            to = block + (core if side == 0 else 1 - core)
            rows = pl.ds(pl.multiple_of(to * share, share), share)
            out_ref[0, rows, :] = piece.astype(F32).T * (1.0 / probes)


def finish(at, line, probes, tiles, same, other, shifted):
    _, rows, share = tiles.shape
    first = pl.BlockSpec((1, share, share), lambda i: (0, 0, 0))
    pair = pl.BlockSpec((2, share, share), lambda i: (0, 0, 0))
    return pl.pallas_call(
        functools.partial(finish_kernel, line, probes),
        grid=(1,),
        in_specs=[pl.BlockSpec(memory_space=pltpu.SMEM)] * 2
        + [pl.BlockSpec(memory_space=pl.ANY), first, first]
        + [pair] * len(shifted),
        out_specs=pl.BlockSpec((1, rows, share), lambda i: (2, 0, 0)),
        out_shape=jax.ShapeDtypeStruct(tiles.shape, F32),
        input_output_aliases={2: 0},
        compiler_params=params("arbitrary"),
        cost_estimate=cost(rows * share * 4, rows * share * 8),
        name="finish",
    )(*at, tiles, same, other, *shifted)


def body(methyl, atlas, panel_ids):
    panels, shares = lax.axis_size("samp"), lax.axis_size("probe")
    rows = methyl.shape[0]
    samples = rows * panels
    probes = methyl.shape[1] * shares
    share = rows // shares
    line = shares // 2
    position = lax.axis_index("probe")
    place, core = position // 2, position % 2
    at = (place[None], core[None])

    def along(value, axis, pairs):
        return lax.ppermute(value, axis, pairs)

    def to_sibling(value):
        return along(value, "probe", [(i, i ^ 1) for i in range(shares)])

    def to_panel(value, by):
        return along(value, "samp", [(i, (i + by) % panels) for i in range(panels)])

    def to_panel_sibling(value, by):
        pairs = [
            (s * shares + i, ((s + by) % panels) * shares + (i ^ 1))
            for s in range(panels)
            for i in range(shares)
        ]
        return along(value, ("samp", "probe"), pairs)

    def swap_panels(value, bit):
        return along(value, "samp", [(i, i ^ bit) for i in range(panels)])

    def on_line(value, pairs):
        return along(value, "probe", [(2 * i + c, 2 * to + c) for i, to in pairs for c in (0, 1)])

    quarter = line // 4
    ends = [*range(quarter), *range(line - quarter, line)]
    inner = [*range(quarter, line - quarter)]

    def among_ends(to):
        high = to >= line - quarter
        return jnp.where(high, to - (line - 2 * quarter), to), (to < quarter) | high

    def among_inner(to):
        return to - quarter, (to >= quarter) & (to < line - quarter)

    ends_mine = to_panel(pick_ends(core[None], methyl, line, share), 1)
    theirs = to_sibling(methyl)
    parts, panel, outer, same, other = project(core[None], panel_ids, atlas, methyl, shares)
    ends_theirs = to_panel_sibling(outer, 1)
    parts = lax.all_to_all(parts, "probe", 0, 0)
    scores, copies = descend(parts)
    design = lax.all_to_all(copies, "probe", 0, 0)
    part = cross_products(design, methyl, panel)
    peers = [swap_panels(part, mask) for mask in range(1, panels)]
    half = lax.dynamic_index_in_dim(design.reshape(line, 2, K, share), core, 1, False)
    design_before = to_panel(half, 1)
    inner_mine = to_panel(same, 1)
    inner_theirs = to_panel_sibling(other, 1)
    facts = solve([part, *peers], panel, 0.0001 * samples, samples)
    more = to_sibling(facts)

    def round_of(by, among=None):
        pairs = [(i, (i + by) % line) for i in range(line)]
        return pairs if among is None else [(i, to) for i, to in pairs if to in among]

    def arrivals(sends, among=None, rounds=None):
        return [
            on_line(value, round_of(j, among))
            for j, value in enumerate(sends, 1)
            if rounds is None or j in rounds
        ]

    zscore, *own_sends, own_keep = own_tile(at, line, design, methyl, theirs, facts, more)
    early = {1, line - 1}
    late = set(range(1, line)) - early
    own_parts = arrivals(own_sends, rounds=early)
    tops = arrivals([value[: rows // 2] for value in own_sends], rounds=late)
    design_ends = jnp.concatenate([design_before[:quarter], design_before[line - quarter :]])
    *sends, keep = pair_tile(
        among_ends, at, line, design_ends, zscore, 0, [facts, more],
        [ends_mine, ends_theirs],
    )
    pair_parts = [keep] + arrivals(sends, ends)
    design_inner = design_before[quarter : line - quarter]
    (partial,) = pair_tile(
        among_inner, at, line, design_inner, zscore, 0, [facts], [inner_mine],
        last=False,
    )
    *sends, keep = pair_tile(
        among_inner, at, line, design_inner, zscore, 1, [more], [inner_theirs],
        given=partial,
    )
    pair_parts.append(keep)
    pair_parts += arrivals(sends, inner, late)
    pair_parts += arrivals(sends, inner, early)
    left, same, other = fold(at, line, pair_parts)
    same = to_panel(same, -1)
    other = to_panel_sibling(other, -1)
    bottoms = arrivals([value[rows // 2 :] for value in own_sends], rounds=late)
    shifted = []
    for j in range(1, line):
        shifted.append(on_line(jnp.stack([same[j], other[j]]), round_of(j)))
    tiles = scale(probes, own_keep, own_parts, tops, bottoms, left)
    return finish(at, line, probes, tiles, same, other, shifted), scores


def solution(mesh):
    placed = (P("samp", "probe"), P(None, "probe"), P())
    return jax.shard_map(
        body,
        mesh=mesh,
        in_specs=placed,
        out_specs=(P(None, "samp", "probe"), P(None, ("samp", "probe"))),
        check_vma=False,
    )
```

```python
import functools

import jax
import jax.numpy as jnp
from jax import lax
from jax.experimental import pallas as pl
from jax.experimental.pallas import tpu as pltpu
from jax.sharding import PartitionSpec as P


K = 32
ITERS = 128
F32, BF16 = jnp.float32, jnp.bfloat16
HIGHEST = lax.Precision.HIGHEST
LANES = 128
HALF = LANES // 2
VMEM_LIMIT = 40 * 1024 * 1024


def nt(a, b):
    return lax.dot_general(a, b, (((1,), (1,)), ((), ())), preferred_element_type=F32)


def tn(a, b):
    return lax.dot_general(a, b, (((0,), (0,)), ((), ())), preferred_element_type=F32)


def params(*semantics):
    return pltpu.CompilerParams(dimension_semantics=semantics, vmem_limit_bytes=VMEM_LIMIT)


def cost(flops, nbytes):
    return pl.CostEstimate(flops=int(flops), bytes_accessed=int(nbytes), transcendentals=0)


def three_terms(value):
    high = value.astype(BF16)
    rest = value - high.astype(F32)
    mid = rest.astype(BF16)
    low = (rest - mid.astype(F32)).astype(BF16)
    return jnp.concatenate([high, mid, low], axis=0)


def project_kernel(
    quarter, core_ref, ids_ref, atlas_ref, methyl_ref, out_ref, panel_ref, outer_ref, same_ref, other_ref,
    gram_ref,
):
    kk = panel_ref.shape[0]
    blocks, _, share = out_ref.shape
    core = core_ref[0]

    @pl.when(pl.program_id(0) == 0)
    def _():
        rows = atlas_ref.shape[0]
        row = lax.broadcasted_iota(jnp.int32, (kk, rows), 0)
        wanted = jnp.zeros((kk, rows), jnp.int32)
        for k in range(kk):
            wanted = jnp.where(row == k, ids_ref[k], wanted)
        pick = wanted == lax.broadcasted_iota(jnp.int32, (kk, rows), 1)
        chosen = jnp.where(pick, 1.0, 0.0).astype(BF16)
        panel = jnp.dot(chosen, atlas_ref[...], preferred_element_type=F32).astype(BF16)
        panel_ref[...] = panel
        gram_ref[...] = nt(panel, panel)

    proj = nt(methyl_ref[...], panel_ref[...]).T
    for b in range(blocks):
        out_ref[b, :kk, :] = proj[:, b * share : (b + 1) * share]
        out_ref[b, kk:, :] = jnp.zeros((kk, share), F32)
        out_ref[b, kk:, :kk] = gram_ref[...]

    def put(ref, side):
        for b in range(blocks // 2):
            start = pl.multiple_of((2 * b + side) * share, share)
            ref[b * share : (b + 1) * share, :] = methyl_ref[pl.ds(start, share), :]

    step, steps = pl.program_id(0), pl.num_programs(0)

    @pl.when((step < quarter) | (step >= steps - quarter))
    def _():
        put(outer_ref, 1 - core)

    @pl.when((step >= quarter) & (step < steps - quarter))
    def _():
        put(same_ref, core)
        put(other_ref, 1 - core)


def project(core, panel_ids, atlas, methyl, shares):
    rows, probes = methyl.shape
    share = rows // shares
    chunk = row_chunk(share)
    steps = rows // chunk
    quarter = steps // 4

    def outer(i):
        return (jnp.where(i < steps - quarter, jnp.minimum(i, quarter - 1), i - steps + 2 * quarter), 0)

    def inner(i):
        return (jnp.clip(i - quarter, 0, steps - 2 * quarter - 1), 0)

    def rows_of(count):
        return jax.ShapeDtypeStruct((count * chunk // 2, probes), BF16)

    return pl.pallas_call(
        functools.partial(project_kernel, quarter),
        grid=(steps,),
        in_specs=[
            pl.BlockSpec(memory_space=pltpu.SMEM),
            pl.BlockSpec(memory_space=pltpu.SMEM),
            pl.BlockSpec(atlas.shape, lambda i: (0, 0)),
            pl.BlockSpec((chunk, probes), lambda i: (i, 0)),
        ],
        out_specs=(
            pl.BlockSpec((chunk // share, 2 * K, share), lambda i: (i, 0, 0)),
            pl.BlockSpec((K, probes), lambda i: (0, 0)),
            pl.BlockSpec((chunk // 2, probes), outer),
            pl.BlockSpec((chunk // 2, probes), inner),
            pl.BlockSpec((chunk // 2, probes), inner),
        ),
        out_shape=(
            jax.ShapeDtypeStruct((shares, 2 * K, share), F32),
            jax.ShapeDtypeStruct((K, probes), BF16),
            rows_of(2 * quarter),
            rows_of(steps - 2 * quarter),
            rows_of(steps - 2 * quarter),
        ),
        scratch_shapes=[pltpu.VMEM((K, K), F32)],
        compiler_params=params("arbitrary"),
        cost_estimate=cost(2 * K * rows * probes, 4 * rows * probes),
        name="project",
    )(core, panel_ids, atlas, methyl)


def copy_kernel(_, from_ref, to_ref):
    to_ref[...] = from_ref[...]


def pick_ends(core, methyl, line, share):
    probes = methyl.shape[1]
    quarter = line // 4

    def block(i, core):
        return (2 * jnp.where(i < quarter, i, i + line - 2 * quarter) + core[0], 0)

    return pl.pallas_call(
        copy_kernel,
        grid_spec=pltpu.PrefetchScalarGridSpec(
            num_scalar_prefetch=1,
            grid=(2 * quarter,),
            in_specs=[pl.BlockSpec((share, probes), block)],
            out_specs=pl.BlockSpec((share, probes), lambda i, core: (i, 0)),
        ),
        out_shape=jax.ShapeDtypeStruct((2 * quarter * share, probes), BF16),
        compiler_params=params("arbitrary"),
        cost_estimate=cost(0, 8 * quarter * share * probes),
        name="pick_ends",
    )(core, methyl)


def row_chunk(share):
    return 2 * share * max(1, 128 // share)


def descend_kernel(parts_ref, scores_ref, design_ref, spread_ref, w_ref):
    kk, share = w_ref.shape
    total = parts_ref[0]
    for peer in range(1, parts_ref.shape[0]):
        total = total + parts_ref[peer]
    gram = total[kk:, :kk]
    row = lax.broadcasted_iota(jnp.int32, (kk, kk), 0)
    col = lax.broadcasted_iota(jnp.int32, (kk, kk), 1)
    trace = jnp.sum(jnp.where(row == col, gram, 0.0), axis=(0, 1), keepdims=True)
    rate = 1.0 / trace
    step = jnp.where(row == col, 1.0, 0.0) - rate * gram
    pull = rate * total[:kk, :]
    for k in range(kk):
        spread_ref[k] = jnp.broadcast_to(step[:, k : k + 1], (kk, share))
    w_ref[...] = jnp.full((kk, share), 1.0 / kk, F32)

    def descend(_, carry):
        acc = [pull, None, None, None]
        for k in range(kk):
            term = spread_ref[k] * w_ref[k : k + 1, :]
            acc[k % 4] = term if acc[k % 4] is None else acc[k % 4] + term
        w_ref[...] = jnp.maximum((acc[0] + acc[1]) + (acc[2] + acc[3]), 0.0)
        return carry

    lax.fori_loop(0, ITERS, descend, 0)
    weights = w_ref[...]
    scores_ref[...] = kk * weights
    design = weights.astype(BF16)
    for peer in range(design_ref.shape[0]):
        design_ref[peer] = design


def descend(parts):
    shares, _, share = parts.shape
    return pl.pallas_call(
        descend_kernel,
        out_shape=(
            jax.ShapeDtypeStruct((K, share), F32),
            jax.ShapeDtypeStruct((shares, K, share), BF16),
        ),
        scratch_shapes=[pltpu.VMEM((K, K, share), F32), pltpu.VMEM((K, share), F32)],
        compiler_params=params(),
        cost_estimate=cost(2 * ITERS * K * K * share, 4 * K * share),
        name="descend",
    )(parts)


def cross_kernel(design_ref, methyl_ref, panel_ref, out_ref):
    blocks, kk, _ = design_ref.shape
    probes = methyl_ref.shape[1]
    design = jnp.concatenate([design_ref[b] for b in range(blocks)], axis=1)

    @pl.when(pl.program_id(0) == 0)
    def _():
        out_ref[...] = jnp.zeros_like(out_ref)

    out_ref[:, probes : probes + kk] += nt(design, design)
    width = min(probes, 512)
    for at in range(0, probes, width):
        cols = slice(at, at + width)
        out_ref[:, cols] += jnp.dot(design, methyl_ref[:, cols], preferred_element_type=F32)
        left = methyl_ref[:, cols].astype(F32) - tn(design, panel_ref[:, cols])
        squares = jnp.sum(left * left, axis=0, keepdims=True)
        for b in range(0, width, HALF):
            row = (at + b) // HALF
            out_ref[row : row + 1, probes + HALF :] += squares[:, b : b + HALF]


def cross_products(design, methyl, panel):
    _, _, share = design.shape
    rows, probes = methyl.shape
    chunk = row_chunk(share)
    return pl.pallas_call(
        cross_kernel,
        grid=(rows // chunk,),
        in_specs=[
            pl.BlockSpec((chunk // share, K, share), lambda i: (i, 0, 0)),
            pl.BlockSpec((chunk, probes), lambda i: (i, 0)),
            pl.BlockSpec((K, probes), lambda i: (0, 0)),
        ],
        out_specs=pl.BlockSpec((K, probes + LANES), lambda i: (0, 0)),
        out_shape=jax.ShapeDtypeStruct((K, probes + LANES), F32),
        compiler_params=params("arbitrary"),
        cost_estimate=cost(4 * K * rows * probes, 2 * rows * probes),
        name="cross",
    )(design, methyl, panel)


def ridge_inverse(matrix):
    kk = matrix.shape[0]
    row = lax.broadcasted_iota(jnp.int32, (kk, kk), 0)
    col = lax.broadcasted_iota(jnp.int32, (kk, kk), 1)
    work = jnp.concatenate([matrix, jnp.where(row == col, 1.0, 0.0)], axis=1)
    which = lax.broadcasted_iota(jnp.int32, (kk, 1), 0)
    for k in range(kk):
        pivot_row = work[k : k + 1, :] / work[k : k + 1, k : k + 1]
        factor = jnp.where(which == k, 0.0, work[:, k : k + 1])
        work = jnp.where(which == k, pivot_row, work - factor * pivot_row)
    return work[:, kk:]


def solve_kernel(ridge, samples, *refs):
    parts, panel_ref, out_ref = refs[:-2], refs[-2], refs[-1]
    kk, probes = panel_ref.shape
    total = parts[0][...]
    for ref in parts[1:]:
        total = total + ref[...]
    cross = total[:, :probes]
    wgram = total[:, probes : probes + kk]
    start = jnp.concatenate(
        [total[r : r + 1, probes + HALF :] for r in range(probes // HALF)], axis=1
    )
    row = lax.broadcasted_iota(jnp.int32, (kk, kk), 0)
    col = lax.broadcasted_iota(jnp.int32, (kk, kk), 1)
    system = wgram + jnp.where(row == col, ridge, 0.0)
    inverse = ridge_inverse(system)
    loadings = jnp.dot(inverse, cross, precision=HIGHEST)
    short = cross - jnp.dot(system, loadings, precision=HIGHEST)
    loadings = loadings + jnp.dot(inverse, short, precision=HIGHEST)
    panel = panel_ref[...].astype(F32)
    slope = jnp.dot(wgram, loadings + panel, precision=HIGHEST) - 2.0 * cross
    spread = start + jnp.sum((loadings - panel) * slope, axis=0, keepdims=True)
    rate = lax.rsqrt(jnp.maximum(spread, 0.0) / samples + 1e-06)
    out_ref[:kk, :] = loadings
    out_ref[kk:, :] = jnp.broadcast_to(rate, (out_ref.shape[0] - kk, probes))


def solve(parts, panel, ridge, samples):
    probes = panel.shape[1]
    return pl.pallas_call(
        functools.partial(solve_kernel, ridge, samples),
        out_shape=jax.ShapeDtypeStruct((K + 8, probes), F32),
        compiler_params=params(),
        cost_estimate=cost(50 * K * K * probes, 20 * K * probes),
        name="solve",
    )(*parts, panel)


def standardise(design, methyl_ref, terms_ref, rate, store):
    probes = methyl_ref.shape[1]
    stacked = jnp.concatenate([design] * 3, axis=0)
    width = min(probes, 512)
    for at in range(0, probes, width):
        cols = slice(at, at + width)
        fitted = tn(stacked, terms_ref[:, cols])
        left = methyl_ref[:, cols].astype(F32) - fitted
        store(at, width, (left * rate[:, cols]).astype(BF16))


def relayed(place, line):
    far = jnp.where(place <= 1, line - 1, 0)
    return jnp.where((place <= 1) | (place >= line - 2), lax.rem(far - place + line, line), 0)


def put_tile(part, own, sends, keep_ref):
    share = keep_ref.shape[1]
    keep = None
    for j, ref in enumerate(sends):
        block = part[:, j * share : (j + 1) * share]
        ref[...] = block.astype(BF16)
        mine = jnp.where(own == j, block, 0.0)
        keep = mine if keep is None else keep + mine
    keep_ref[...] = keep


def own_kernel(
    steps, line, place_ref, core_ref, design_ref, mine_ref, theirs_ref, facts_ref, more_ref, *refs
):
    (z_ref, *sends), (keep_ref, half_ref, terms_ref, moreterms_ref) = (
        refs[: line + 1],
        refs[line + 1 :],
    )
    step = pl.program_id(0)
    blocks, kk, share = design_ref.shape
    chunk, probes = mine_ref.shape
    place, core = place_ref[0], core_ref[0]

    @pl.when(step == 0)
    def _():
        terms_ref[...] = three_terms(facts_ref[:kk, :])
        moreterms_ref[...] = three_terms(more_ref[:kk, :])

    @pl.when(step < steps)
    def _():
        design = jnp.concatenate([design_ref[b] for b in range(blocks)], axis=1)
        rows = pl.ds(pl.multiple_of(step * chunk, chunk), chunk)

        def store(base, at, width, value):
            z_ref[rows, base + at : base + at + width] = value

        standardise(design, mine_ref, terms_ref, facts_ref[kk : kk + 1, :], functools.partial(store, 0))
        standardise(
            design, theirs_ref, moreterms_ref, more_ref[kk : kk + 1, :], functools.partial(store, probes)
        )
        for b in range(blocks // 2):
            here = pl.ds(pl.multiple_of(step * chunk + (2 * b + core) * share, share), share)
            away = lax.rem(step * (blocks // 2) + b - place + line, line)
            skipped = relayed(place, line)
            slot = jnp.where(away == 0, skipped, jnp.where(away == skipped, 0, away))
            half_ref[pl.ds(pl.multiple_of(slot * share, share), share), :] = z_ref[here, :]

    @pl.when(step >= steps)
    def _():
        tall = keep_ref.shape[0]
        rows = pl.ds(pl.multiple_of((step - steps) * tall, tall), tall)
        put_tile(nt(z_ref[rows, :], half_ref[...]), relayed(place, line), sends, keep_ref)


def own_tile(at, line, design, mine, theirs, facts, more):
    _, _, share = design.shape
    rows, probes = mine.shape
    chunk = row_chunk(share)
    steps, tall = rows // chunk, 2 * chunk

    def first(i, *_):
        return (jnp.minimum(i, steps - 1), 0)

    def second(i, *_):
        return (jnp.maximum(i - steps, 0), 0)

    whole = pl.BlockSpec((K + 8, probes), lambda i, *_: (0, 0))
    return pl.pallas_call(
        functools.partial(own_kernel, steps, line),
        grid_spec=pltpu.PrefetchScalarGridSpec(
            num_scalar_prefetch=2,
            grid=(steps + rows // tall,),
            in_specs=[
                pl.BlockSpec((chunk // share, K, share), lambda i, *_: (*first(i), 0)),
                pl.BlockSpec((chunk, probes), first),
                pl.BlockSpec((chunk, probes), first),
                whole,
                whole,
            ],
            out_specs=[pl.BlockSpec(memory_space=pltpu.VMEM)]
            + [pl.BlockSpec((tall, share), second)] * (line + 1),
            scratch_shapes=[
                pltpu.VMEM((rows // 2, 2 * probes), BF16),
                pltpu.VMEM((3 * K, probes), BF16),
                pltpu.VMEM((3 * K, probes), BF16),
            ],
        ),
        out_shape=[pltpu.VMEM((rows, 2 * probes), BF16)]
        + [jax.ShapeDtypeStruct((rows, share), BF16)] * line
        + [jax.ShapeDtypeStruct((rows, share), F32)],
        compiler_params=params("arbitrary"),
        cost_estimate=cost(2 * rows * rows * probes, 12 * rows * probes),
        name="own",
    )(*at, design, mine, theirs, facts, more)


def pair_kernel(index_of, line, first, sides, given, last, place_ref, design_ref, zscore_ref, *refs):
    facts, raws, refs = refs[:sides], refs[sides : 2 * sides], refs[2 * sides :]
    given_ref, refs = (refs[0], refs[1:]) if given else (None, refs)
    outs, (z_ref, *terms) = refs[: -1 - sides], refs[-1 - sides :]
    blocks, kk, share = design_ref.shape
    probes = facts[0].shape[1]
    tall = outs[0].shape[0]
    step, place = pl.program_id(0), place_ref[0]

    @pl.when(step == 0)
    def _():
        design = jnp.concatenate([design_ref[b] for b in range(blocks)], axis=1)
        for side in range(sides):
            terms[side][...] = three_terms(facts[side][:kk, :])

            def store(at, width, value):
                z_ref[:, side * probes + at : side * probes + at + width] = value

            standardise(design, raws[side], terms[side], facts[side][kk : kk + 1, :], store)

    @pl.when(step > 0)
    def _():
        rows = pl.ds(pl.multiple_of((step - 1) * tall, tall), tall)
        part = nt(zscore_ref[rows, first * probes : (first + sides) * probes], z_ref[...])
        if given:
            part = part + given_ref[rows, :]
        if not last:
            outs[0][...] = part
            return
        *sends, keep_ref = outs
        for j, ref in enumerate([keep_ref, *sends]):
            index, inside = index_of(lax.rem(place + j, line))
            block = part[:, :share]
            for b in range(1, blocks):
                block = jnp.where(index == b, part[:, b * share : (b + 1) * share], block)
            if j == 0:
                block = jnp.where(inside, block, 0.0)
            ref[...] = block.astype(ref.dtype)


def pair_tile(index_of, at, line, design, zscore, first, facts, raws, given=None, last=True):
    blocks, _, share = design.shape
    rows, depth = zscore.shape
    probes, sides = depth // 2, len(facts)
    tall = 2 * row_chunk(share)
    given = [] if given is None else [given]
    width = share if last else blocks * share
    column = pl.BlockSpec((tall, width), lambda i, *_: (jnp.maximum(i - 1, 0), 0))
    whole = jax.ShapeDtypeStruct((rows, width), F32)
    sends = [jax.ShapeDtypeStruct((rows, share), BF16)] * (line - 1)
    return pl.pallas_call(
        functools.partial(pair_kernel, index_of, line, first, sides, bool(given), last),
        grid_spec=pltpu.PrefetchScalarGridSpec(
            num_scalar_prefetch=1,
            grid=(1 + rows // tall,),
            in_specs=[pl.BlockSpec(memory_space=pltpu.VMEM)] * (2 + 2 * sides + len(given)),
            out_specs=[column] * line if last else [column],
            scratch_shapes=[pltpu.VMEM((blocks * share, sides * probes), BF16)]
            + [pltpu.VMEM((3 * K, probes), BF16)] * sides,
        ),
        out_shape=sends + [whole] if last else [whole],
        compiler_params=params("arbitrary"),
        cost_estimate=cost(2 * rows * blocks * share * sides * probes, 4 * rows * probes),
    )(at[0], design, zscore, *facts, *raws, *given)


def fold_kernel(line, place_ref, core_ref, *refs):
    (keep_ref, *parts), (total_ref, same_ref, other_ref) = refs[:-3], refs[-3:]
    place, core = place_ref[0], core_ref[0]
    share = same_ref.shape[1]
    total = keep_ref[...]
    for ref in parts:
        total = total + ref[...].astype(F32)
    total_ref[...] = total
    for j in range(line):
        block = 2 * lax.rem(place + j, line)
        same = pl.ds(pl.multiple_of((block + core) * share, share), share)
        other = pl.ds(pl.multiple_of((block + 1 - core) * share, share), share)
        same_ref[j] = total_ref[same, :].astype(BF16)
        other_ref[j] = total_ref[other, :].astype(BF16)


def fold(at, line, parts):
    rows, share = parts[0].shape
    blocks = jax.ShapeDtypeStruct((line, share, share), BF16)
    vmem = pl.BlockSpec(memory_space=pltpu.VMEM)
    return pl.pallas_call(
        functools.partial(fold_kernel, line),
        in_specs=[pl.BlockSpec(memory_space=pltpu.SMEM)] * 2 + [vmem] * len(parts),
        out_shape=(jax.ShapeDtypeStruct((rows, share), F32), blocks, blocks),
        compiler_params=params(),
        cost_estimate=cost(rows * share * 8, rows * share * 16),
        name="fold",
    )(*at, *parts)


def scale_kernel(probes, wholes, own_ref, *refs):
    parts, halves, (left_ref, out_ref) = refs[:wholes], refs[wholes:-2], refs[-2:]
    total = own_ref[...]
    for ref in parts:
        total = total + ref[...].astype(F32)
    for top, bottom in zip(halves[: len(halves) // 2], halves[len(halves) // 2 :]):
        total = total + jnp.concatenate([top[...], bottom[...]], axis=0).astype(F32)
    out_ref[0] = total * (1.0 / probes)
    out_ref[1] = left_ref[...] * (1.0 / probes)


def scale(probes, keep, parts, tops, bottoms, left):
    rows, share = keep.shape
    whole = pl.BlockSpec((rows, share), lambda i: (0, 0))
    half = pl.BlockSpec((rows // 2, share), lambda i: (0, 0))
    return pl.pallas_call(
        functools.partial(scale_kernel, probes, len(parts)),
        grid=(1,),
        in_specs=[whole] * (1 + len(parts)) + [half] * (2 * len(tops)) + [whole],
        out_specs=pl.BlockSpec((2, rows, share), lambda i: (0, 0, 0)),
        out_shape=jax.ShapeDtypeStruct((3, rows, share), F32),
        compiler_params=params("arbitrary"),
        cost_estimate=cost(rows * share * 16, rows * share * 30),
        name="scale",
    )(keep, *parts, *tops, *bottoms, left)


def finish_kernel(line, probes, place_ref, core_ref, _, same_ref, other_ref, *refs):
    shifted, out_ref = refs[:-1], refs[-1]
    place, core = place_ref[0], core_ref[0]
    share = same_ref.shape[1]
    for j in range(line):
        block = 2 * lax.rem(place - j + line, line)
        for side in range(2):
            piece = (same_ref, other_ref)[side][0] if j == 0 else shifted[j - 1][side]
            to = block + (core if side == 0 else 1 - core)
            rows = pl.ds(pl.multiple_of(to * share, share), share)
            out_ref[0, rows, :] = piece.astype(F32).T * (1.0 / probes)


def finish(at, line, probes, tiles, same, other, shifted):
    _, rows, share = tiles.shape
    first = pl.BlockSpec((1, share, share), lambda i: (0, 0, 0))
    pair = pl.BlockSpec((2, share, share), lambda i: (0, 0, 0))
    return pl.pallas_call(
        functools.partial(finish_kernel, line, probes),
        grid=(1,),
        in_specs=[pl.BlockSpec(memory_space=pltpu.SMEM)] * 2
        + [pl.BlockSpec(memory_space=pl.ANY), first, first]
        + [pair] * len(shifted),
        out_specs=pl.BlockSpec((1, rows, share), lambda i: (2, 0, 0)),
        out_shape=jax.ShapeDtypeStruct(tiles.shape, F32),
        input_output_aliases={2: 0},
        compiler_params=params("arbitrary"),
        cost_estimate=cost(rows * share * 4, rows * share * 8),
        name="finish",
    )(*at, tiles, same, other, *shifted)


def body(methyl, atlas, panel_ids):
    panels, shares = lax.axis_size("samp"), lax.axis_size("probe")
    rows = methyl.shape[0]
    samples = rows * panels
    probes = methyl.shape[1] * shares
    share = rows // shares
    line = shares // 2
    position = lax.axis_index("probe")
    place, core = position // 2, position % 2
    at = (place[None], core[None])

    def along(value, axis, pairs):
        return lax.ppermute(value, axis, pairs)

    def to_sibling(value):
        return along(value, "probe", [(i, i ^ 1) for i in range(shares)])

    def to_panel(value, by):
        return along(value, "samp", [(i, (i + by) % panels) for i in range(panels)])

    def to_panel_sibling(value, by):
        pairs = [
            (s * shares + i, ((s + by) % panels) * shares + (i ^ 1))
            for s in range(panels)
            for i in range(shares)
        ]
        return along(value, ("samp", "probe"), pairs)

    def swap_panels(value, bit):
        return along(value, "samp", [(i, i ^ bit) for i in range(panels)])

    def on_line(value, pairs):
        return along(value, "probe", [(2 * i + c, 2 * to + c) for i, to in pairs for c in (0, 1)])

    quarter = line // 4
    ends = [*range(quarter), *range(line - quarter, line)]
    inner = [*range(quarter, line - quarter)]

    def among_ends(to):
        high = to >= line - quarter
        return jnp.where(high, to - (line - 2 * quarter), to), (to < quarter) | high

    def among_inner(to):
        return to - quarter, (to >= quarter) & (to < line - quarter)

    ends_mine = to_panel(pick_ends(core[None], methyl, line, share), 1)
    theirs = to_sibling(methyl)
    parts, panel, outer, same, other = project(core[None], panel_ids, atlas, methyl, shares)
    ends_theirs = to_panel_sibling(outer, 1)
    parts = lax.all_to_all(parts, "probe", 0, 0)
    scores, copies = descend(parts)
    design = lax.all_to_all(copies, "probe", 0, 0)
    part = cross_products(design, methyl, panel)
    peers = [swap_panels(part, mask) for mask in range(1, panels)]
    half = lax.dynamic_index_in_dim(design.reshape(line, 2, K, share), core, 1, False)
    design_before = to_panel(half, 1)
    inner_mine = to_panel(same, 1)
    inner_theirs = to_panel_sibling(other, 1)
    facts = solve([part, *peers], panel, 0.0001 * samples, samples)
    more = to_sibling(facts)

    def round_of(by, among=None):
        pairs = [(i, (i + by) % line) for i in range(line)]
        return pairs if among is None else [(i, to) for i, to in pairs if to in among]

    def arrivals(sends, among=None, rounds=None):
        return [
            on_line(value, round_of(j, among))
            for j, value in enumerate(sends, 1)
            if rounds is None or j in rounds
        ]

    def near_round(by):
        return [(i, to) for i, to in round_of(by) if line <= 3 or abs(to - i) < line - 1]

    zscore, *own_sends, own_keep = own_tile(at, line, design, methyl, theirs, facts, more)
    early = {1, line - 1}
    late = set(range(1, line)) - early
    relay = on_line(own_sends[0], [(0, 1), (line - 1, line - 2)])
    own_parts = [on_line(own_sends[j], near_round(j)) for j in sorted(early)]
    design_ends = jnp.concatenate([design_before[:quarter], design_before[line - quarter :]])
    *sends, keep = pair_tile(
        among_ends, at, line, design_ends, zscore, 0, [facts, more],
        [ends_mine, ends_theirs],
    )
    joined = (own_sends[0].astype(F32) + relay.astype(F32)).astype(BF16)
    for j in sorted(late):
        passing = ((place == 1) & (j == line - 2)) | ((place == line - 2) & (j == 2))
        own_parts.append(on_line(jnp.where(passing, joined, own_sends[j]), near_round(j)))
    pair_parts = [keep] + arrivals(sends, ends)
    design_inner = design_before[quarter : line - quarter]
    (partial,) = pair_tile(
        among_inner, at, line, design_inner, zscore, 0, [facts], [inner_mine],
        last=False,
    )
    *sends, keep = pair_tile(
        among_inner, at, line, design_inner, zscore, 1, [more], [inner_theirs],
        given=partial,
    )
    pair_parts.append(keep)
    pair_parts += arrivals(sends, inner, late)
    pair_parts += arrivals(sends, inner, early)
    left, same, other = fold(at, line, pair_parts)
    same = to_panel(same, -1)
    other = to_panel_sibling(other, -1)
    shifted = []
    for j in range(1, line):
        shifted.append(on_line(jnp.stack([same[j], other[j]]), round_of(j)))
    tiles = scale(probes, own_keep, own_parts, [], [], left)
    return finish(at, line, probes, tiles, same, other, shifted), scores


def solution(mesh):
    placed = (P("samp", "probe"), P(None, "probe"), P())
    return jax.shard_map(
        body,
        mesh=mesh,
        in_specs=placed,
        out_specs=(P(None, "samp", "probe"), P(None, ("samp", "probe"))),
        check_vma=False,
    )
```

```python
import functools

import jax
import jax.numpy as jnp
from jax import lax
from jax.experimental import pallas as pl
from jax.experimental.pallas import tpu as pltpu
from jax.sharding import PartitionSpec as P


K = 32
ITERS = 128
F32, BF16 = jnp.float32, jnp.bfloat16
HIGHEST = lax.Precision.HIGHEST
LANES = 128
HALF = LANES // 2
VMEM_LIMIT = 40 * 1024 * 1024


def nt(a, b):
    return lax.dot_general(a, b, (((1,), (1,)), ((), ())), preferred_element_type=F32)


def tn(a, b):
    return lax.dot_general(a, b, (((0,), (0,)), ((), ())), preferred_element_type=F32)


def params(*semantics):
    return pltpu.CompilerParams(dimension_semantics=semantics, vmem_limit_bytes=VMEM_LIMIT)


def cost(flops, nbytes):
    return pl.CostEstimate(flops=int(flops), bytes_accessed=int(nbytes), transcendentals=0)


def three_terms(value):
    high = value.astype(BF16)
    rest = value - high.astype(F32)
    mid = rest.astype(BF16)
    low = (rest - mid.astype(F32)).astype(BF16)
    return jnp.concatenate([high, mid, low], axis=0)


def project_kernel(
    quarter, core_ref, ids_ref, atlas_ref, methyl_ref, out_ref, panel_ref, outer_ref, same_ref, other_ref,
    gram_ref,
):
    kk = panel_ref.shape[0]
    blocks, _, share = out_ref.shape
    core = core_ref[0]

    @pl.when(pl.program_id(0) == 0)
    def _():
        rows = atlas_ref.shape[0]
        row = lax.broadcasted_iota(jnp.int32, (kk, rows), 0)
        wanted = jnp.zeros((kk, rows), jnp.int32)
        for k in range(kk):
            wanted = jnp.where(row == k, ids_ref[k], wanted)
        pick = wanted == lax.broadcasted_iota(jnp.int32, (kk, rows), 1)
        chosen = jnp.where(pick, 1.0, 0.0).astype(BF16)
        panel = jnp.dot(chosen, atlas_ref[...], preferred_element_type=F32).astype(BF16)
        panel_ref[...] = panel
        gram_ref[...] = nt(panel, panel)

    proj = nt(methyl_ref[...], panel_ref[...]).T
    for b in range(blocks):
        out_ref[b, :kk, :] = proj[:, b * share : (b + 1) * share]
        out_ref[b, kk:, :] = jnp.zeros((kk, share), F32)
        out_ref[b, kk:, :kk] = gram_ref[...]

    def put(ref, side):
        for b in range(blocks // 2):
            start = pl.multiple_of((2 * b + side) * share, share)
            ref[b * share : (b + 1) * share, :] = methyl_ref[pl.ds(start, share), :]

    step, steps = pl.program_id(0), pl.num_programs(0)

    @pl.when((step < quarter) | (step >= steps - quarter))
    def _():
        put(outer_ref, 1 - core)

    @pl.when((step >= quarter) & (step < steps - quarter))
    def _():
        put(same_ref, core)
        put(other_ref, 1 - core)


def project(core, panel_ids, atlas, methyl, shares):
    rows, probes = methyl.shape
    share = rows // shares
    chunk = row_chunk(share)
    steps = rows // chunk
    quarter = steps // 4

    def outer(i):
        return (jnp.where(i < steps - quarter, jnp.minimum(i, quarter - 1), i - steps + 2 * quarter), 0)

    def inner(i):
        return (jnp.clip(i - quarter, 0, steps - 2 * quarter - 1), 0)

    def rows_of(count):
        return jax.ShapeDtypeStruct((count * chunk // 2, probes), BF16)

    return pl.pallas_call(
        functools.partial(project_kernel, quarter),
        grid=(steps,),
        in_specs=[
            pl.BlockSpec(memory_space=pltpu.SMEM),
            pl.BlockSpec(memory_space=pltpu.SMEM),
            pl.BlockSpec(atlas.shape, lambda i: (0, 0)),
            pl.BlockSpec((chunk, probes), lambda i: (i, 0)),
        ],
        out_specs=(
            pl.BlockSpec((chunk // share, 2 * K, share), lambda i: (i, 0, 0)),
            pl.BlockSpec((K, probes), lambda i: (0, 0)),
            pl.BlockSpec((chunk // 2, probes), outer),
            pl.BlockSpec((chunk // 2, probes), inner),
            pl.BlockSpec((chunk // 2, probes), inner),
        ),
        out_shape=(
            jax.ShapeDtypeStruct((shares, 2 * K, share), F32),
            jax.ShapeDtypeStruct((K, probes), BF16),
            rows_of(2 * quarter),
            rows_of(steps - 2 * quarter),
            rows_of(steps - 2 * quarter),
        ),
        scratch_shapes=[pltpu.VMEM((K, K), F32)],
        compiler_params=params("arbitrary"),
        cost_estimate=cost(2 * K * rows * probes, 4 * rows * probes),
        name="project",
    )(core, panel_ids, atlas, methyl)


def copy_kernel(_, from_ref, to_ref):
    to_ref[...] = from_ref[...]


def pick_ends(core, methyl, line, share):
    probes = methyl.shape[1]
    quarter = line // 4

    def block(i, core):
        return (2 * jnp.where(i < quarter, i, i + line - 2 * quarter) + core[0], 0)

    return pl.pallas_call(
        copy_kernel,
        grid_spec=pltpu.PrefetchScalarGridSpec(
            num_scalar_prefetch=1,
            grid=(2 * quarter,),
            in_specs=[pl.BlockSpec((share, probes), block)],
            out_specs=pl.BlockSpec((share, probes), lambda i, core: (i, 0)),
        ),
        out_shape=jax.ShapeDtypeStruct((2 * quarter * share, probes), BF16),
        compiler_params=params("arbitrary"),
        cost_estimate=cost(0, 8 * quarter * share * probes),
        name="pick_ends",
    )(core, methyl)


def row_chunk(share):
    return 2 * share * max(1, 128 // share)


def descend_kernel(parts_ref, scores_ref, design_ref, spread_ref, w_ref):
    kk, share = w_ref.shape
    total = parts_ref[0]
    for peer in range(1, parts_ref.shape[0]):
        total = total + parts_ref[peer]
    gram = total[kk:, :kk]
    row = lax.broadcasted_iota(jnp.int32, (kk, kk), 0)
    col = lax.broadcasted_iota(jnp.int32, (kk, kk), 1)
    trace = jnp.sum(jnp.where(row == col, gram, 0.0), axis=(0, 1), keepdims=True)
    rate = 1.0 / trace
    step = jnp.where(row == col, 1.0, 0.0) - rate * gram
    pull = rate * total[:kk, :]
    for k in range(kk):
        spread_ref[k] = jnp.broadcast_to(step[:, k : k + 1], (kk, share))
    w_ref[...] = jnp.full((kk, share), 1.0 / kk, F32)

    def descend(_, carry):
        acc = [pull, None, None, None]
        for k in range(kk):
            term = spread_ref[k] * w_ref[k : k + 1, :]
            acc[k % 4] = term if acc[k % 4] is None else acc[k % 4] + term
        w_ref[...] = jnp.maximum((acc[0] + acc[1]) + (acc[2] + acc[3]), 0.0)
        return carry

    lax.fori_loop(0, ITERS, descend, 0)
    weights = w_ref[...]
    scores_ref[...] = kk * weights
    design = weights.astype(BF16)
    for peer in range(design_ref.shape[0]):
        design_ref[peer] = design


def descend(parts):
    shares, _, share = parts.shape
    return pl.pallas_call(
        descend_kernel,
        out_shape=(
            jax.ShapeDtypeStruct((K, share), F32),
            jax.ShapeDtypeStruct((shares, K, share), BF16),
        ),
        scratch_shapes=[pltpu.VMEM((K, K, share), F32), pltpu.VMEM((K, share), F32)],
        compiler_params=params(),
        cost_estimate=cost(2 * ITERS * K * K * share, 4 * K * share),
        name="descend",
    )(parts)


def cross_kernel(design_ref, methyl_ref, panel_ref, out_ref):
    blocks, kk, _ = design_ref.shape
    probes = methyl_ref.shape[1]
    design = jnp.concatenate([design_ref[b] for b in range(blocks)], axis=1)

    @pl.when(pl.program_id(0) == 0)
    def _():
        out_ref[...] = jnp.zeros_like(out_ref)

    out_ref[:, probes : probes + kk] += nt(design, design)
    width = min(probes, 512)
    for at in range(0, probes, width):
        cols = slice(at, at + width)
        out_ref[:, cols] += jnp.dot(design, methyl_ref[:, cols], preferred_element_type=F32)
        left = methyl_ref[:, cols].astype(F32) - tn(design, panel_ref[:, cols])
        squares = jnp.sum(left * left, axis=0, keepdims=True)
        for b in range(0, width, HALF):
            row = (at + b) // HALF
            out_ref[row : row + 1, probes + HALF :] += squares[:, b : b + HALF]


def cross_products(design, methyl, panel):
    _, _, share = design.shape
    rows, probes = methyl.shape
    chunk = row_chunk(share)
    return pl.pallas_call(
        cross_kernel,
        grid=(rows // chunk,),
        in_specs=[
            pl.BlockSpec((chunk // share, K, share), lambda i: (i, 0, 0)),
            pl.BlockSpec((chunk, probes), lambda i: (i, 0)),
            pl.BlockSpec((K, probes), lambda i: (0, 0)),
        ],
        out_specs=pl.BlockSpec((K, probes + LANES), lambda i: (0, 0)),
        out_shape=jax.ShapeDtypeStruct((K, probes + LANES), F32),
        compiler_params=params("arbitrary"),
        cost_estimate=cost(4 * K * rows * probes, 2 * rows * probes),
        name="cross",
    )(design, methyl, panel)


def ridge_inverse(matrix):
    kk = matrix.shape[0]
    row = lax.broadcasted_iota(jnp.int32, (kk, kk), 0)
    col = lax.broadcasted_iota(jnp.int32, (kk, kk), 1)
    work = jnp.concatenate([matrix, jnp.where(row == col, 1.0, 0.0)], axis=1)
    which = lax.broadcasted_iota(jnp.int32, (kk, 1), 0)
    for k in range(kk):
        pivot_row = work[k : k + 1, :] / work[k : k + 1, k : k + 1]
        factor = jnp.where(which == k, 0.0, work[:, k : k + 1])
        work = jnp.where(which == k, pivot_row, work - factor * pivot_row)
    return work[:, kk:]


def solve_kernel(ridge, samples, *refs):
    parts, panel_ref, out_ref = refs[:-2], refs[-2], refs[-1]
    kk, probes = panel_ref.shape
    total = parts[0][...]
    for ref in parts[1:]:
        total = total + ref[...]
    cross = total[:, :probes]
    wgram = total[:, probes : probes + kk]
    start = jnp.concatenate(
        [total[r : r + 1, probes + HALF :] for r in range(probes // HALF)], axis=1
    )
    row = lax.broadcasted_iota(jnp.int32, (kk, kk), 0)
    col = lax.broadcasted_iota(jnp.int32, (kk, kk), 1)
    system = wgram + jnp.where(row == col, ridge, 0.0)
    inverse = ridge_inverse(system)
    loadings = jnp.dot(inverse, cross, precision=HIGHEST)
    short = cross - jnp.dot(system, loadings, precision=HIGHEST)
    loadings = loadings + jnp.dot(inverse, short, precision=HIGHEST)
    panel = panel_ref[...].astype(F32)
    slope = jnp.dot(wgram, loadings + panel, precision=HIGHEST) - 2.0 * cross
    spread = start + jnp.sum((loadings - panel) * slope, axis=0, keepdims=True)
    rate = lax.rsqrt(jnp.maximum(spread, 0.0) / samples + 1e-06)
    out_ref[:kk, :] = loadings
    out_ref[kk:, :] = jnp.broadcast_to(rate, (out_ref.shape[0] - kk, probes))


def solve(parts, panel, ridge, samples):
    probes = panel.shape[1]
    return pl.pallas_call(
        functools.partial(solve_kernel, ridge, samples),
        out_shape=jax.ShapeDtypeStruct((K + 8, probes), F32),
        compiler_params=params(),
        cost_estimate=cost(50 * K * K * probes, 20 * K * probes),
        name="solve",
    )(*parts, panel)


def standardise(design, methyl_ref, terms_ref, rate, store):
    probes = methyl_ref.shape[1]
    stacked = jnp.concatenate([design] * 3, axis=0)
    width = min(probes, 512)
    for at in range(0, probes, width):
        cols = slice(at, at + width)
        fitted = tn(stacked, terms_ref[:, cols])
        left = methyl_ref[:, cols].astype(F32) - fitted
        store(at, width, (left * rate[:, cols]).astype(BF16))


def put_tile(part, sends, keep_ref):
    share = keep_ref.shape[1]
    keep_ref[...] = part[:, :share]
    for j, ref in enumerate(sends, 1):
        ref[...] = part[:, j * share : (j + 1) * share].astype(BF16)


def own_kernel(
    steps, line, place_ref, core_ref, design_ref, mine_ref, theirs_ref, facts_ref, more_ref, *refs
):
    (z_ref, *sends), (keep_ref, half_ref, terms_ref, moreterms_ref) = refs[:line], refs[line:]
    step = pl.program_id(0)
    blocks, kk, share = design_ref.shape
    chunk, probes = mine_ref.shape
    place, core = place_ref[0], core_ref[0]

    @pl.when(step == 0)
    def _():
        terms_ref[...] = three_terms(facts_ref[:kk, :])
        moreterms_ref[...] = three_terms(more_ref[:kk, :])

    @pl.when(step < steps)
    def _():
        design = jnp.concatenate([design_ref[b] for b in range(blocks)], axis=1)
        rows = pl.ds(pl.multiple_of(step * chunk, chunk), chunk)

        def store(base, at, width, value):
            z_ref[rows, base + at : base + at + width] = value

        standardise(design, mine_ref, terms_ref, facts_ref[kk : kk + 1, :], functools.partial(store, 0))
        standardise(
            design, theirs_ref, moreterms_ref, more_ref[kk : kk + 1, :], functools.partial(store, probes)
        )
        for b in range(blocks // 2):
            here = pl.ds(pl.multiple_of(step * chunk + (2 * b + core) * share, share), share)
            slot = lax.rem(step * (blocks // 2) + b - place + line, line)
            half_ref[pl.ds(pl.multiple_of(slot * share, share), share), :] = z_ref[here, :]

    @pl.when(step >= steps)
    def _():
        tall = keep_ref.shape[0]
        rows = pl.ds(pl.multiple_of((step - steps) * tall, tall), tall)
        put_tile(nt(z_ref[rows, :], half_ref[...]), sends, keep_ref)


def own_tile(at, line, design, mine, theirs, facts, more):
    _, _, share = design.shape
    rows, probes = mine.shape
    chunk = row_chunk(share)
    steps, tall = rows // chunk, 2 * chunk

    def first(i, *_):
        return (jnp.minimum(i, steps - 1), 0)

    def second(i, *_):
        return (jnp.maximum(i - steps, 0), 0)

    whole = pl.BlockSpec((K + 8, probes), lambda i, *_: (0, 0))
    return pl.pallas_call(
        functools.partial(own_kernel, steps, line),
        grid_spec=pltpu.PrefetchScalarGridSpec(
            num_scalar_prefetch=2,
            grid=(steps + rows // tall,),
            in_specs=[
                pl.BlockSpec((chunk // share, K, share), lambda i, *_: (*first(i), 0)),
                pl.BlockSpec((chunk, probes), first),
                pl.BlockSpec((chunk, probes), first),
                whole,
                whole,
            ],
            out_specs=[pl.BlockSpec(memory_space=pltpu.VMEM)]
            + [pl.BlockSpec((tall, share), second)] * line,
            scratch_shapes=[
                pltpu.VMEM((rows // 2, 2 * probes), BF16),
                pltpu.VMEM((3 * K, probes), BF16),
                pltpu.VMEM((3 * K, probes), BF16),
            ],
        ),
        out_shape=[pltpu.VMEM((rows, 2 * probes), BF16)]
        + [jax.ShapeDtypeStruct((rows, share), BF16)] * (line - 1)
        + [jax.ShapeDtypeStruct((rows, share), F32)],
        compiler_params=params("arbitrary"),
        cost_estimate=cost(2 * rows * rows * probes, 12 * rows * probes),
        name="own",
    )(*at, design, mine, theirs, facts, more)


def pair_kernel(index_of, line, first, sides, given, last, place_ref, design_ref, zscore_ref, *refs):
    facts, raws, refs = refs[:sides], refs[sides : 2 * sides], refs[2 * sides :]
    given_ref, refs = (refs[0], refs[1:]) if given else (None, refs)
    outs, (z_ref, *terms) = refs[: -1 - sides], refs[-1 - sides :]
    blocks, kk, share = design_ref.shape
    probes = facts[0].shape[1]
    tall = outs[0].shape[-2]
    step, place = pl.program_id(0), place_ref[0]

    @pl.when(step == 0)
    def _():
        design = jnp.concatenate([design_ref[b] for b in range(blocks)], axis=1)
        for side in range(sides):
            terms[side][...] = three_terms(facts[side][:kk, :])

            def store(at, width, value):
                z_ref[:, side * probes + at : side * probes + at + width] = value

            standardise(design, raws[side], terms[side], facts[side][kk : kk + 1, :], store)

    @pl.when(step > 0)
    def _():
        rows = pl.ds(pl.multiple_of((step - 1) * tall, tall), tall)
        part = nt(zscore_ref[rows, first * probes : (first + sides) * probes], z_ref[...])
        if given:
            part = part + given_ref[rows, :]
        if not last:
            outs[0][...] = part
            return
        if index_of is None:
            swap_ref, keep_ref = outs
            odd = lax.rem(place, 2) == 1
            for k in range(blocks // 2):
                low = part[:, 2 * k * share : (2 * k + 1) * share]
                high = part[:, (2 * k + 1) * share : (2 * k + 2) * share]
                swap_ref[k] = jnp.where(odd, low, high).astype(BF16)
                keep_ref[k] = jnp.where(odd, high, low)
            return
        *sends, keep_ref = outs
        for j, ref in enumerate([keep_ref, *sends]):
            index, inside = index_of(lax.rem(place + j, line))
            block = part[:, :share]
            for b in range(1, blocks):
                block = jnp.where(index == b, part[:, b * share : (b + 1) * share], block)
            if j == 0:
                block = jnp.where(inside, block, 0.0)
            ref[...] = block.astype(ref.dtype)


def pair_tile(index_of, at, line, design, zscore, first, facts, raws, given=None, last=True):
    blocks, _, share = design.shape
    rows, depth = zscore.shape
    probes, sides = depth // 2, len(facts)
    tall = 2 * row_chunk(share)
    given = [] if given is None else [given]
    width = share if last else blocks * share
    column = pl.BlockSpec((tall, width), lambda i, *_: (jnp.maximum(i - 1, 0), 0))
    whole = jax.ShapeDtypeStruct((rows, width), F32)
    sends = [jax.ShapeDtypeStruct((rows, share), BF16)] * (line - 1)
    out_specs = [column] * line if last else [column]
    out_shape = sends + [whole] if last else [whole]
    if last and index_of is None:
        halves = (blocks // 2, tall, share)
        out_specs = [pl.BlockSpec(halves, lambda i, *_: (0, jnp.maximum(i - 1, 0), 0))] * 2
        out_shape = [jax.ShapeDtypeStruct((blocks // 2, rows, share), t) for t in (BF16, F32)]
    return pl.pallas_call(
        functools.partial(pair_kernel, index_of, line, first, sides, bool(given), last),
        grid_spec=pltpu.PrefetchScalarGridSpec(
            num_scalar_prefetch=1,
            grid=(1 + rows // tall,),
            in_specs=[pl.BlockSpec(memory_space=pltpu.VMEM)] * (2 + 2 * sides + len(given)),
            out_specs=out_specs,
            scratch_shapes=[pltpu.VMEM((blocks * share, sides * probes), BF16)]
            + [pltpu.VMEM((3 * K, probes), BF16)] * sides,
        ),
        out_shape=out_shape,
        compiler_params=params("arbitrary"),
        cost_estimate=cost(2 * rows * blocks * share * sides * probes, 4 * rows * probes),
    )(at[0], design, zscore, *facts, *raws, *given)


def fold_kernel(line, place_ref, core_ref, *refs):
    (keep_ref, *parts), (total_ref, same_ref, other_ref) = refs[:-3], refs[-3:]
    place, core = place_ref[0], core_ref[0]
    share = same_ref.shape[1]
    total = keep_ref[...]
    for ref in parts:
        total = total + ref[...].astype(F32)
    total_ref[...] = total
    for j in range(line):
        block = 2 * lax.rem(place + j, line)
        same = pl.ds(pl.multiple_of((block + core) * share, share), share)
        other = pl.ds(pl.multiple_of((block + 1 - core) * share, share), share)
        same_ref[j] = total_ref[same, :].astype(BF16)
        other_ref[j] = total_ref[other, :].astype(BF16)


def fold(at, line, parts):
    rows, share = parts[0].shape
    blocks = jax.ShapeDtypeStruct((line, share, share), BF16)
    vmem = pl.BlockSpec(memory_space=pltpu.VMEM)
    return pl.pallas_call(
        functools.partial(fold_kernel, line),
        in_specs=[pl.BlockSpec(memory_space=pltpu.SMEM)] * 2 + [vmem] * len(parts),
        out_shape=(jax.ShapeDtypeStruct((rows, share), F32), blocks, blocks),
        compiler_params=params(),
        cost_estimate=cost(rows * share * 8, rows * share * 16),
        name="fold",
    )(*at, *parts)


def scale_kernel(probes, wholes, own_ref, *refs):
    parts, halves, (left_ref, out_ref) = refs[:wholes], refs[wholes:-2], refs[-2:]
    total = own_ref[...]
    for ref in parts:
        total = total + ref[...].astype(F32)
    for top, bottom in zip(halves[: len(halves) // 2], halves[len(halves) // 2 :]):
        total = total + jnp.concatenate([top[...], bottom[...]], axis=0).astype(F32)
    out_ref[0] = total * (1.0 / probes)
    out_ref[1] = left_ref[...] * (1.0 / probes)


def scale(probes, keep, parts, tops, bottoms, left):
    rows, share = keep.shape
    whole = pl.BlockSpec((rows, share), lambda i: (0, 0))
    half = pl.BlockSpec((rows // 2, share), lambda i: (0, 0))
    return pl.pallas_call(
        functools.partial(scale_kernel, probes, len(parts)),
        grid=(1,),
        in_specs=[whole] * (1 + len(parts)) + [half] * (2 * len(tops)) + [whole],
        out_specs=pl.BlockSpec((2, rows, share), lambda i: (0, 0, 0)),
        out_shape=jax.ShapeDtypeStruct((3, rows, share), F32),
        compiler_params=params("arbitrary"),
        cost_estimate=cost(rows * share * 16, rows * share * 30),
        name="scale",
    )(keep, *parts, *tops, *bottoms, left)


def finish_kernel(line, probes, place_ref, core_ref, _, same_ref, other_ref, *refs):
    shifted, out_ref = refs[:-1], refs[-1]
    place, core = place_ref[0], core_ref[0]
    share = same_ref.shape[1]
    for j in range(line):
        block = 2 * lax.rem(place - j + line, line)
        for side in range(2):
            piece = (same_ref, other_ref)[side][0] if j == 0 else shifted[j - 1][side]
            to = block + (core if side == 0 else 1 - core)
            rows = pl.ds(pl.multiple_of(to * share, share), share)
            out_ref[0, rows, :] = piece.astype(F32).T * (1.0 / probes)


def finish(at, line, probes, tiles, same, other, shifted):
    _, rows, share = tiles.shape
    first = pl.BlockSpec((1, share, share), lambda i: (0, 0, 0))
    pair = pl.BlockSpec((2, share, share), lambda i: (0, 0, 0))
    return pl.pallas_call(
        functools.partial(finish_kernel, line, probes),
        grid=(1,),
        in_specs=[pl.BlockSpec(memory_space=pltpu.SMEM)] * 2
        + [pl.BlockSpec(memory_space=pl.ANY), first, first]
        + [pair] * len(shifted),
        out_specs=pl.BlockSpec((1, rows, share), lambda i: (2, 0, 0)),
        out_shape=jax.ShapeDtypeStruct(tiles.shape, F32),
        input_output_aliases={2: 0},
        compiler_params=params("arbitrary"),
        cost_estimate=cost(rows * share * 4, rows * share * 8),
        name="finish",
    )(*at, tiles, same, other, *shifted)


def body(methyl, atlas, panel_ids):
    panels, shares = lax.axis_size("samp"), lax.axis_size("probe")
    rows = methyl.shape[0]
    samples = rows * panels
    probes = methyl.shape[1] * shares
    share = rows // shares
    line = shares // 2
    position = lax.axis_index("probe")
    place, core = position // 2, position % 2
    at = (place[None], core[None])

    def along(value, axis, pairs):
        return lax.ppermute(value, axis, pairs)

    def to_sibling(value):
        return along(value, "probe", [(i, i ^ 1) for i in range(shares)])

    def to_panel(value, by):
        return along(value, "samp", [(i, (i + by) % panels) for i in range(panels)])

    def to_panel_sibling(value, by):
        pairs = [
            (s * shares + i, ((s + by) % panels) * shares + (i ^ 1))
            for s in range(panels)
            for i in range(shares)
        ]
        return along(value, ("samp", "probe"), pairs)

    def swap_panels(value, bit):
        return along(value, "samp", [(i, i ^ bit) for i in range(panels)])

    def on_line(value, pairs):
        return along(value, "probe", [(2 * i + c, 2 * to + c) for i, to in pairs for c in (0, 1)])

    quarter = line // 4
    ends = [*range(quarter), *range(line - quarter, line)]
    inner = [*range(quarter, line - quarter)]

    def among_inner(to):
        return to - quarter, (to >= quarter) & (to < line - quarter)

    ends_mine = to_panel(pick_ends(core[None], methyl, line, share), 1)
    theirs = to_sibling(methyl)
    parts, panel, outer, same, other = project(core[None], panel_ids, atlas, methyl, shares)
    ends_theirs = to_panel_sibling(outer, 1)
    parts = lax.all_to_all(parts, "probe", 0, 0)
    scores, copies = descend(parts)
    design = lax.all_to_all(copies, "probe", 0, 0)
    part = cross_products(design, methyl, panel)
    peers = [swap_panels(part, mask) for mask in range(1, panels)]
    half = lax.dynamic_index_in_dim(design.reshape(line, 2, K, share), core, 1, False)
    design_before = to_panel(half, 1)
    inner_mine = to_panel(same, 1)
    inner_theirs = to_panel_sibling(other, 1)
    facts = solve([part, *peers], panel, 0.0001 * samples, samples)
    more = to_sibling(facts)

    def round_of(by, among=None):
        pairs = [(i, (i + by) % line) for i in range(line)]
        return pairs if among is None else [(i, to) for i, to in pairs if to in among]

    def arrivals(sends, among=None, rounds=None):
        return [
            on_line(value, round_of(j, among))
            for j, value in enumerate(sends, 1)
            if rounds is None or j in rounds
        ]

    zscore, *own_sends, own_keep = own_tile(at, line, design, methyl, theirs, facts, more)
    early = {1, line - 1}
    late = set(range(1, line)) - early
    own_parts = arrivals(own_sends, rounds=early)
    tops = arrivals([value[: rows // 2] for value in own_sends], rounds=late)
    design_ends = jnp.concatenate([design_before[:quarter], design_before[line - quarter :]])
    swap, keep = pair_tile(
        None, at, line, design_ends, zscore, 0, [facts, more],
        [ends_mine, ends_theirs],
    )
    given = on_line(swap, [(i, i ^ 1) for i in range(line)])
    design_inner = design_before[quarter : line - quarter]
    (partial,) = pair_tile(
        among_inner, at, line, design_inner, zscore, 0, [facts], [inner_mine],
        last=False,
    )
    keep = keep + given.astype(F32)

    def sum_for(to):
        if quarter == 1:
            return keep[0]
        which = jnp.where(to >= line - quarter, to - line + 2 * quarter, to) // 2
        return lax.dynamic_index_in_dim(keep, jnp.clip(which, 0, quarter - 1), 0, False)

    pair_parts = [jnp.where((place < quarter) | (place >= line - quarter), sum_for(place), 0.0)]
    for j in range(2, line, 2):
        pair_parts.append(on_line(sum_for((place + j) % line).astype(BF16), round_of(j, ends)))
    *sends, keep = pair_tile(
        among_inner, at, line, design_inner, zscore, 1, [more], [inner_theirs],
        given=partial,
    )
    pair_parts.append(keep)
    pair_parts += arrivals(sends, inner, late)
    pair_parts += arrivals(sends, inner, early)
    left, same, other = fold(at, line, pair_parts)
    same = to_panel(same, -1)
    other = to_panel_sibling(other, -1)
    bottoms = arrivals([value[rows // 2 :] for value in own_sends], rounds=late)
    shifted = []
    for j in range(1, line):
        shifted.append(on_line(jnp.stack([same[j], other[j]]), round_of(j)))
    tiles = scale(probes, own_keep, own_parts, tops, bottoms, left)
    return finish(at, line, probes, tiles, same, other, shifted), scores


def solution(mesh):
    placed = (P("samp", "probe"), P(None, "probe"), P())
    return jax.shard_map(
        body,
        mesh=mesh,
        in_specs=placed,
        out_specs=(P(None, "samp", "probe"), P(None, ("samp", "probe"))),
        check_vma=False,
    )
```
